256 devices in a mesh: tp: 8 (over z_hi, core), ex: 8 (over y, z_lo), co: 4 (over x).
Axes of the slice: x: 4, y: 4, z: 8 (z_hi: 4, z_lo: 2; z = z_hi * 2 + z_lo), core: 2. Of those that a mesh axis runs over, the one named last changes fastest.
Arguments:
- query_states: bfloat16 [8192, 4096], P('ex'), may hold values from -6 to 6
- out_cotangent: bfloat16 [8192, 4096], P('ex', ('tp', 'co')), may hold values from -6 to 6
- query_of_token: int32 [8192], P('ex'), may hold values from 0 to 31, as said below
- gate_weight: bfloat16 [4096, 14336], P(None, ('tp', 'co')), may hold values from -0.09375 to 0.09375
- up_weight: bfloat16 [4096, 14336], P(None, ('tp', 'co')), may hold values from -0.09375 to 0.09375
- proj_in: bfloat16 [14336, 128], P(('tp', 'co')), may hold values from -0.19209402 to 0.19209402, as said below
- proj_out: bfloat16 [4096, 128], P(('tp', 'co')), may hold values from -0.09375 to 0.09375
- database: bfloat16 [8192, 16384], P('ex', ('tp', 'co')), may hold values from -6 to 6
- stored_ids: int32 [8192], P('ex'), may hold values from 0 to 8191, each once
Outputs:
- solution: float32 [16384, 32], P(('tp', 'co'))
- scores: float32 [8192, 32], P('ex')
The draws below stay inside these ranges and needn't reach their ends.
Inputs may be any that keep to these rules, and one draw needn't show every extreme that they name: `query_of_token`: the tokens in rows b * 1024 to (b + 1) * 1024 - 1 belong to queries b * 4 to (b + 1) * 4 - 1, and every query has at least one token. `stored_ids`: every example id appears exactly once. `proj_in`: every entry lies within plus or minus 23 * 14336 ** -0.5.
All inputs are finite; a program needn't handle non-finite values.
Results may differ from the reference program's by a relative error of at most 0.03.
Values sent between devices are 32-bit elements; how exact they have to be, the bound alone decides.
A program may use at most 64 MiB of HBM per device.

```python
import math
import jax
import jax.numpy as jnp
from jax import lax

D = 4096
FF = 14336
RIN = 128
ROUT = 128
K = 16384
TOK_DEV = 1024
QPG = 4
QUERIES = 32
QTOK = 8192
NSTORE = 8192
ITERS = 2


def draw_query_of_token(key, part):
    blocks = QTOK // TOK_DEV
    key_labels, key_shuffle = jax.random.split(jax.random.fold_in(key, 11))
    local_ids = jax.random.randint(key_labels, (blocks, TOK_DEV), 0, QPG)
    local_ids = local_ids.at[:, :QPG].set(jnp.arange(QPG, dtype=jnp.int32)[None, :])
    shuffle = jax.vmap(lambda subkey: jax.random.permutation(subkey, TOK_DEV))(jax.random.split(key_shuffle, blocks))
    local_ids = jnp.take_along_axis(local_ids, shuffle, axis=1)
    offsets = jnp.arange(blocks, dtype=jnp.int32)[:, None] * QPG
    return (local_ids + offsets).reshape(QTOK).astype(jnp.int32)


def draw_proj_in(key, part):
    key_entries, key_jitter = jax.random.split(jax.random.fold_in(key, 7), 2)
    jitter = jax.random.uniform(key_jitter, (RIN,), minval=-0.15, maxval=0.15)
    log_ramp = jnp.linspace(-0.5, 0.5, RIN)
    entries = jnp.clip(jax.random.normal(key_entries, (FF, RIN)), -4.0, 4.0)
    scales = 10.0 ** (log_ramp + jitter)
    values = entries * scales[None, :] / math.sqrt(FF)
    return values.astype(jnp.float32).astype(jnp.bfloat16)


def steps_of(key, dims, cuts, low, largest):
    level = 1.0
    for dim, blocks in cuts:
        heights = jax.random.uniform(jax.random.fold_in(jax.random.fold_in(key, 6), dim), (blocks,), jnp.float32, low / len(cuts), largest / len(cuts))
        level = level * jnp.repeat(jnp.exp(heights), dims[dim] // blocks).reshape((-1,) + (1,) * (len(dims) - 1 - dim))
    return level


def scatter_about(stream_key, shape, width, most, shards=(), kind=jnp.bfloat16):
    factor_of = steps_of(stream_key, shape, shards, -0.22, 0.18) if shards else 1.0
    values = jax.random.normal(stream_key, shape, jnp.float32) * width * factor_of
    return jnp.minimum(jnp.maximum(values, -most), most).astype(kind)


def setup_inputs(seed: int = 0) -> dict:
    arg_keys = jax.random.split(jax.random.key(seed), 10)
    query_states = scatter_about(arg_keys[0], (QTOK, D), 1.0, 6.0, ((0, 8),))
    out_cotangent = scatter_about(arg_keys[1], (QTOK, D), 1.0, 6.0, ((0, 8), (1, 32)))
    query_of_token = draw_query_of_token(jax.random.fold_in(arg_keys[9], 71), 0)
    gate_weight = scatter_about(arg_keys[3], (D, FF), D ** -0.5, 0.09375, ((1, 32),))
    up_weight = scatter_about(arg_keys[4], (D, FF), D ** -0.5, 0.09375, ((1, 32),))
    proj_in = draw_proj_in(jax.random.fold_in(arg_keys[9], 71), 0)
    proj_out = scatter_about(arg_keys[6], (D, ROUT), D ** -0.5, 0.09375, ((0, 32),))
    database = scatter_about(arg_keys[7], (NSTORE, K), 1.0, 6.0, ((0, 8), (1, 32)))
    stored_ids = jax.random.permutation(arg_keys[8], NSTORE).astype(jnp.int32)
    return dict(query_states=query_states, out_cotangent=out_cotangent, query_of_token=query_of_token, gate_weight=gate_weight, up_weight=up_weight, proj_in=proj_in, proj_out=proj_out, database=database, stored_ids=stored_ids)


DAMPING = 1.0
HIGHEST = lax.Precision.HIGHEST

def inner_gram(first, second):
    return lax.dot_general(first.astype(jnp.float32), second.astype(jnp.float32), (((0,), (0,)), ((), ())), precision=HIGHEST, preferred_element_type=jnp.float32)

def times_small(matrix, coeffs):
    return jnp.dot(matrix.astype(jnp.float32), coeffs.astype(jnp.float32), precision=HIGHEST, preferred_element_type=jnp.float32)

def solve_spd(matrix, target):
    factor = jnp.linalg.cholesky(matrix)
    return jax.scipy.linalg.cho_solve((factor, True), target)

def symmetric(matrix):
    return 0.5 * (matrix + matrix.T)

def reference(query_states, out_cotangent, query_of_token, gate_weight, up_weight, proj_in, proj_out, database, stored_ids):
    gate_act = jnp.dot(query_states.astype(jnp.float32), gate_weight.astype(jnp.float32), preferred_element_type=jnp.float32)
    up_act = jnp.dot(query_states.astype(jnp.float32), up_weight.astype(jnp.float32), preferred_element_type=jnp.float32)
    hidden = (jax.nn.silu(gate_act) * up_act).astype(jnp.bfloat16)
    left_proj = jnp.dot(hidden.astype(jnp.float32), proj_in.astype(jnp.float32), preferred_element_type=jnp.float32)
    right_proj = jnp.dot(out_cotangent.astype(jnp.float32), proj_out.astype(jnp.float32), preferred_element_type=jnp.float32)
    onehot = (query_of_token[:, None] == jnp.arange(QUERIES, dtype=jnp.int32)[None, :]).astype(jnp.float32)
    weighted = (left_proj[:, :, None] * onehot[:, None, :]).reshape(QTOK, RIN * QUERIES)
    targets = inner_gram(weighted, right_proj)
    targets = targets.reshape(RIN, QUERIES, ROUT).transpose(0, 2, 1).reshape(K, QUERIES)
    gram_scale = 1.0 / math.sqrt(float(NSTORE))
    solution = jnp.zeros_like(targets)
    residual = targets
    direction = targets
    norm_now = inner_gram(residual, residual)
    for step_index in range(ITERS):
        packed = direction.astype(jnp.bfloat16)
        row_sums = jnp.dot(database.astype(jnp.float32), packed.astype(jnp.float32), preferred_element_type=jnp.float32)
        rows_low = (row_sums * gram_scale).astype(jnp.bfloat16)
        back_sum = lax.dot_general(database.astype(jnp.float32), rows_low.astype(jnp.float32), (((0,), (0,)), ((), ())), preferred_element_type=jnp.float32)
        image = back_sum * gram_scale + DAMPING * direction
        curvature = symmetric(inner_gram(direction, image))
        step_size = solve_spd(curvature, norm_now)
        solution = solution + times_small(direction, step_size)
        residual = residual - times_small(image, step_size)
        if step_index + 1 < ITERS:
            norm_next = inner_gram(residual, residual)
            mixing = solve_spd(norm_now, norm_next)
            direction = residual + times_small(direction, mixing)
            norm_now = norm_next
    final_low = solution.astype(jnp.bfloat16)
    score_rows = jnp.dot(database.astype(jnp.float32), final_low.astype(jnp.float32), preferred_element_type=jnp.float32) * (1.0 / math.sqrt(K))
    scores = jnp.zeros((NSTORE, QUERIES), jnp.float32).at[stored_ids].set(score_rows)
    return (solution, scores)
```

```python
import math

import jax
import jax.numpy as jnp
from jax import lax
from jax.sharding import Mesh
from jax.sharding import PartitionSpec as P

ROUT = 128
K = 16384
QPG = 4
ITERS = 2
TP_CO = ("tp_0", "tp_1", "co")


DAMPING = 1.0
HIGHEST = lax.Precision.HIGHEST


def from_everyone(value, axis):
    devices = lax.axis_size(axis)
    return lax.all_to_all(
        jnp.broadcast_to(value[None], (devices, *value.shape)), axis, 0, 0, tiled=True
    )


def of_everyone(value, axis):
    return from_everyone(value, axis).sum(axis=0)


def split_up(value, dim, devices):
    before, after = (value.shape[:dim], value.shape[dim + 1 :])
    return jnp.moveaxis(value.reshape(*before, devices, -1, *after), dim, 0)


def sent_and_summed(value, axis, dim):
    devices = lax.axis_size(axis)
    pieces = lax.all_to_all(split_up(value, dim, devices), axis, 0, 0, tiled=True)
    return jnp.sum(pieces, axis=0)


def sum_by_axis(value, axes, dim):
    far, near = axes
    pieces = split_up(value, dim, lax.axis_size(far))
    nearer = sent_and_summed(pieces, near, dim + 1)
    arrived = lax.all_to_all(nearer, far, split_axis=0, concat_axis=0, tiled=True)
    return arrived.sum(axis=0)


def filled_up(lines, devices):
    spare = -lines.shape[0] % devices
    if not spare:
        return lines
    return jnp.concatenate([lines, jnp.zeros((spare, *lines.shape[1:]), lines.dtype)])


def joined_along(pieces, dim):
    pieces = jnp.moveaxis(pieces, 0, dim)
    dims = pieces.shape
    return pieces.reshape(*dims[:dim], dims[dim] * dims[dim + 1], *dims[dim + 2 :])


def gathered_by_axis(value, axes, dim):
    far, near = axes
    pieces = from_everyone(from_everyone(value, far), near)
    return joined_along(pieces.swapaxes(0, 1).reshape(-1, *value.shape), dim)


def sum_by_parts(value, axes):
    own = sum_by_axis(filled_up(value, lax.axis_size(axes[0]) * lax.axis_size(axes[1])), axes, 0)
    whole = gathered_by_axis(own, axes, 0)
    return whole[: len(value)].reshape(value.shape)


def in_one(arrays, axis):
    ravelled, at, outs = (jnp.concatenate([a.reshape(-1) for a in arrays]), 0, [])
    so_far = sum_by_parts(ravelled, axis)
    for a in arrays:
        outs.append(so_far[at : at + a.size].reshape(a.shape))
        at += a.size
    return tuple(outs)


def gather_directly(value, axis, dim):
    pieces = from_everyone(value, axis)
    return joined_along(pieces, dim)


def nested_sum(value, axes):
    own = sent_and_summed(filled_up(value, lax.axis_size(axes)), axes, 0)
    whole = gather_directly(own, axes, 0)
    return whole[: len(value)].reshape(value.shape)


def in_one_2(arrays, axis):
    ends = [0]
    for a in arrays:
        ends.append(ends[-1] + a.size)
    so_far = nested_sum(jnp.concatenate([a.ravel() for a in arrays]), axis)
    return tuple((so_far[b:e].reshape(a.shape) for a, b, e in zip(arrays, ends, ends[1:])))


def together(arrays, axis):
    ends = [0]
    for a in arrays:
        ends.append(ends[-1] + a.size)
    so_far = of_everyone(jnp.concatenate([a.ravel() for a in arrays]), axis)
    return tuple((so_far[b:e].reshape(a.shape) for a, b, e in zip(arrays, ends, ends[1:])))


def total_of(value, axes):
    lines = value.reshape(-1, value.shape[-1])
    own = sent_and_summed(filled_up(lines, lax.axis_size(axes)), axes, 0)
    whole = gather_directly(own, axes, 0)
    return whole[: len(lines)].reshape(value.shape)


def in_one_piece(arrays, axis, dim, along):
    columns = [a.reshape(*a.shape[:along], -1) for a in arrays]
    both = jnp.concatenate(columns, axis=along)
    whole, at, outs = (lax.all_gather(both, axis, axis=dim, tiled=True), 0, [])
    for a, column in zip(arrays, columns):
        piece = whole[..., at : at + column.shape[along]]
        outs.append(piece.reshape(*piece.shape[:along], *a.shape[along:]))
        at += column.shape[along]
    return tuple(outs)


def inner_gram(first, second):
    return lax.dot_general(
        first,
        second,
        (((0,), (0,)), ((), ())),
        precision=HIGHEST,
        preferred_element_type=jnp.float32,
    )


def times_small(matrix, coeffs):
    return jnp.dot(matrix, coeffs, precision=HIGHEST, preferred_element_type=jnp.float32)


def solve_spd(matrix, target):
    factor = jnp.linalg.cholesky(matrix)
    return jax.scipy.linalg.cho_solve((factor, True), target)


def symmetric(matrix):
    return 0.5 * (matrix + matrix.T)


def residual_gram(residual):
    return of_everyone(inner_gram(residual, residual), TP_CO)


def outer_grads(left_cols, right_full, onehot):
    tokens = left_cols.shape[0]
    columns = left_cols.shape[1]
    per_query = onehot.shape[1]
    weighted = (left_cols[:, :, None] * onehot[:, None, :]).reshape(tokens, columns * per_query)
    grads = inner_gram(weighted, right_full)
    return (
        grads.reshape(columns, per_query, ROUT)
        .transpose(0, 2, 1)
        .reshape(columns * ROUT, per_query)
    )


def local(
    query_states,
    out_cotangent,
    query_of_token,
    gate_weight,
    up_weight,
    proj_in,
    proj_out,
    database,
    stored_ids,
):
    learners = lax.axis_size(TP_CO)
    learner = lax.axis_index(TP_CO)
    ex_count = lax.axis_size("ex")
    ex_index = lax.axis_index("ex")
    band_cols = proj_in.shape[1] // learners
    local_ids = query_of_token - ex_index * QPG
    onehot = (local_ids[:, None] == jnp.arange(QPG, dtype=jnp.int32)[None, :]).astype(jnp.float32)
    right_part = jnp.dot(out_cotangent, proj_out, preferred_element_type=jnp.float32)
    gate_act = jnp.dot(query_states, gate_weight, preferred_element_type=jnp.float32)
    up_act = jnp.dot(query_states, up_weight, preferred_element_type=jnp.float32)
    hidden = (jax.nn.silu(gate_act) * up_act).astype(jnp.bfloat16)
    left_part = jnp.dot(hidden, proj_in, preferred_element_type=jnp.float32)
    left_full, right_full = in_one((left_part, right_part), ("tp_0", ("tp_1", "co")))
    left_band = lax.dynamic_slice_in_dim(left_full, learner * band_cols, band_cols, 1)
    local_grads = outer_grads(left_band, right_full, onehot)
    targets = gather_directly(local_grads, "ex", 1)
    rows_local = database.shape[0]
    gram_scale = 1.0 / math.sqrt(float(rows_local * ex_count))
    packed = targets.astype(jnp.bfloat16)
    rows_part = jnp.dot(database, packed, preferred_element_type=jnp.float32)
    rows0, norm0 = in_one_2((rows_part, inner_gram(targets, targets)), TP_CO)
    low0 = (rows0 * gram_scale).astype(jnp.bfloat16)
    back_term = lax.dot_general(
        database, low0, (((0,), (0,)), ((), ())), preferred_element_type=jnp.float32
    )
    back_sum, rows_gram = together((back_term, inner_gram(rows0, rows0)), "ex")
    image = back_sum * gram_scale + DAMPING * targets
    step0 = solve_spd(rows_gram * gram_scale**2 + DAMPING * norm0, norm0)
    residual = targets - times_small(image, step0)
    rows_part = jnp.dot(
        database, residual.astype(jnp.bfloat16), preferred_element_type=jnp.float32
    )
    rows_r, norm1, cross = in_one_2(
        (rows_part, inner_gram(residual, residual), inner_gram(targets, residual)), TP_CO
    )
    mixing = solve_spd(norm0, norm1)
    rows1 = rows_r + times_small(rows0, mixing)
    mixed = inner_gram(mixing, cross)
    gram1 = norm1 + mixed + mixed.T + inner_gram(mixing, times_small(norm0, mixing))
    (rows_gram1,) = together((inner_gram(rows1, rows1),), "ex")
    step1 = solve_spd(symmetric(rows_gram1 * gram_scale**2 + DAMPING * gram1), norm1)
    direction = residual + times_small(targets, mixing)
    solution = times_small(targets, step0) + times_small(direction, step1)
    score_rows = (times_small(rows0, step0) + times_small(rows1, step1)) * (1.0 / math.sqrt(K))
    all_scores, all_ids = in_one_piece((score_rows, stored_ids.astype(jnp.float32)), "ex", 0, 1)
    position = all_ids.astype(jnp.int32) - ex_index * rows_local
    inside = (position >= 0) & (position < rows_local)
    position = jnp.where(inside, position, rows_local)
    placed = (
        jnp.zeros((rows_local, all_scores.shape[1]), jnp.float32)
        .at[position]
        .set(all_scores, mode="drop")
    )
    return (solution, placed)


def solution(mesh):
    finer = Mesh(
        mesh.devices.reshape(4, 2, mesh.shape["ex"], mesh.shape["co"]), ("tp_0", "tp_1", "ex", "co")
    )
    in_specs = (
        P("ex", None),
        P("ex", TP_CO),
        P("ex"),
        P(None, TP_CO),
        P(None, TP_CO),
        P(TP_CO, None),
        P(TP_CO, None),
        P("ex", TP_CO),
        P("ex"),
    )
    out_specs = (P(TP_CO, None), P("ex", None))
    return jax.shard_map(local, mesh=finer, in_specs=in_specs, out_specs=out_specs, check_vma=False)
```

```python
import functools
import math

import jax
import jax.numpy as jnp
from jax import lax
from jax.experimental import pallas as pl
from jax.experimental.pallas import tpu as pltpu
from jax.sharding import PartitionSpec as P

D = 4096
FFL = 448
TOK = 1024
CHUNK = 256
CHUNKS = TOK // CHUNK
KB = 512
KSTEPS = D // KB
R = 128
Q = 32
QPG = 4
COORDS = 512
ROWS = 1024
EX = 8
GROUP = 8
ZH = 4
K = 16384
NSTORE = 8192
DAMPING = 1.0
HIGHEST = lax.Precision.HIGHEST
MESH = pl.DeviceIdType.MESH
F32 = jnp.float32
BF16 = jnp.bfloat16

PHASES = (
    ["ids", "r1", "r2", "r3"]
    + [f"l1{c}" for c in range(CHUNKS)]
    + [f"l2{c}" for c in range(CHUNKS)]
    + ["b", "y10", "y20", "y30", "z1", "z3", "s0", "y11", "y21", "y31", "s1", "c1"]
)
PHASE = {name: at for at, name in enumerate(PHASES)}


def fdot(a, b, dims=((1,), (0,))):
    return lax.dot_general(a, b, (dims, ((), ())), precision=HIGHEST, preferred_element_type=F32)


def bdot(a, b, dims=((1,), (0,))):
    return lax.dot_general(a, b, (dims, ((), ())), preferred_element_type=F32)


TN = ((0,), (0,))
NT = ((1,), (1,))


def eliminated(matrix, target):
    n = matrix.shape[0]
    both = jnp.concatenate([matrix, target], axis=1)
    lines = lax.broadcasted_iota(jnp.int32, both.shape, 0)
    for k in range(n):
        row = both[k : k + 1, :] / both[k : k + 1, k : k + 1]
        both = jnp.where(lines == k, row, both - both[:, k : k + 1] * row)
    return both[:, n:]


def kernel(
    q_hbm, cot_hbm, qot_hbm, gw_hbm, uw_hbm, pin_hbm, pout_hbm, db_hbm, ids_hbm,
    sol_ref, score_ref,
    q_v, cot_v, qot_v, gw_v, uw_v, pin_v, pout_v, db_v,
    acc_g, acc_u,
    ids_all, rsend, r1, r2, right,
    lsend, l1, l2,
    bbuf,
    ysend, y1, y2, yfull,
    zsend, z1, zfull,
    cbuf, s0, s1, picked, where_v, where_s,
    small_sem, q_sem, w_sem, send_sem, recv_sem,
):
    tp = lax.axis_index("tp")
    e = lax.axis_index("ex")
    x = lax.axis_index("co")
    zh = tp // 2
    core = tp % 2
    g = core * 4 + x
    scale = 1.0 / math.sqrt(float(NSTORE))

    def in_group(p):
        return {"tp": zh * 2 + p // 4, "co": p % 4}

    def in_z(p):
        return {"tp": p * 2 + core}

    def in_ex(p):
        return {"ex": p}

    def push(phase, src_of, dst, me, n, device_of):
        at = PHASE[phase]
        for d in range(1, n):
            p = (me + d) % n
            pltpu.make_async_remote_copy(
                src_of(p), dst, send_sem.at[at], recv_sem.at[at], device_of(p), MESH
            ).start()

    def arrived(phase, slots):
        pltpu.make_async_copy(slots, slots, recv_sem.at[PHASE[phase]]).wait()

    def sent(phase, slots):
        pltpu.make_async_copy(slots, slots, send_sem.at[PHASE[phase]]).wait()

    copies = [
        pltpu.make_async_copy(cot_hbm, cot_v, small_sem.at[0]),
        pltpu.make_async_copy(pout_hbm, pout_v, small_sem.at[1]),
        pltpu.make_async_copy(ids_hbm, ids_all.at[e], small_sem.at[2]),
        pltpu.make_async_copy(qot_hbm, qot_v, small_sem.at[3]),
        pltpu.make_async_copy(pin_hbm, pin_v, small_sem.at[4]),
        pltpu.make_async_copy(db_hbm, db_v, small_sem.at[5]),
    ]

    def q_copy(c):
        rows = pl.ds(c * CHUNK, CHUNK)
        return pltpu.make_async_copy(q_hbm.at[rows, :], q_v.at[rows, :], q_sem.at[c])

    def w_copy(k, side):
        cols = pl.ds(pl.multiple_of(k * KB, KB), KB)
        src, dst = ((gw_hbm, gw_v), (uw_hbm, uw_v))[side]
        return pltpu.make_async_copy(src.at[:, cols], dst.at[:, cols], w_sem.at[side, k])

    copies[0].start()
    copies[1].start()
    copies[2].start()
    q_copy(0).start()
    for k in range(KSTEPS):
        w_copy(k, 0).start()
        w_copy(k, 1).start()
        if k == 1:
            copies[3].start()
            copies[4].start()
    for c in range(1, CHUNKS):
        q_copy(c).start()
    copies[5].start()

    barrier = pltpu.get_barrier_semaphore()
    for n, me, device_of in ((GROUP, g, in_group), (ZH, zh, in_z), (EX, e, in_ex)):
        for d in range(1, n):
            pl.semaphore_signal(
                barrier, inc=1, device_id=device_of((me + d) % n), device_id_type=MESH
            )

    copies[0].wait()
    copies[1].wait()
    rsend[...] = bdot(cot_v[...], pout_v[...]).reshape(GROUP, R, R)
    copies[2].wait()

    pl.semaphore_wait(barrier, (GROUP - 1) + (ZH - 1) + (EX - 1))
    push("ids", lambda p: ids_all.at[e], ids_all.at[e], e, EX, in_ex)
    push("r1", lambda p: rsend.at[p], r1.at[g], g, GROUP, in_group)
    r1[g] = rsend[g]

    def matmul(c, first):
        rows = pl.ds(c * CHUNK, CHUNK)
        q_copy(c).wait()
        acc_g[...] = jnp.zeros_like(acc_g)
        acc_u[...] = jnp.zeros_like(acc_u)

        def step(k, carry):
            if first:
                w_copy(k, 0).wait()
                w_copy(k, 1).wait()
            cols = pl.ds(pl.multiple_of(k * KB, KB), KB)
            a = q_v[rows, cols]
            acc_g[...] += bdot(gw_v[:, cols], a, NT)
            acc_u[...] += bdot(uw_v[:, cols], a, NT)
            return carry

        lax.fori_loop(0, KSTEPS, step, 0)
        gate = acc_g[...]
        hidden = ((gate / (1.0 + jnp.exp(-gate))) * acc_u[...]).astype(BF16)
        left = bdot(pin_v[...], hidden, TN)
        a, b = left[:, :R], left[:, R:]
        low = lax.broadcasted_iota(jnp.int32, (R, R), 0) % 8 < 4
        lsend[c, 0] = jnp.where(low, a, pltpu.roll(b, 4, 0)).reshape(ZH, 4, 8, R)
        lsend[c, 1] = jnp.where(low, pltpu.roll(a, R - 4, 0), b).reshape(ZH, 4, 8, R)
        push(
            f"l1{c}", lambda p: lsend.at[c, p % 2, :, p // 2], l1.at[c, g], g, GROUP, in_group
        )
        l1[c, g] = lsend[c, g % 2, :, g // 2]

    def left_second(c):
        arrived(f"l1{c}", l1.at[c, pl.ds(0, GROUP - 1)])
        total = l1[c, 0]
        for s in range(1, GROUP):
            total = total + l1[c, s]
        sent(f"l1{c}", l1.at[c, pl.ds(0, GROUP - 1)])
        lsend[c, 0, 0] = total
        l2[c, zh] = lsend[c, 0, 0, zh]
        push(f"l2{c}", lambda p: lsend.at[c, 0, 0, p], l2.at[c, zh], zh, ZH, in_z)

    for c in range(CHUNKS):
        if c == 0:
            copies[4].wait()
        matmul(c, c == 0)
        if c == 0:
            arrived("r1", r1.at[pl.ds(0, GROUP - 1)])
            sent("r1", r1.at[pl.ds(0, GROUP - 1)])
            total = r1[0]
            for s in range(1, GROUP):
                total = total + r1[s]
            r2[zh] = total
            push("r2", lambda p: r2.at[zh], r2.at[zh], zh, ZH, in_z)
        if c == 1:
            arrived("r2", r2.at[pl.ds(0, ZH - 1)])
            right[g] = r2[0] + r2[1] + r2[2] + r2[3]
            push("r3", lambda p: right.at[g], right.at[g], g, GROUP, in_group)
        if c > 0:
            left_second(c - 1)

    arrived("ids", ids_all.at[pl.ds(0, EX - 1)])
    kinds = lax.broadcasted_iota(jnp.int32, (Q, R), 0)
    lane = lax.broadcasted_iota(jnp.int32, (Q, R), 1)
    places = jnp.zeros((Q, 2 * Q), F32)
    for s in range(EX):
        his, los = [], []
        for r in range(8):
            own = ids_all[s, pl.ds(r, 1), :] - e * ROWS
            hit_low = (own & 31) == kinds
            part = s * 2 + r % 2 + 16 * (r // 2)
            his.append(jnp.where((own >> 5) == kinds, 1.0, 0.0).astype(BF16))
            los.append(
                jnp.concatenate(
                    [
                        jnp.where(hit_low, float(part), 0.0),
                        jnp.where(hit_low, lane.astype(F32), 0.0),
                    ],
                    axis=0,
                ).astype(BF16)
            )
        places = places + bdot(
            jnp.concatenate(his, axis=1), jnp.concatenate(los, axis=1), NT
        )
    part = places[:, :Q].astype(jnp.int32)
    at = (part & 15) * R + places[:, Q:].astype(jnp.int32)
    where_v[...] = jnp.concatenate([at, part >> 4, at, at], axis=1)
    to_scalar = pltpu.make_async_copy(where_v, where_s, small_sem.at[6])
    to_scalar.start()

    left_second(CHUNKS - 1)
    arrived("r3", right.at[pl.ds(0, GROUP - 1)])
    copies[3].wait()
    copies[5].wait()
    high = lax.broadcasted_iota(jnp.int32, (8, R), 0) >= 4
    pieces, queries = [], []
    local = qot_v[...] - e * QPG
    for c in range(CHUNKS):
        arrived(f"l2{c}", l2.at[c, pl.ds(0, ZH - 1)])
        tile = l2[c, 0] + l2[c, 1] + l2[c, 2] + l2[c, 3]
        pieces.append(jnp.where(high, 0.0, tile))
        pieces.append(jnp.where(high, tile, 0.0))
        queries.append(local[2 * c : 2 * c + 1, :])
        queries.append(local[2 * c + 1 : 2 * c + 2, :])
    left = jnp.concatenate(pieces, axis=1)
    query = jnp.concatenate(queries, axis=1)
    weighted = jnp.concatenate(
        [jnp.where(query == k, left, 0.0) for k in range(QPG)], axis=0
    )
    grads = fdot(weighted, right[...].reshape(TOK, R))
    grads = grads + pltpu.roll(grads, 28, 0)
    mine = jnp.concatenate(
        [
            jnp.where(high, pltpu.roll(grads[8:16], 4, 0), grads[0:8]),
            jnp.where(high, pltpu.roll(grads[24:32], 4, 0), grads[16:24]),
        ],
        axis=0,
    )
    own_rows = pl.ds(pl.multiple_of(e * 16, 16), 16)
    bbuf[own_rows, :] = mine
    push("b", lambda p: bbuf.at[own_rows, :], bbuf.at[own_rows, :], e, EX, in_ex)
    arrived("b", bbuf.at[pl.ds(0, 16 * (EX - 1)), :])
    base = jnp.concatenate([bbuf[pl.ds(i, Q, stride=4), :] for i in range(4)], axis=1)

    def reduced(k, vectors, gram):
        part = bdot(vectors.astype(BF16), db_v[...], NT)
        for p in range(GROUP):
            ysend[k, p, :Q] = part[:, p * R : (p + 1) * R]
            ysend[k, p, Q:] = gram
        push(f"y1{k}", lambda p: ysend.at[k, p], y1.at[k, g], g, GROUP, in_group)
        y1[k, g] = ysend[k, g]
        arrived(f"y1{k}", y1.at[k, pl.ds(0, GROUP - 1)])
        total = y1[k, 0]
        for s in range(1, GROUP):
            total = total + y1[k, s]
        y2[k, zh] = total
        push(f"y2{k}", lambda p: y2.at[k, zh], y2.at[k, zh], zh, ZH, in_z)
        arrived(f"y2{k}", y2.at[k, pl.ds(0, ZH - 1)])
        total = y2[k, 0] + y2[k, 1] + y2[k, 2] + y2[k, 3]
        yfull[k, g] = total[:Q]
        push(f"y3{k}", lambda p: yfull.at[k, g], yfull.at[k, g], g, GROUP, in_group)
        return total[Q:]

    def rows_of(k):
        arrived(f"y3{k}", yfull.at[k, pl.ds(0, GROUP - 1)])
        return [yfull[k, s] for s in range(GROUP)]

    def packed(blocks):
        tall = [
            jnp.concatenate([blocks[2 * i + h] for i in range(4)], axis=0).T for h in range(2)
        ]
        return jnp.concatenate(tall, axis=0)

    gram0 = reduced(0, base, fdot(base, jnp.concatenate([base] * 4, axis=0), NT))
    norm0 = gram0[:, :Q]
    eye = (
        lax.broadcasted_iota(jnp.int32, (Q, Q), 0) == lax.broadcasted_iota(jnp.int32, (Q, Q), 1)
    ).astype(F32)
    inverse0 = eliminated(norm0, eye)
    blocks0 = rows_of(0)
    rows0 = jnp.concatenate(blocks0, axis=1)

    back = bdot((rows0 * scale).astype(BF16), db_v[...])
    row_gram = fdot(rows0, jnp.concatenate([rows0] * 4, axis=0), NT)
    for p in range(EX):
        zsend[p, :16] = back[16 * (p // 4) : 16 * (p // 4) + 16, (p % 4) * R : (p % 4 + 1) * R]
        zsend[p, 16:] = row_gram
    push("z1", lambda p: zsend.at[p], z1.at[e], e, EX, in_ex)
    z1[e] = zsend[e]
    arrived("z1", z1.at[pl.ds(0, EX - 1)])
    total = z1[0]
    for s in range(1, EX):
        total = total + z1[s]
    zfull[e] = total[:16]
    push("z3", lambda p: zfull.at[e], zfull.at[e], e, EX, in_ex)
    step0 = eliminated(total[16:, :Q] * (scale * scale) + DAMPING * norm0, norm0)
    arrived("z3", zfull.at[pl.ds(0, EX - 1)])
    back = jnp.concatenate(
        [jnp.concatenate([zfull[4 * h + j] for j in range(4)], axis=1) for h in range(2)], axis=0
    )
    image = back * scale + DAMPING * base
    residual = base - fdot(step0, image, TN)

    gram1 = reduced(
        1, residual, fdot(residual, jnp.concatenate([residual, base] * 2, axis=0), NT)
    )
    s0[e] = packed(blocks0)
    push("s0", lambda p: s0.at[e], s0.at[e], e, EX, in_ex)
    norm1 = gram1[:, :Q]
    cross = gram1[:, Q : 2 * Q]
    mixing = fdot(inverse0, norm1)
    blocks1 = rows_of(1)
    s1[e] = packed(blocks1)
    rows1 = jnp.concatenate(blocks1, axis=1) + fdot(mixing, rows0, TN)
    cbuf[e] = fdot(rows1, jnp.concatenate([rows1] * 4, axis=0), NT)
    push("c1", lambda p: cbuf.at[e], cbuf.at[e], e, EX, in_ex)
    push("s1", lambda p: s1.at[e], s1.at[e], e, EX, in_ex)
    gram = (
        norm1
        + fdot(cross, mixing)
        + fdot(mixing, cross, ((0,), (1,)))
        + fdot(mixing, fdot(norm0, mixing), TN)
    )
    to_scalar.wait()
    arrived("s0", s0.at[pl.ds(0, EX - 1)])

    def pick(source, side):
        groups = lax.broadcasted_iota(jnp.int32, (1, R), 1) // Q

        def line(hi, carry):
            for lo in range(Q):
                at = where_s[hi, lo] & (EX * 256 - 1)
                group = where_s[hi, Q + lo]
                row = source[at // 256, pl.ds(at % 256, 1), :]
                picked[side, pl.ds(hi * Q + lo, 1), :] = jnp.where(groups == group, row, 0.0)
            return carry

        lax.fori_loop(0, Q, line, 0)

    pick(s0, 0)
    arrived("c1", cbuf.at[pl.ds(0, EX - 1)])
    total = cbuf[0]
    for s in range(1, EX):
        total = total + cbuf[s]
    step1 = eliminated(total[:, :Q] * (scale * scale) + DAMPING * gram, norm1)
    first = step0 + fdot(mixing, step1)
    sol_ref[...] = fdot(first, base, TN) + fdot(step1, residual, TN)
    arrived("s1", s1.at[pl.ds(0, EX - 1)])
    pick(s1, 1)
    mix = ((0,), (1,))
    scores = fdot(jnp.concatenate([first] * 4, axis=0), picked[0], mix) + fdot(
        jnp.concatenate([step1] * 4, axis=0), picked[1], mix
    )
    score_ref[...] = scores * (1.0 / math.sqrt(K))

    sent("ids", ids_all.at[pl.ds(0, EX - 1)])
    sent("r2", r2.at[pl.ds(0, ZH - 1)])
    sent("r3", right.at[pl.ds(0, GROUP - 1)])
    for c in range(CHUNKS):
        sent(f"l2{c}", l2.at[c, pl.ds(0, ZH - 1)])
    sent("b", bbuf.at[pl.ds(0, 16 * (EX - 1)), :])
    for k in range(2):
        sent(f"y1{k}", y1.at[k, pl.ds(0, GROUP - 1)])
        sent(f"y2{k}", y2.at[k, pl.ds(0, ZH - 1)])
        sent(f"y3{k}", yfull.at[k, pl.ds(0, GROUP - 1)])
    sent("z1", z1.at[pl.ds(0, EX - 1)])
    sent("z3", zfull.at[pl.ds(0, EX - 1)])
    sent("s0", s0.at[pl.ds(0, EX - 1)])
    sent("s1", s1.at[pl.ds(0, EX - 1)])
    sent("c1", cbuf.at[pl.ds(0, EX - 1)])


def local(
    query_states, out_cotangent, query_of_token, gate_weight, up_weight, proj_in, proj_out,
    database, stored_ids,
):
    anywhere = pl.BlockSpec(memory_space=pl.ANY)
    vmem = pl.BlockSpec(memory_space=pltpu.VMEM)
    sol, scores = pl.pallas_call(
        kernel,
        out_shape=(
            jax.ShapeDtypeStruct((Q, COORDS), F32),
            jax.ShapeDtypeStruct((Q, ROWS), F32),
        ),
        in_specs=[anywhere] * 9,
        out_specs=(vmem, vmem),
        scratch_shapes=[
            pltpu.VMEM((TOK, D), BF16),
            pltpu.VMEM((TOK, R), BF16),
            pltpu.VMEM((8, R), jnp.int32),
            pltpu.VMEM((FFL, D), BF16),
            pltpu.VMEM((FFL, D), BF16),
            pltpu.VMEM((FFL, R), BF16),
            pltpu.VMEM((R, R), BF16),
            pltpu.VMEM((ROWS, COORDS), BF16),
            pltpu.VMEM((FFL, CHUNK), F32),
            pltpu.VMEM((FFL, CHUNK), F32),
            pltpu.VMEM((EX, 8, R), jnp.int32),
            pltpu.VMEM((GROUP, R, R), F32),
            pltpu.VMEM((GROUP, R, R), F32),
            pltpu.VMEM((ZH, R, R), F32),
            pltpu.VMEM((GROUP, R, R), F32),
            pltpu.VMEM((CHUNKS, 2, ZH, 4, 8, R), F32),
            pltpu.VMEM((CHUNKS, GROUP, ZH, 8, R), F32),
            pltpu.VMEM((CHUNKS, ZH, 8, R), F32),
            pltpu.VMEM((16 * EX, R), F32),
            pltpu.VMEM((2, GROUP, 2 * Q, R), F32),
            pltpu.VMEM((2, GROUP, 2 * Q, R), F32),
            pltpu.VMEM((2, ZH, 2 * Q, R), F32),
            pltpu.VMEM((2, GROUP, Q, R), F32),
            pltpu.VMEM((EX, 16 + Q, R), F32),
            pltpu.VMEM((EX, 16 + Q, R), F32),
            pltpu.VMEM((EX, 16, R), F32),
            pltpu.VMEM((EX, Q, R), F32),
            pltpu.VMEM((EX, 256, R), F32),
            pltpu.VMEM((EX, 256, R), F32),
            pltpu.VMEM((2, ROWS, R), F32),
            pltpu.VMEM((Q, R), jnp.int32),
            pltpu.SMEM((Q, R), jnp.int32),
            pltpu.SemaphoreType.DMA((7,)),
            pltpu.SemaphoreType.DMA((CHUNKS,)),
            pltpu.SemaphoreType.DMA((2, KSTEPS)),
            pltpu.SemaphoreType.DMA((len(PHASES),)),
            pltpu.SemaphoreType.DMA((len(PHASES),)),
        ],
        compiler_params=pltpu.CompilerParams(
            collective_id=0, has_side_effects=True, vmem_limit_bytes=60 * 1024 * 1024
        ),
        name="logra",
    )(
        query_states,
        out_cotangent,
        query_of_token.reshape(8, R),
        gate_weight.T,
        up_weight.T,
        proj_in,
        proj_out,
        database,
        stored_ids.reshape(8, R),
    )
    return sol.T, scores.T


def solution(mesh):
    both = ("tp", "co")
    in_specs = (
        P("ex", None),
        P("ex", both),
        P("ex"),
        P(None, both),
        P(None, both),
        P(both, None),
        P(both, None),
        P("ex", both),
        P("ex"),
    )
    out_specs = (P(both, None), P("ex", None))
    return jax.shard_map(local, mesh=mesh, in_specs=in_specs, out_specs=out_specs, check_vma=False)
```

```python
import functools
import math

import jax
import jax.numpy as jnp
from jax import lax
from jax.experimental import pallas as pl
from jax.experimental.pallas import tpu as pltpu
from jax.sharding import PartitionSpec as P

D = 4096
FFL = 448
TOK = 1024
CHUNK = 256
CHUNKS = TOK // CHUNK
R = 128
Q = 32
QPG = 4
COORDS = 512
ROWS = 1024
EX = 8
GROUP = 8
ZH = 4
K = 16384
NSTORE = 8192
DAMPING = 1.0
HIGHEST = lax.Precision.HIGHEST
MESH = pl.DeviceIdType.MESH
F32 = jnp.float32
BF16 = jnp.bfloat16

PHASES = (
    ["ids", "r1", "r2", "r3"]
    + [f"l1{c}" for c in range(CHUNKS)]
    + ["l2", "gz", "b", "z1", "zg", "z3", "c1"]
    + [f"{name}{k}" for name in ("y1", "y2", "y3", "g1", "g2", "sa", "sb", "fa", "fb") for k in (0, 1)]
)
PHASE = {name: at for at, name in enumerate(PHASES)}


def fdot(a, b, dims=((1,), (0,))):
    return lax.dot_general(a, b, (dims, ((), ())), precision=HIGHEST, preferred_element_type=F32)


def bdot(a, b, dims=((1,), (0,))):
    return lax.dot_general(a, b, (dims, ((), ())), preferred_element_type=F32)


TN = ((0,), (0,))
NT = ((1,), (1,))


def eliminated(matrix, target):
    n = matrix.shape[0]
    both = jnp.concatenate([matrix, target], axis=1)
    lines = lax.broadcasted_iota(jnp.int32, both.shape, 0)
    for k in range(n):
        row = both[k : k + 1, :] / both[k : k + 1, k : k + 1]
        both = jnp.where(lines == k, row, both - both[:, k : k + 1] * row)
    return both[:, n:]


def three_pass(a, b, dims):
    a_high, b_high = a.astype(BF16), b.astype(BF16)
    a_low, b_low = (a - a_high.astype(F32)).astype(BF16), (b - b_high.astype(F32)).astype(BF16)
    return bdot(a_high, b_high, dims) + bdot(a_low, b_high, dims) + bdot(a_high, b_low, dims)


def repeated_gram(a, b):
    return fdot(a, jnp.concatenate([b] * 4, axis=0), NT)


def folded(gram):
    groups = lax.broadcasted_iota(jnp.int32, (8, R), 1) // Q
    out = jnp.where(groups == 0, gram[:8], 0.0)
    for k in range(1, 4):
        out = jnp.where(groups == k, gram[8 * k : 8 * k + 8], out)
    return out


def unfolded(tile):
    parts = [tile] + [pltpu.roll(tile, R - Q * k, 1) for k in range(1, 4)]
    return jnp.concatenate(parts, axis=0)[:, :Q]


def summed(slots):
    total = slots[0]
    for s in slots[1:]:
        total = total + s
    return total


def kernel(
    q_hbm, cot_hbm, qot_hbm, gw_hbm, uw_hbm, pin_hbm, pout_hbm, db_hbm, ids_hbm,
    sol_ref, score_ref,
    q_v, cot_v, qot_v, gw_v, uw_v, pin_v, pout_v, db_v,
    ids_all, rsend, r1, r2s, r2, right,
    lsend, l1, l2s, l2, gsend, gz,
    bbuf,
    ysend, y1, y2, yfull, gram1_v, gram2_v,
    zsend, z1, zg, zfull,
    cbuf, s0, s1, picked, mask_v, where_v, where_s,
    small_sem, q_sem, w_sem, send_sem, recv_sem,
):
    tp = lax.axis_index("tp")
    e = lax.axis_index("ex")
    x = lax.axis_index("co")
    zh = tp // 2
    core = tp % 2
    g = core * 4 + x
    scale = 1.0 / math.sqrt(float(NSTORE))

    def in_group(p):
        return {"tp": zh * 2 + p // 4, "co": p % 4}

    def in_z(p):
        return {"tp": p * 2 + core}

    def in_ex(p):
        return {"ex": p}

    pending = {}

    def send(phase, src, dst, device):
        at = PHASE[phase]
        pltpu.make_async_remote_copy(
            src, dst, send_sem.at[at], recv_sem.at[at], device, MESH
        ).start()

    def push(phase, src_of, dst, me, n, device_of, slots):
        pending[phase] = slots
        for d in range(1, n):
            p = (me + d) % n
            send(phase, src_of(p), dst, device_of(p))

    def arrived(phase):
        slots = pending[phase]
        pltpu.make_async_copy(slots, slots, recv_sem.at[PHASE[phase]]).wait()

    def sent(phase):
        slots = pending.pop(phase)
        pltpu.make_async_copy(slots, slots, send_sem.at[PHASE[phase]]).wait()

    copies = [
        pltpu.make_async_copy(cot_hbm, cot_v, small_sem.at[0]),
        pltpu.make_async_copy(pout_hbm, pout_v, small_sem.at[1]),
        pltpu.make_async_copy(ids_hbm, ids_all.at[e], small_sem.at[2]),
        pltpu.make_async_copy(qot_hbm, qot_v, small_sem.at[3]),
        pltpu.make_async_copy(pin_hbm, pin_v, small_sem.at[4]),
        pltpu.make_async_copy(db_hbm, db_v, small_sem.at[5]),
        pltpu.make_async_copy(gw_hbm, gw_v, w_sem.at[0]),
        pltpu.make_async_copy(uw_hbm, uw_v, w_sem.at[1]),
    ]

    def q_copy(c):
        rows = pl.ds(c * CHUNK, CHUNK)
        return pltpu.make_async_copy(q_hbm.at[rows, :], q_v.at[rows, :], q_sem.at[c])

    for at in (0, 1, 2, 4):
        copies[at].start()
    q_copy(0).start()
    copies[6].start()
    copies[7].start()
    for c in range(1, CHUNKS):
        q_copy(c).start()
    copies[3].start()
    copies[5].start()

    barrier = pltpu.get_barrier_semaphore()
    for n, me, device_of in ((GROUP, g, in_group), (ZH, zh, in_z), (EX, e, in_ex)):
        for d in range(1, n):
            pl.semaphore_signal(
                barrier, inc=1, device_id=device_of((me + d) % n), device_id_type=MESH
            )

    copies[0].wait()
    copies[1].wait()
    rsend[...] = bdot(cot_v[...], pout_v[...]).reshape(ZH, GROUP, Q, R)
    copies[4].wait()
    old = lax.broadcasted_iota(jnp.int32, (R, R), 0)
    new = lax.broadcasted_iota(jnp.int32, (R, R), 1)
    moved = old == 32 * ((new >> 2) & 3) + 4 * (new >> 4) + (new & 3)
    proj = bdot(pin_v[...], jnp.where(moved, 1.0, 0.0).astype(BF16))
    pin_v[...] = proj.astype(BF16)
    copies[2].wait()

    pl.semaphore_wait(barrier, (GROUP - 1) + (ZH - 1) + (EX - 1))
    push(
        "r1", lambda p: rsend.at[:, p], r1.at[g], g, GROUP, in_group, r1.at[pl.ds(0, GROUP - 1)]
    )
    push(
        "ids", lambda p: ids_all.at[e], ids_all.at[e], e, EX, in_ex, ids_all.at[pl.ds(0, EX - 1)]
    )
    r1[g] = rsend[:, g]
    copies[6].wait()
    copies[7].wait()

    def matmul(c):
        q_copy(c).wait()
        a = q_v[c * CHUNK : (c + 1) * CHUNK, :]
        gate = bdot(gw_v[...], a, NT)
        up = bdot(uw_v[...], a, NT)
        hidden = ((gate / (1.0 + jnp.exp(-gate))) * up).astype(BF16)
        lsend[c] = bdot(pin_v[...], hidden, TN).reshape(GROUP, 16, CHUNK)
        push(
            f"l1{c}", lambda p: lsend.at[c, p], l1.at[c, g], g, GROUP, in_group,
            l1.at[c, pl.ds(0, GROUP - 1)],
        )
        l1[c, g] = lsend[c, g]

    pending["l2"] = l2.at[pl.ds(0, ZH - 1)]

    def left_second(c):
        arrived(f"l1{c}")
        l2s[c] = summed([l1[c, s] for s in range(GROUP)])

        @pl.when(zh != c)
        def _():
            send("l2", l2s.at[c], l2.at[zh], in_z(c))

        @pl.when(zh == c)
        def _():
            l2[zh] = l2s[c]

    matmul(0)
    matmul(1)
    left_second(0)
    matmul(2)
    left_second(1)
    matmul(3)

    arrived("r1")
    r2s[...] = summed([r1[s] for s in range(GROUP)])
    push("r2", lambda p: r2s.at[p], r2.at[zh], zh, ZH, in_z, r2.at[pl.ds(0, ZH - 1)])
    r2[zh] = r2s[zh]
    left_second(2)

    arrived("ids")
    kinds = lax.broadcasted_iota(jnp.int32, (Q, R), 0)
    lane = lax.broadcasted_iota(jnp.int32, (Q, R), 1)
    places = jnp.zeros((Q, 2 * Q), F32)
    places_t = jnp.zeros((Q, Q), F32)
    for d in range(EX):
        his, los = [], []
        for r in range(8):
            own = ids_all[(e + d) % EX, pl.ds(r, 1), :] - e * ROWS
            hit_low = (own & 31) == kinds
            part = d + 8 * (r % 2) + 16 * (r // 2)
            his.append(jnp.where((own >> 5) == kinds, 1.0, 0.0).astype(BF16))
            los.append(
                jnp.concatenate(
                    [
                        jnp.where(hit_low, float(part), 0.0),
                        jnp.where(hit_low, lane.astype(F32), 0.0),
                    ],
                    axis=0,
                ).astype(BF16)
            )
        his = jnp.concatenate(his, axis=1)
        los = jnp.concatenate(los, axis=1)
        places = places + bdot(his, los, NT)
        places_t = places_t + bdot(los[:Q], his, NT)
    at = (places[:, :Q].astype(jnp.int32) & 15) * R + places[:, Q:].astype(jnp.int32)
    where_v[...] = jnp.concatenate([at] * 4, axis=1)
    to_scalar = pltpu.make_async_copy(where_v, where_s, small_sem.at[6])
    to_scalar.start()
    group_t = places_t.astype(jnp.int32) >> 4
    for hi in range(Q):
        mask_v[hi * Q : (hi + 1) * Q, :] = jnp.where(
            group_t[:, hi : hi + 1] == (lane >> 5), 1.0, 0.0
        )

    arrived("r2")
    right[g] = summed([r2[s] for s in range(ZH)])
    push(
        "r3", lambda p: right.at[g], right.at[g], g, GROUP, in_group,
        right.at[pl.ds(0, GROUP - 1)],
    )
    left_second(3)
    copies[3].wait()
    query = (
        jnp.concatenate([qot_v[pl.ds(2 * zh, 1), :], qot_v[pl.ds(2 * zh + 1, 1), :]], axis=1)
        - e * QPG
    )
    arrived("r3")
    arrived("l2")
    left = summed([l2[s] for s in range(ZH)])
    weighted = jnp.concatenate([jnp.where(query == k, left, 0.0) for k in range(QPG)], axis=0)
    grads = fdot(weighted, right[...].reshape(CHUNK, R))
    low = lax.broadcasted_iota(jnp.int32, (8, R), 0) < 4
    for p in range(ZH):
        for pair in range(2):
            one, two = [
                grads[q * 16 + 8 * (p // 2) : q * 16 + 8 * (p // 2) + 8]
                for q in (2 * pair, 2 * pair + 1)
            ]
            if p % 2:
                tile = jnp.where(low, pltpu.roll(one, 4, 0), two)
            else:
                tile = jnp.where(low, one, pltpu.roll(two, 4, 0))
            gsend[p, 8 * pair : 8 * pair + 8] = tile
    push("gz", lambda p: gsend.at[p], gz.at[zh], zh, ZH, in_z, gz.at[pl.ds(0, ZH - 1)])
    gz[zh] = gsend[zh]
    arrived("gz")
    own_rows = pl.ds(pl.multiple_of(e * 16, 16), 16)
    bbuf[own_rows, :] = summed([gz[s] for s in range(ZH)])
    push(
        "b", lambda p: bbuf.at[own_rows, :], bbuf.at[own_rows, :], e, EX, in_ex,
        bbuf.at[pl.ds(0, 16 * (EX - 1)), :],
    )
    copies[5].wait()
    arrived("b")
    base = jnp.concatenate([bbuf[pl.ds(i, Q, stride=4), :] for i in range(4)], axis=1)

    def first_stage(k, vectors):
        part = bdot(vectors.astype(BF16), db_v[...], NT)
        for p in range(GROUP):
            ysend[k, p] = part[:, p * R : (p + 1) * R]
        push(
            f"y1{k}", lambda p: ysend.at[k, p], y1.at[k, g], g, GROUP, in_group,
            y1.at[k, pl.ds(0, GROUP - 1)],
        )
        y1[k, g] = ysend[k, g]

    def first_grams(k, tiles):
        rows = pl.ds(0, 8 * len(tiles))
        gram1_v[k, g, rows] = jnp.concatenate(tiles, axis=0)
        push(
            f"g1{k}", lambda p: gram1_v.at[k, g, rows], gram1_v.at[k, g, rows], g, GROUP, in_group,
            gram1_v.at[k, pl.ds(0, GROUP - 1), rows],
        )

    def second_stage(k):
        arrived(f"y1{k}")
        y2[k, zh] = summed([y1[k, s] for s in range(GROUP)])
        push(
            f"y2{k}", lambda p: y2.at[k, zh], y2.at[k, zh], zh, ZH, in_z,
            y2.at[k, pl.ds(0, ZH - 1)],
        )

    def second_grams(k, count):
        rows = pl.ds(0, 8 * count)
        arrived(f"g1{k}")
        gram2_v[k, zh, rows] = summed([gram1_v[k, s, rows] for s in range(GROUP)])
        push(
            f"g2{k}", lambda p: gram2_v.at[k, zh, rows], gram2_v.at[k, zh, rows], zh, ZH, in_z,
            gram2_v.at[k, pl.ds(0, ZH - 1), rows],
        )

    def third_stage(k):
        arrived(f"y2{k}")
        yfull[k, g] = summed([y2[k, s] for s in range(ZH)])
        push(
            f"y3{k}", lambda p: yfull.at[k, g], yfull.at[k, g], g, GROUP, in_group,
            yfull.at[k, pl.ds(0, GROUP - 1)],
        )

    def grams_of(k, count):
        rows = pl.ds(0, 8 * count)
        arrived(f"g2{k}")
        total = summed([gram2_v[k, s, rows] for s in range(ZH)])
        return [unfolded(total[8 * at : 8 * at + 8]) for at in range(count)]

    def rows_of(k):
        arrived(f"y3{k}")
        return [yfull[k, s] for s in range(GROUP)]

    def own_packed(buf, blocks):
        for h in range(2):
            tall = jnp.concatenate([blocks[2 * i + h] for i in range(4)], axis=0)
            buf[h * ROWS : h * ROWS + R, :] = tall.T

    def half(d, count=1):
        return pl.ds(pl.multiple_of(core * ROWS + d * R, R), count * R)

    def spread(k, buf):
        for name, lo, hi in (("sa", 4, 8), ("sb", 1, 4)):
            pending[f"{name}{k}"] = buf.at[half(lo, hi - lo), :]
            for slot in range(lo, hi):
                send(f"{name}{k}", buf.at[half(0), :], buf.at[half(slot), :], in_ex((e - slot) % EX))

    def forward(k, buf, name):
        lo, hi = (4, 8) if name == "a" else (1, 4)
        arrived(f"s{name}{k}")
        part = buf.at[half(lo, hi - lo), :]
        pending[f"f{name}{k}"] = part
        send(f"f{name}{k}", part, part, {"tp": zh * 2 + (1 - core)})

    first_stage(0, base)
    first_grams(0, [folded(repeated_gram(base, base))])
    second_stage(0)
    second_grams(0, 1)
    third_stage(0)
    (norm0,) = grams_of(0, 1)
    eye = (
        lax.broadcasted_iota(jnp.int32, (Q, Q), 0) == lax.broadcasted_iota(jnp.int32, (Q, Q), 1)
    ).astype(F32)
    inverse0 = eliminated(norm0, eye)
    blocks0 = rows_of(0)
    rows0 = jnp.concatenate(blocks0, axis=1)

    back = bdot((rows0 * scale).astype(BF16), db_v[...])
    for p in range(EX):
        zsend[p] = back[16 * (p // 4) : 16 * (p // 4) + 16, (p % 4) * R : (p % 4 + 1) * R]
    push("z1", lambda p: zsend.at[p], z1.at[e], e, EX, in_ex, z1.at[pl.ds(0, EX - 1)])
    z1[e] = zsend[e]
    zg[e] = folded(repeated_gram(rows0, rows0))
    push("zg", lambda p: zg.at[e], zg.at[e], e, EX, in_ex, zg.at[pl.ds(0, EX - 1)])
    own_packed(s0, blocks0)
    arrived("z1")
    zfull[e] = summed([z1[s] for s in range(EX)])
    push("z3", lambda p: zfull.at[e], zfull.at[e], e, EX, in_ex, zfull.at[pl.ds(0, EX - 1)])
    arrived("zg")
    row_gram = unfolded(summed([zg[s] for s in range(EX)]))
    step0 = eliminated(row_gram * (scale * scale) + DAMPING * norm0, norm0)
    arrived("z3")
    spread(0, s0)
    back = jnp.concatenate(
        [jnp.concatenate([zfull[4 * h + j] for j in range(4)], axis=1) for h in range(2)], axis=0
    )
    image = back * scale + DAMPING * base
    residual = base - fdot(step0, image, TN)

    first_stage(1, residual)
    first_grams(
        1, [folded(repeated_gram(residual, residual)), folded(repeated_gram(residual, base))]
    )
    second_stage(1)
    second_grams(1, 2)
    forward(0, s0, "a")
    forward(0, s0, "b")
    to_scalar.wait()
    third_stage(1)
    norm1, cross = grams_of(1, 2)
    mixing = fdot(inverse0, norm1)

    def pick(source, side):
        def line(hi, carry):
            for lo in range(Q):
                at = where_s[hi, lo] & (2 * ROWS - 1)
                picked[side, pl.ds(hi * Q + lo, 1), :] = source[pl.ds(at, 1), :]
            return carry

        lax.fori_loop(0, Q, line, 0)

    arrived("fa0")
    arrived("fb0")
    pick(s0, 0)
    blocks1 = rows_of(1)
    rows1 = jnp.concatenate(blocks1, axis=1) + fdot(mixing, rows0, TN)
    cbuf[e] = folded(repeated_gram(rows1, rows1))
    push("c1", lambda p: cbuf.at[e], cbuf.at[e], e, EX, in_ex, cbuf.at[pl.ds(0, EX - 1)])
    own_packed(s1, blocks1)
    spread(1, s1)
    gram = (
        norm1
        + fdot(cross, mixing)
        + fdot(mixing, cross, ((0,), (1,)))
        + fdot(mixing, fdot(norm0, mixing), TN)
    )
    arrived("c1")
    row_gram = unfolded(summed([cbuf[s] for s in range(EX)]))
    step1 = eliminated(row_gram * (scale * scale) + DAMPING * gram, norm1)
    forward(1, s1, "a")
    first = step0 + fdot(mixing, step1)
    sol_ref[...] = fdot(first, base, TN) + fdot(step1, residual, TN)
    forward(1, s1, "b")
    arrived("fa1")
    arrived("fb1")
    pick(s1, 1)
    mask = mask_v[...]
    chosen = jnp.concatenate([picked[0] * mask, picked[1] * mask], axis=1)
    coeffs = jnp.concatenate([first] * 4 + [step1] * 4, axis=0) * (1.0 / math.sqrt(K))
    score_ref[...] = three_pass(coeffs, chosen, ((0,), (1,)))

    for phase in list(pending):
        sent(phase)


def local(
    query_states, out_cotangent, query_of_token, gate_weight, up_weight, proj_in, proj_out,
    database, stored_ids,
):
    anywhere = pl.BlockSpec(memory_space=pl.ANY)
    vmem = pl.BlockSpec(memory_space=pltpu.VMEM)
    sol, scores = pl.pallas_call(
        kernel,
        out_shape=(
            jax.ShapeDtypeStruct((Q, COORDS), F32),
            jax.ShapeDtypeStruct((Q, ROWS), F32),
        ),
        in_specs=[anywhere] * 9,
        out_specs=(vmem, vmem),
        scratch_shapes=[
            pltpu.VMEM((TOK, D), BF16),
            pltpu.VMEM((TOK, R), BF16),
            pltpu.VMEM((8, R), jnp.int32),
            pltpu.VMEM((FFL, D), BF16),
            pltpu.VMEM((FFL, D), BF16),
            pltpu.VMEM((FFL, R), BF16),
            pltpu.VMEM((R, R), BF16),
            pltpu.VMEM((ROWS, COORDS), BF16),
            pltpu.VMEM((EX, 8, R), jnp.int32),
            pltpu.VMEM((ZH, GROUP, Q, R), F32),
            pltpu.VMEM((GROUP, ZH, Q, R), F32),
            pltpu.VMEM((ZH, Q, R), F32),
            pltpu.VMEM((ZH, Q, R), F32),
            pltpu.VMEM((GROUP, Q, R), F32),
            pltpu.VMEM((CHUNKS, GROUP, 16, CHUNK), F32),
            pltpu.VMEM((CHUNKS, GROUP, 16, CHUNK), F32),
            pltpu.VMEM((CHUNKS, 16, CHUNK), F32),
            pltpu.VMEM((ZH, 16, CHUNK), F32),
            pltpu.VMEM((ZH, 16, R), F32),
            pltpu.VMEM((ZH, 16, R), F32),
            pltpu.VMEM((16 * EX, R), F32),
            pltpu.VMEM((2, GROUP, Q, R), F32),
            pltpu.VMEM((2, GROUP, Q, R), F32),
            pltpu.VMEM((2, ZH, Q, R), F32),
            pltpu.VMEM((2, GROUP, Q, R), F32),
            pltpu.VMEM((2, GROUP, 16, R), F32),
            pltpu.VMEM((2, ZH, 16, R), F32),
            pltpu.VMEM((EX, 16, R), F32),
            pltpu.VMEM((EX, 16, R), F32),
            pltpu.VMEM((EX, 8, R), F32),
            pltpu.VMEM((EX, 16, R), F32),
            pltpu.VMEM((EX, 8, R), F32),
            pltpu.VMEM((2 * ROWS, R), F32),
            pltpu.VMEM((2 * ROWS, R), F32),
            pltpu.VMEM((2, ROWS, R), F32),
            pltpu.VMEM((ROWS, R), F32),
            pltpu.VMEM((Q, R), jnp.int32),
            pltpu.SMEM((Q, R), jnp.int32),
            pltpu.SemaphoreType.DMA((7,)),
            pltpu.SemaphoreType.DMA((CHUNKS,)),
            pltpu.SemaphoreType.DMA((2,)),
            pltpu.SemaphoreType.DMA((len(PHASES),)),
            pltpu.SemaphoreType.DMA((len(PHASES),)),
        ],
        compiler_params=pltpu.CompilerParams(
            collective_id=0, has_side_effects=True, vmem_limit_bytes=60 * 1024 * 1024
        ),
        name="logra",
    )(
        query_states,
        out_cotangent,
        query_of_token.reshape(8, R),
        gate_weight.T,
        up_weight.T,
        proj_in,
        proj_out,
        database,
        stored_ids.reshape(8, R),
    )
    return sol.T, scores.T


def solution(mesh):
    both = ("tp", "co")
    in_specs = (
        P("ex", None),
        P("ex", both),
        P("ex"),
        P(None, both),
        P(None, both),
        P(both, None),
        P(both, None),
        P("ex", both),
        P("ex"),
    )
    out_specs = (P(both, None), P("ex", None))
    return jax.shard_map(local, mesh=mesh, in_specs=in_specs, out_specs=out_specs, check_vma=False)
```

```python
import functools
import math

import jax
import jax.numpy as jnp
from jax import lax
from jax.experimental import pallas as pl
from jax.experimental.pallas import tpu as pltpu
from jax.sharding import PartitionSpec as P

D = 4096
FFL = 448
TOK = 1024
CHUNK = 256
CHUNKS = TOK // CHUNK
R = 128
Q = 32
QPG = 4
COORDS = 512
ROWS = 1024
EX = 8
GROUP = 8
ZH = 4
K = 16384
NSTORE = 8192
DAMPING = 1.0
HIGHEST = lax.Precision.HIGHEST
MESH = pl.DeviceIdType.MESH
F32 = jnp.float32
BF16 = jnp.bfloat16

PHASES = (
    ["ids", "r1", "r2", "r3"]
    + [f"l1{c}" for c in range(CHUNKS)]
    + ["l2", "gz", "b", "z1", "zg", "z3", "c1", "c2"]
    + [f"{name}{k}" for name in ("y1", "y2", "y3", "g1", "g2", "sa", "sb", "fa", "fb") for k in (0, 1)]
)
FAR_FIRST = {4: (2, 1), 5: (1, 1), 6: (3, 1), 7: (2, 0), 1: (1, 0), 2: (3, 0), 3: (0, 1)}
PHASE = {name: at for at, name in enumerate(PHASES)}


def fdot(a, b, dims=((1,), (0,))):
    return lax.dot_general(a, b, (dims, ((), ())), precision=HIGHEST, preferred_element_type=F32)


def bdot(a, b, dims=((1,), (0,))):
    return lax.dot_general(a, b, (dims, ((), ())), preferred_element_type=F32)


TN = ((0,), (0,))
NT = ((1,), (1,))


def eliminated(matrix, target):
    n = matrix.shape[0]
    both = jnp.concatenate([matrix, target], axis=1)
    lines = lax.broadcasted_iota(jnp.int32, both.shape, 0)
    for k in range(n):
        row = both[k : k + 1, :] / both[k : k + 1, k : k + 1]
        both = jnp.where(lines == k, row, both - both[:, k : k + 1] * row)
    return both[:, n:]


def three_pass(a, b, dims):
    a_high, b_high = a.astype(BF16), b.astype(BF16)
    a_low, b_low = (a - a_high.astype(F32)).astype(BF16), (b - b_high.astype(F32)).astype(BF16)
    return bdot(a_high, b_high, dims) + bdot(a_low, b_high, dims) + bdot(a_high, b_low, dims)


def repeated_gram(a, b):
    return fdot(a, jnp.concatenate([b] * 4, axis=0), NT)


def folded(gram):
    groups = lax.broadcasted_iota(jnp.int32, (8, R), 1) // Q
    out = jnp.where(groups == 0, gram[:8], 0.0)
    for k in range(1, 4):
        out = jnp.where(groups == k, gram[8 * k : 8 * k + 8], out)
    return out


def unfolded(tile):
    parts = [tile] + [pltpu.roll(tile, R - Q * k, 1) for k in range(1, 4)]
    return jnp.concatenate(parts, axis=0)[:, :Q]


def summed(slots):
    total = slots[0]
    for s in slots[1:]:
        total = total + s
    return total


def kernel(
    q_hbm, cot_hbm, qot_hbm, gw_hbm, uw_hbm, pin_hbm, pout_hbm, db_hbm, ids_hbm,
    out_ref,
    q_v, cot_v, qot_v, gw_v, uw_v, pin_v, pout_v, db_v,
    ids_all, rsend, r1, r2s, r2, right,
    lsend, l1, l2s, l2, gsend, gz,
    bbuf,
    ysend, y1, y2, yfull, gram1_v, gram2_v,
    zsend, z1, zg, zfull,
    cbuf, dbuf, s0, s1, picked, mask_v, where_v, where_s,
    small_sem, q_sem, w_sem, send_sem, recv_sem,
):
    tp = lax.axis_index("tp")
    e = lax.axis_index("ex")
    x = lax.axis_index("co")
    zh = tp // 2
    core = tp % 2
    g = core * 4 + x
    scale = 1.0 / math.sqrt(float(NSTORE))

    def in_group(p):
        return {"tp": zh * 2 + p // 4, "co": p % 4}

    def in_z(p):
        return {"tp": p * 2 + core}

    def in_ex(p):
        return {"ex": p}

    y, z_lo = e // 2, e % 2

    def peers(me, n):
        if n == ZH:
            return [(zh + d) % ZH for d in (2, 1, 3)]
        if me is e:
            return [
                ((y + dy) % 4) * 2 + (z_lo + dz) % 2
                for dy, dz in ((2, 1), (2, 0), (1, 1), (3, 1), (1, 0), (3, 0), (0, 1))
            ]
        return [
            ((core + dc) % 2) * 4 + (x + dx) % 4
            for dx, dc in ((2, 1), (2, 0), (1, 1), (3, 1), (1, 0), (3, 0), (0, 1))
        ]

    pending = {}

    def send(phase, src, dst, device):
        at = PHASE[phase]
        pltpu.make_async_remote_copy(
            src, dst, send_sem.at[at], recv_sem.at[at], device, MESH
        ).start()

    def push(phase, src_of, dst, me, n, device_of, slots):
        pending[phase] = slots
        for p in peers(me, n):
            send(phase, src_of(p), dst, device_of(p))

    def arrived(phase):
        slots = pending[phase]
        pltpu.make_async_copy(slots, slots, recv_sem.at[PHASE[phase]]).wait()

    def sent(phase):
        slots = pending.pop(phase)
        pltpu.make_async_copy(slots, slots, send_sem.at[PHASE[phase]]).wait()

    copies = [
        pltpu.make_async_copy(cot_hbm, cot_v, small_sem.at[0]),
        pltpu.make_async_copy(pout_hbm, pout_v, small_sem.at[1]),
        pltpu.make_async_copy(ids_hbm, ids_all.at[e], small_sem.at[2]),
        pltpu.make_async_copy(qot_hbm, qot_v, small_sem.at[3]),
        pltpu.make_async_copy(pin_hbm, pin_v, small_sem.at[4]),
        pltpu.make_async_copy(db_hbm, db_v, small_sem.at[5]),
        pltpu.make_async_copy(gw_hbm, gw_v, w_sem.at[0]),
        pltpu.make_async_copy(uw_hbm, uw_v, w_sem.at[1]),
    ]

    def q_copy(c):
        rows = pl.ds(c * CHUNK, CHUNK)
        return pltpu.make_async_copy(q_hbm.at[rows, :], q_v.at[rows, :], q_sem.at[c])

    barrier = pltpu.get_barrier_semaphore()
    for n, me, device_of in ((ZH, zh, in_z), (EX, e, in_ex), (GROUP, g, in_group)):
        for p in peers(me, n):
            pl.semaphore_signal(barrier, inc=1, device_id=device_of(p), device_id_type=MESH)

    for at in (0, 1, 2, 4):
        copies[at].start()
    q_copy(0).start()
    copies[6].start()
    copies[7].start()
    for c in range(1, CHUNKS):
        q_copy(c).start()
    copies[3].start()
    copies[5].start()

    copies[0].wait()
    copies[1].wait()
    rsend[...] = bdot(cot_v[...], pout_v[...]).reshape(ZH, GROUP, Q, R)
    copies[2].wait()

    pl.semaphore_wait(barrier, (GROUP - 1) + (ZH - 1) + (EX - 1))
    push(
        "r1", lambda p: rsend.at[:, p], r1.at[g], g, GROUP, in_group, r1.at[pl.ds(0, GROUP - 1)]
    )
    push(
        "ids", lambda p: ids_all.at[e], ids_all.at[e], e, EX, in_ex, ids_all.at[pl.ds(0, EX - 1)]
    )
    r1[g] = rsend[:, g]
    copies[4].wait()
    old = lax.broadcasted_iota(jnp.int32, (R, R), 0)
    new = lax.broadcasted_iota(jnp.int32, (R, R), 1)
    moved = old == 32 * ((new >> 2) & 3) + 4 * (new >> 4) + (new & 3)
    proj = bdot(pin_v[...], jnp.where(moved, 1.0, 0.0).astype(BF16))
    pin_v[...] = proj.astype(BF16)
    copies[6].wait()
    copies[7].wait()

    def matmul(c):
        q_copy(c).wait()
        a = q_v[c * CHUNK : (c + 1) * CHUNK, :]
        gate = bdot(gw_v[...], a, NT)
        up = bdot(uw_v[...], a, NT)
        hidden = ((gate / (1.0 + jnp.exp(-gate))) * up).astype(BF16)
        lsend[c] = bdot(pin_v[...], hidden, TN).reshape(GROUP, 16, CHUNK)
        push(
            f"l1{c}", lambda p: lsend.at[c, p], l1.at[c, g], g, GROUP, in_group,
            l1.at[c, pl.ds(0, GROUP - 1)],
        )
        l1[c, g] = lsend[c, g]

    def left_second(c):
        pending["l2"] = l2.at[pl.ds(0, ZH - 1)]
        arrived(f"l1{c}")
        l2s[c] = summed([l1[c, s] for s in range(GROUP)])

        @pl.when(zh != c)
        def _():
            send("l2", l2s.at[c], l2.at[zh], in_z(c))

        @pl.when(zh == c)
        def _():
            l2[zh] = l2s[c]

    matmul(0)
    matmul(1)
    matmul(2)
    arrived("r1")
    r2s[...] = summed([r1[s] for s in range(GROUP)])
    push("r2", lambda p: r2s.at[p], r2.at[zh], zh, ZH, in_z, r2.at[pl.ds(0, ZH - 1)])
    r2[zh] = r2s[zh]
    matmul(3)
    left_second(0)
    left_second(1)
    left_second(2)

    arrived("ids")
    kinds = lax.broadcasted_iota(jnp.int32, (Q, R), 0)
    lane = lax.broadcasted_iota(jnp.int32, (Q, R), 1)
    places = jnp.zeros((Q, 2 * Q), F32)
    places_t = jnp.zeros((Q, Q), F32)
    for d in range(EX):
        dy, dz = FAR_FIRST[d] if d else (0, 0)
        source = ((y + dy) % 4) * 2 + (z_lo + dz) % 2
        his, los = [], []
        for r in range(8):
            own = ids_all[source, pl.ds(r, 1), :] - e * ROWS
            hit_low = (own & 31) == kinds
            part = d + 8 * (r % 2) + 16 * (r // 2)
            his.append(jnp.where((own >> 5) == kinds, 1.0, 0.0).astype(BF16))
            los.append(
                jnp.concatenate(
                    [
                        jnp.where(hit_low, float(part), 0.0),
                        jnp.where(hit_low, lane.astype(F32), 0.0),
                    ],
                    axis=0,
                ).astype(BF16)
            )
        his = jnp.concatenate(his, axis=1)
        los = jnp.concatenate(los, axis=1)
        places = places + bdot(his, los, NT)
        places_t = places_t + bdot(los[:Q], his, NT)
    at = (places[:, :Q].astype(jnp.int32) & 15) * R + places[:, Q:].astype(jnp.int32)
    where_v[...] = jnp.concatenate([at] * 4, axis=1)
    to_scalar = pltpu.make_async_copy(where_v, where_s, small_sem.at[6])
    to_scalar.start()
    group_t = places_t.astype(jnp.int32) >> 4
    for hi in range(Q):
        mask_v[hi * Q : (hi + 1) * Q, :] = jnp.where(
            group_t[:, hi : hi + 1] == (lane >> 5), 1.0, 0.0
        )

    arrived("r2")
    right[g] = summed([r2[s] for s in range(ZH)])
    push(
        "r3", lambda p: right.at[g], right.at[g], g, GROUP, in_group,
        right.at[pl.ds(0, GROUP - 1)],
    )
    left_second(3)
    copies[3].wait()
    query = (
        jnp.concatenate([qot_v[pl.ds(2 * zh, 1), :], qot_v[pl.ds(2 * zh + 1, 1), :]], axis=1)
        - e * QPG
    )
    arrived("r3")
    arrived("l2")
    left = summed([l2[s] for s in range(ZH)])
    weighted = jnp.concatenate([jnp.where(query == k, left, 0.0) for k in range(QPG)], axis=0)
    grads = fdot(weighted, right[...].reshape(CHUNK, R))
    low = lax.broadcasted_iota(jnp.int32, (8, R), 0) < 4
    for p in range(ZH):
        for pair in range(2):
            one, two = [
                grads[q * 16 + 8 * (p // 2) : q * 16 + 8 * (p // 2) + 8]
                for q in (2 * pair, 2 * pair + 1)
            ]
            if p % 2:
                tile = jnp.where(low, pltpu.roll(one, 4, 0), two)
            else:
                tile = jnp.where(low, one, pltpu.roll(two, 4, 0))
            gsend[p, 8 * pair : 8 * pair + 8] = tile
    push("gz", lambda p: gsend.at[p], gz.at[zh], zh, ZH, in_z, gz.at[pl.ds(0, ZH - 1)])
    gz[zh] = gsend[zh]
    arrived("gz")
    own_rows = pl.ds(pl.multiple_of(e * 16, 16), 16)
    bbuf[own_rows, :] = summed([gz[s] for s in range(ZH)])
    push(
        "b", lambda p: bbuf.at[own_rows, :], bbuf.at[own_rows, :], e, EX, in_ex,
        bbuf.at[pl.ds(0, 16 * (EX - 1)), :],
    )
    copies[5].wait()
    arrived("b")
    base = jnp.concatenate([bbuf[pl.ds(i, Q, stride=4), :] for i in range(4)], axis=1)

    def first_stage(k, vectors):
        part = bdot(vectors.astype(BF16), db_v[...], NT)
        for p in range(GROUP):
            ysend[k, p] = part[:, p * R : (p + 1) * R]
        push(
            f"y1{k}", lambda p: ysend.at[k, p], y1.at[k, g], g, GROUP, in_group,
            y1.at[k, pl.ds(0, GROUP - 1)],
        )
        y1[k, g] = ysend[k, g]

    def first_grams(k, tiles):
        rows = pl.ds(0, 8 * len(tiles))
        gram1_v[k, g, rows] = jnp.concatenate(tiles, axis=0)
        push(
            f"g1{k}", lambda p: gram1_v.at[k, g, rows], gram1_v.at[k, g, rows], g, GROUP, in_group,
            gram1_v.at[k, pl.ds(0, GROUP - 1), rows],
        )

    def second_stage(k):
        arrived(f"y1{k}")
        y2[k, zh] = summed([y1[k, s] for s in range(GROUP)])
        push(
            f"y2{k}", lambda p: y2.at[k, zh], y2.at[k, zh], zh, ZH, in_z,
            y2.at[k, pl.ds(0, ZH - 1)],
        )

    def second_grams(k, count):
        rows = pl.ds(0, 8 * count)
        arrived(f"g1{k}")
        gram2_v[k, zh, rows] = summed([gram1_v[k, s, rows] for s in range(GROUP)])
        push(
            f"g2{k}", lambda p: gram2_v.at[k, zh, rows], gram2_v.at[k, zh, rows], zh, ZH, in_z,
            gram2_v.at[k, pl.ds(0, ZH - 1), rows],
        )

    def third_stage(k):
        arrived(f"y2{k}")
        yfull[k, g] = summed([y2[k, s] for s in range(ZH)])
        push(
            f"y3{k}", lambda p: yfull.at[k, g], yfull.at[k, g], g, GROUP, in_group,
            yfull.at[k, pl.ds(0, GROUP - 1)],
        )

    def grams_of(k, count):
        rows = pl.ds(0, 8 * count)
        arrived(f"g2{k}")
        total = summed([gram2_v[k, s, rows] for s in range(ZH)])
        return [unfolded(total[8 * at : 8 * at + 8]) for at in range(count)]

    def rows_of(k):
        arrived(f"y3{k}")
        return [yfull[k, s] for s in range(GROUP)]

    def own_packed(buf, blocks):
        for h in range(2):
            tall = jnp.concatenate([blocks[2 * i + h] for i in range(4)], axis=0)
            buf[h * ROWS : h * ROWS + R, :] = tall.T

    def half(d, count=1):
        return pl.ds(pl.multiple_of(core * ROWS + d * R, R), count * R)

    def spread(k, buf):
        for name, lo, hi in (("sa", 4, 8), ("sb", 1, 4)):
            pending[f"{name}{k}"] = buf.at[half(lo, hi - lo), :]
            for slot in range(lo, hi):
                dy, dz = FAR_FIRST[slot]
                p = ((y - dy) % 4) * 2 + (z_lo + dz) % 2
                send(f"{name}{k}", buf.at[half(0), :], buf.at[half(slot), :], in_ex(p))

    def forward(k, buf, name):
        lo, hi = (4, 8) if name == "a" else (1, 4)
        arrived(f"s{name}{k}")
        part = buf.at[half(lo, hi - lo), :]
        pending[f"f{name}{k}"] = part
        send(f"f{name}{k}", part, part, {"tp": zh * 2 + (1 - core)})

    first_stage(0, base)
    first_grams(0, [folded(repeated_gram(base, base))])
    second_stage(0)
    second_grams(0, 1)
    third_stage(0)
    (norm0,) = grams_of(0, 1)
    eye = (
        lax.broadcasted_iota(jnp.int32, (Q, Q), 0) == lax.broadcasted_iota(jnp.int32, (Q, Q), 1)
    ).astype(F32)
    inverse0 = eliminated(norm0, eye)
    blocks0 = rows_of(0)
    rows0 = jnp.concatenate(blocks0, axis=1)

    back = bdot((rows0 * scale).astype(BF16), db_v[...])
    for p in range(EX):
        zsend[p] = back[16 * (p // 4) : 16 * (p // 4) + 16, (p % 4) * R : (p % 4 + 1) * R]
    push("z1", lambda p: zsend.at[p], z1.at[e], e, EX, in_ex, z1.at[pl.ds(0, EX - 1)])
    z1[e] = zsend[e]
    zg[e] = folded(repeated_gram(rows0, rows0))
    push("zg", lambda p: zg.at[e], zg.at[e], e, EX, in_ex, zg.at[pl.ds(0, EX - 1)])
    own_packed(s0, blocks0)
    arrived("z1")
    zfull[e] = summed([z1[s] for s in range(EX)])
    push("z3", lambda p: zfull.at[e], zfull.at[e], e, EX, in_ex, zfull.at[pl.ds(0, EX - 1)])
    arrived("zg")
    row_gram = unfolded(summed([zg[s] for s in range(EX)]))
    step0 = eliminated(row_gram * (scale * scale) + DAMPING * norm0, norm0)
    arrived("z3")
    spread(0, s0)
    back = jnp.concatenate(
        [jnp.concatenate([zfull[4 * h + j] for j in range(4)], axis=1) for h in range(2)], axis=0
    )
    image = back * scale + DAMPING * base
    residual = base - fdot(step0, image, TN)

    first_stage(1, residual)
    first_grams(
        1, [folded(repeated_gram(residual, residual)), folded(repeated_gram(residual, base))]
    )
    second_stage(1)
    second_grams(1, 2)
    forward(0, s0, "a")
    forward(0, s0, "b")
    to_scalar.wait()
    third_stage(1)
    block0, block1 = yfull[0, g], yfull[1, g]
    cbuf[e] = jnp.concatenate(
        [folded(repeated_gram(block1, block1)), folded(repeated_gram(block1, block0))], axis=0
    )
    push("c1", lambda p: cbuf.at[e], cbuf.at[e], e, EX, in_ex, cbuf.at[pl.ds(0, EX - 1)])
    norm1, cross = grams_of(1, 2)
    mixing = fdot(inverse0, norm1)

    def pick(source, side):
        def line(hi, carry):
            for lo in range(Q):
                at = where_s[hi, lo] & (2 * ROWS - 1)
                picked[side, pl.ds(hi * Q + lo, 1), :] = source[pl.ds(at, 1), :]
            return carry

        lax.fori_loop(0, Q, line, 0)

    blocks1 = rows_of(1)
    own_packed(s1, blocks1)
    arrived("c1")
    dbuf[g] = summed([cbuf[s] for s in range(EX)])
    push("c2", lambda p: dbuf.at[g], dbuf.at[g], g, GROUP, in_group, dbuf.at[pl.ds(0, GROUP - 1)])
    spread(1, s1)
    gram = (
        norm1
        + fdot(cross, mixing)
        + fdot(mixing, cross, ((0,), (1,)))
        + fdot(mixing, fdot(norm0, mixing), TN)
    )
    arrived("fa0")
    arrived("fb0")
    pick(s0, 0)
    arrived("c2")
    total = summed([dbuf[s] for s in range(GROUP)])
    square, mixed = unfolded(total[:8]), unfolded(total[8:])
    rows_gram = (
        square
        + fdot(mixed, mixing)
        + fdot(mixing, mixed, ((0,), (1,)))
        + fdot(mixing, fdot(row_gram, mixing), TN)
    )
    step1 = eliminated(rows_gram * (scale * scale) + DAMPING * gram, norm1)
    forward(1, s1, "a")
    first = step0 + fdot(mixing, step1)
    out_ref[:, :COORDS] = fdot(first, base, TN) + fdot(step1, residual, TN)
    forward(1, s1, "b")
    arrived("fa1")
    arrived("fb1")
    pick(s1, 1)
    mask = mask_v[...]
    chosen = jnp.concatenate([picked[0] * mask, picked[1] * mask], axis=1)
    coeffs = jnp.concatenate([first] * 4 + [step1] * 4, axis=0)
    out_ref[:, COORDS:] = three_pass(coeffs, chosen, ((0,), (1,)))

    for phase in list(pending):
        sent(phase)


def local(
    query_states, out_cotangent, query_of_token, gate_weight, up_weight, proj_in, proj_out,
    database, stored_ids,
):
    anywhere = pl.BlockSpec(memory_space=pl.ANY)
    vmem = pl.BlockSpec(memory_space=pltpu.VMEM)
    out = pl.pallas_call(
        kernel,
        out_shape=jax.ShapeDtypeStruct((Q, COORDS + ROWS), F32),
        in_specs=[anywhere] * 9,
        out_specs=vmem,
        scratch_shapes=[
            pltpu.VMEM((TOK, D), BF16),
            pltpu.VMEM((TOK, R), BF16),
            pltpu.VMEM((8, R), jnp.int32),
            pltpu.VMEM((FFL, D), BF16),
            pltpu.VMEM((FFL, D), BF16),
            pltpu.VMEM((FFL, R), BF16),
            pltpu.VMEM((R, R), BF16),
            pltpu.VMEM((ROWS, COORDS), BF16),
            pltpu.VMEM((EX, 8, R), jnp.int32),
            pltpu.VMEM((ZH, GROUP, Q, R), F32),
            pltpu.VMEM((GROUP, ZH, Q, R), F32),
            pltpu.VMEM((ZH, Q, R), F32),
            pltpu.VMEM((ZH, Q, R), F32),
            pltpu.VMEM((GROUP, Q, R), F32),
            pltpu.VMEM((CHUNKS, GROUP, 16, CHUNK), F32),
            pltpu.VMEM((CHUNKS, GROUP, 16, CHUNK), F32),
            pltpu.VMEM((CHUNKS, 16, CHUNK), F32),
            pltpu.VMEM((ZH, 16, CHUNK), F32),
            pltpu.VMEM((ZH, 16, R), F32),
            pltpu.VMEM((ZH, 16, R), F32),
            pltpu.VMEM((16 * EX, R), F32),
            pltpu.VMEM((2, GROUP, Q, R), F32),
            pltpu.VMEM((2, GROUP, Q, R), F32),
            pltpu.VMEM((2, ZH, Q, R), F32),
            pltpu.VMEM((2, GROUP, Q, R), F32),
            pltpu.VMEM((2, GROUP, 16, R), F32),
            pltpu.VMEM((2, ZH, 16, R), F32),
            pltpu.VMEM((EX, 16, R), F32),
            pltpu.VMEM((EX, 16, R), F32),
            pltpu.VMEM((EX, 8, R), F32),
            pltpu.VMEM((EX, 16, R), F32),
            pltpu.VMEM((EX, 16, R), F32),
            pltpu.VMEM((GROUP, 16, R), F32),
            pltpu.VMEM((2 * ROWS, R), F32),
            pltpu.VMEM((2 * ROWS, R), F32),
            pltpu.VMEM((2, ROWS, R), F32),
            pltpu.VMEM((ROWS, R), F32),
            pltpu.VMEM((Q, R), jnp.int32),
            pltpu.SMEM((Q, R), jnp.int32),
            pltpu.SemaphoreType.DMA((7,)),
            pltpu.SemaphoreType.DMA((CHUNKS,)),
            pltpu.SemaphoreType.DMA((2,)),
            pltpu.SemaphoreType.DMA((len(PHASES),)),
            pltpu.SemaphoreType.DMA((len(PHASES),)),
        ],
        compiler_params=pltpu.CompilerParams(
            collective_id=0, has_side_effects=True, vmem_limit_bytes=60 * 1024 * 1024
        ),
        name="logra",
    )(
        query_states,
        out_cotangent,
        query_of_token.reshape(8, R),
        gate_weight.T,
        up_weight.T,
        proj_in,
        proj_out,
        database,
        stored_ids.reshape(8, R),
    )
    return out[:, :COORDS].T, out[:, COORDS:].T * (1.0 / math.sqrt(K))


def solution(mesh):
    both = ("tp", "co")
    in_specs = (
        P("ex", None),
        P("ex", both),
        P("ex"),
        P(None, both),
        P(None, both),
        P(both, None),
        P(both, None),
        P("ex", both),
        P("ex"),
    )
    out_specs = (P(both, None), P("ex", None))
    return jax.shard_map(local, mesh=mesh, in_specs=in_specs, out_specs=out_specs, check_vma=False)
```

```python
import functools
import math

import jax
import jax.numpy as jnp
from jax import lax
from jax.experimental import pallas as pl
from jax.experimental.pallas import tpu as pltpu
from jax.sharding import PartitionSpec as P

D = 4096
FFL = 448
TOK = 1024
CHUNK = 256
CHUNKS = TOK // CHUNK
R = 128
Q = 32
QPG = 4
COORDS = 512
ROWS = 1024
EX = 8
GROUP = 8
ZH = 4
K = 16384
NSTORE = 8192
DAMPING = 1.0
HIGHEST = lax.Precision.HIGHEST
MESH = pl.DeviceIdType.MESH
F32 = jnp.float32
BF16 = jnp.bfloat16

PHASES = (
    ["ids", "r1", "r2", "r3"]
    + [f"l1{c}" for c in range(CHUNKS)]
    + ["l2", "gz", "b", "z1", "zg", "z3", "c1", "c2", "ma", "mx"]
    + [f"{name}{k}" for name in ("y1", "y2", "y3", "g1", "g2", "sa", "sb", "fa", "fb") for k in (0, 1)]
)
FAR_FIRST = {4: (2, 1), 5: (1, 1), 6: (3, 1), 7: (2, 0), 1: (1, 0), 2: (3, 0), 3: (0, 1)}
PHASE = {name: at for at, name in enumerate(PHASES)}


def fdot(a, b, dims=((1,), (0,))):
    return lax.dot_general(a, b, (dims, ((), ())), precision=HIGHEST, preferred_element_type=F32)


def bdot(a, b, dims=((1,), (0,))):
    return lax.dot_general(a, b, (dims, ((), ())), preferred_element_type=F32)


TN = ((0,), (0,))
NT = ((1,), (1,))


def eliminated(matrix, target):
    n = matrix.shape[0]
    both = jnp.concatenate([matrix, target], axis=1)
    lines = lax.broadcasted_iota(jnp.int32, both.shape, 0)
    for k in range(n):
        row = both[k : k + 1, :] / both[k : k + 1, k : k + 1]
        both = jnp.where(lines == k, row, both - both[:, k : k + 1] * row)
    return both[:, n:]


def three_pass(a, b, dims):
    a_high, b_high = a.astype(BF16), b.astype(BF16)
    a_low, b_low = (a - a_high.astype(F32)).astype(BF16), (b - b_high.astype(F32)).astype(BF16)
    return bdot(a_high, b_high, dims) + bdot(a_low, b_high, dims) + bdot(a_high, b_low, dims)


def repeated_gram(a, b):
    return fdot(a, jnp.concatenate([b] * 4, axis=0), NT)


def folded(gram):
    groups = lax.broadcasted_iota(jnp.int32, (8, R), 1) // Q
    out = jnp.where(groups == 0, gram[:8], 0.0)
    for k in range(1, 4):
        out = jnp.where(groups == k, gram[8 * k : 8 * k + 8], out)
    return out


def unfolded(tile):
    parts = [tile] + [pltpu.roll(tile, R - Q * k, 1) for k in range(1, 4)]
    return jnp.concatenate(parts, axis=0)[:, :Q]


def summed(slots):
    total = slots[0]
    for s in slots[1:]:
        total = total + s
    return total


def kernel(
    q_hbm, cot_hbm, qot_hbm, gw_hbm, uw_hbm, pin_hbm, pout_hbm, db_hbm, ids_hbm,
    out_ref,
    q_v, cot_v, qot_v, gw_v, uw_v, pin_v, pout_v, db_v,
    ids_all, rsend, r1, r2s, r2, right,
    lsend, l1, l2s, l2, gsend, gz,
    bbuf,
    ysend, y1, y2, yfull, gram1_v, gram2_v,
    zsend, z1, zg, zfull,
    cbuf, dbuf, far, s0, s1, picked, mask_v, where_v, where_s,
    small_sem, q_sem, w_sem, send_sem, recv_sem,
):
    tp = lax.axis_index("tp")
    e = lax.axis_index("ex")
    x = lax.axis_index("co")
    zh = tp // 2
    core = tp % 2
    g = core * 4 + x
    scale = 1.0 / math.sqrt(float(NSTORE))

    def in_group(p):
        return {"tp": zh * 2 + p // 4, "co": p % 4}

    def in_z(p):
        return {"tp": p * 2 + core}

    def in_ex(p):
        return {"ex": p}

    y, z_lo = e // 2, e % 2

    def peers(me, n):
        if n == ZH:
            return [(zh + d) % ZH for d in (2, 1, 3)]
        if me is e:
            return [
                ((y + dy) % 4) * 2 + (z_lo + dz) % 2
                for dy, dz in ((2, 1), (2, 0), (1, 1), (3, 1), (1, 0), (3, 0), (0, 1))
            ]
        return [
            ((core + dc) % 2) * 4 + (x + dx) % 4
            for dx, dc in ((2, 1), (2, 0), (1, 1), (3, 1), (1, 0), (3, 0), (0, 1))
        ]

    pending = {}

    def send(phase, src, dst, device):
        at = PHASE[phase]
        pltpu.make_async_remote_copy(
            src, dst, send_sem.at[at], recv_sem.at[at], device, MESH
        ).start()

    def push(phase, src_of, dst, me, n, device_of, slots):
        pending[phase] = slots
        for p in peers(me, n):
            send(phase, src_of(p), dst, device_of(p))

    def arrived(phase):
        slots = pending[phase]
        pltpu.make_async_copy(slots, slots, recv_sem.at[PHASE[phase]]).wait()

    def sent(phase):
        slots = pending.pop(phase)
        pltpu.make_async_copy(slots, slots, send_sem.at[PHASE[phase]]).wait()

    copies = [
        pltpu.make_async_copy(cot_hbm, cot_v, small_sem.at[0]),
        pltpu.make_async_copy(pout_hbm, pout_v, small_sem.at[1]),
        pltpu.make_async_copy(ids_hbm, ids_all.at[e], small_sem.at[2]),
        pltpu.make_async_copy(qot_hbm, qot_v, small_sem.at[3]),
        pltpu.make_async_copy(pin_hbm, pin_v, small_sem.at[4]),
        pltpu.make_async_copy(db_hbm, db_v, small_sem.at[5]),
        pltpu.make_async_copy(gw_hbm, gw_v, w_sem.at[0]),
        pltpu.make_async_copy(uw_hbm, uw_v, w_sem.at[1]),
    ]

    def q_copy(c):
        rows = pl.ds(c * CHUNK, CHUNK)
        return pltpu.make_async_copy(q_hbm.at[rows, :], q_v.at[rows, :], q_sem.at[c])

    barrier = pltpu.get_barrier_semaphore()
    for n, me, device_of in ((ZH, zh, in_z), (EX, e, in_ex), (GROUP, g, in_group)):
        for p in peers(me, n):
            pl.semaphore_signal(barrier, inc=1, device_id=device_of(p), device_id_type=MESH)

    for at in (0, 1, 2, 4):
        copies[at].start()
    q_copy(0).start()
    copies[6].start()
    copies[7].start()
    for c in range(1, CHUNKS):
        q_copy(c).start()
    copies[3].start()
    copies[5].start()

    copies[0].wait()
    copies[1].wait()
    rsend[...] = bdot(cot_v[...], pout_v[...]).reshape(ZH, GROUP, Q, R)
    copies[2].wait()

    pl.semaphore_wait(barrier, (GROUP - 1) + (ZH - 1) + (EX - 1))
    push(
        "r1", lambda p: rsend.at[:, p], r1.at[g], g, GROUP, in_group, r1.at[pl.ds(0, GROUP - 1)]
    )
    push(
        "ids", lambda p: ids_all.at[e], ids_all.at[e], e, EX, in_ex, ids_all.at[pl.ds(0, EX - 1)]
    )
    r1[g] = rsend[:, g]
    copies[4].wait()
    old = lax.broadcasted_iota(jnp.int32, (R, R), 0)
    new = lax.broadcasted_iota(jnp.int32, (R, R), 1)
    moved = old == 32 * ((new >> 2) & 3) + 4 * (new >> 4) + (new & 3)
    proj = bdot(pin_v[...], jnp.where(moved, 1.0, 0.0).astype(BF16))
    pin_v[...] = proj.astype(BF16)
    copies[6].wait()
    copies[7].wait()

    def matmul(c):
        q_copy(c).wait()
        a = q_v[c * CHUNK : (c + 1) * CHUNK, :]
        gate = bdot(gw_v[...], a, NT)
        up = bdot(uw_v[...], a, NT)
        hidden = ((gate / (1.0 + jnp.exp(-gate))) * up).astype(BF16)
        lsend[c] = bdot(pin_v[...], hidden, TN).reshape(GROUP, 16, CHUNK)
        push(
            f"l1{c}", lambda p: lsend.at[c, p], l1.at[c, g], g, GROUP, in_group,
            l1.at[c, pl.ds(0, GROUP - 1)],
        )
        l1[c, g] = lsend[c, g]

    def left_second(c):
        pending["l2"] = l2.at[pl.ds(0, ZH - 1)]
        arrived(f"l1{c}")
        l2s[c] = summed([l1[c, s] for s in range(GROUP)])

        @pl.when(zh != c)
        def _():
            send("l2", l2s.at[c], l2.at[zh], in_z(c))

        @pl.when(zh == c)
        def _():
            l2[zh] = l2s[c]

    matmul(0)
    matmul(1)
    matmul(2)
    arrived("r1")
    r2s[...] = summed([r1[s] for s in range(GROUP)])
    push("r2", lambda p: r2s.at[p], r2.at[zh], zh, ZH, in_z, r2.at[pl.ds(0, ZH - 1)])
    r2[zh] = r2s[zh]
    matmul(3)
    left_second(0)
    left_second(1)
    left_second(2)

    arrived("ids")
    kinds = lax.broadcasted_iota(jnp.int32, (Q, R), 0)
    lane = lax.broadcasted_iota(jnp.int32, (Q, R), 1)
    places = jnp.zeros((Q, 2 * Q), F32)
    places_t = jnp.zeros((Q, Q), F32)
    for d in range(EX):
        dy, dz = FAR_FIRST[d] if d else (0, 0)
        source = ((y + dy) % 4) * 2 + (z_lo + dz) % 2
        his, los = [], []
        for r in range(8):
            own = ids_all[source, pl.ds(r, 1), :] - e * ROWS
            hit_low = (own & 31) == kinds
            part = d + 8 * (r // 4) + 16 * (r % 4)
            his.append(jnp.where((own >> 5) == kinds, 1.0, 0.0).astype(BF16))
            los.append(
                jnp.concatenate(
                    [
                        jnp.where(hit_low, float(part), 0.0),
                        jnp.where(hit_low, lane.astype(F32), 0.0),
                    ],
                    axis=0,
                ).astype(BF16)
            )
        his = jnp.concatenate(his, axis=1)
        los = jnp.concatenate(los, axis=1)
        places = places + bdot(his, los, NT)
        places_t = places_t + bdot(los[:Q], his, NT)
    at = (places[:, :Q].astype(jnp.int32) & 15) * R + places[:, Q:].astype(jnp.int32)
    where_v[...] = jnp.concatenate([at] * 4, axis=1)
    to_scalar = pltpu.make_async_copy(where_v, where_s, small_sem.at[6])
    to_scalar.start()
    group_t = places_t.astype(jnp.int32) >> 4
    for hi in range(Q):
        mask_v[hi * Q : (hi + 1) * Q, :] = jnp.where(
            group_t[:, hi : hi + 1] == (lane >> 5), 1.0, 0.0
        )

    arrived("r2")
    right[g] = summed([r2[s] for s in range(ZH)])
    push(
        "r3", lambda p: right.at[g], right.at[g], g, GROUP, in_group,
        right.at[pl.ds(0, GROUP - 1)],
    )
    left_second(3)
    copies[3].wait()
    query = (
        jnp.concatenate([qot_v[pl.ds(2 * zh, 1), :], qot_v[pl.ds(2 * zh + 1, 1), :]], axis=1)
        - e * QPG
    )
    arrived("r3")
    arrived("l2")
    left = summed([l2[s] for s in range(ZH)])
    weighted = jnp.concatenate([jnp.where(query == k, left, 0.0) for k in range(QPG)], axis=0)
    grads = fdot(weighted, right[...].reshape(CHUNK, R))
    low = lax.broadcasted_iota(jnp.int32, (8, R), 0) < 4
    for p in range(ZH):
        for pair in range(2):
            one, two = [
                grads[q * 16 + 8 * (p // 2) : q * 16 + 8 * (p // 2) + 8]
                for q in (2 * pair, 2 * pair + 1)
            ]
            if p % 2:
                tile = jnp.where(low, pltpu.roll(one, 4, 0), two)
            else:
                tile = jnp.where(low, one, pltpu.roll(two, 4, 0))
            gsend[p, 8 * pair : 8 * pair + 8] = tile
    push("gz", lambda p: gsend.at[p], gz.at[zh], zh, ZH, in_z, gz.at[pl.ds(0, ZH - 1)])
    gz[zh] = gsend[zh]
    arrived("gz")
    own_rows = pl.ds(pl.multiple_of(e * 16, 16), 16)
    bbuf[own_rows, :] = summed([gz[s] for s in range(ZH)])
    push(
        "b", lambda p: bbuf.at[own_rows, :], bbuf.at[own_rows, :], e, EX, in_ex,
        bbuf.at[pl.ds(0, 16 * (EX - 1)), :],
    )
    copies[5].wait()
    arrived("b")
    base = jnp.concatenate([bbuf[pl.ds(i, Q, stride=4), :] for i in range(4)], axis=1)

    def first_stage(k, vectors):
        part = bdot(vectors.astype(BF16), db_v[...], NT)
        for p in range(GROUP):
            ysend[k, p] = part[:, p * R : (p + 1) * R]
        push(
            f"y1{k}", lambda p: ysend.at[k, p], y1.at[k, g], g, GROUP, in_group,
            y1.at[k, pl.ds(0, GROUP - 1)],
        )
        y1[k, g] = ysend[k, g]

    def first_grams(k, tiles):
        rows = pl.ds(0, 8 * len(tiles))
        gram1_v[k, g, rows] = jnp.concatenate(tiles, axis=0)
        push(
            f"g1{k}", lambda p: gram1_v.at[k, g, rows], gram1_v.at[k, g, rows], g, GROUP, in_group,
            gram1_v.at[k, pl.ds(0, GROUP - 1), rows],
        )

    def second_stage(k):
        arrived(f"y1{k}")
        y2[k, zh] = summed([y1[k, s] for s in range(GROUP)])
        push(
            f"y2{k}", lambda p: y2.at[k, zh], y2.at[k, zh], zh, ZH, in_z,
            y2.at[k, pl.ds(0, ZH - 1)],
        )

    def second_grams(k, count):
        rows = pl.ds(0, 8 * count)
        arrived(f"g1{k}")
        gram2_v[k, zh, rows] = summed([gram1_v[k, s, rows] for s in range(GROUP)])
        push(
            f"g2{k}", lambda p: gram2_v.at[k, zh, rows], gram2_v.at[k, zh, rows], zh, ZH, in_z,
            gram2_v.at[k, pl.ds(0, ZH - 1), rows],
        )

    def third_stage(k):
        arrived(f"y2{k}")
        yfull[k, g] = summed([y2[k, s] for s in range(ZH)])
        push(
            f"y3{k}", lambda p: yfull.at[k, g], yfull.at[k, g], g, GROUP, in_group,
            yfull.at[k, pl.ds(0, GROUP - 1)],
        )

    def grams_of(k, count):
        rows = pl.ds(0, 8 * count)
        arrived(f"g2{k}")
        total = summed([gram2_v[k, s, rows] for s in range(ZH)])
        return [unfolded(total[8 * at : 8 * at + 8]) for at in range(count)]

    def rows_of(k):
        arrived(f"y3{k}")
        return [yfull[k, s] for s in range(GROUP)]

    def own_packed(buf, blocks):
        for h in range(2):
            tall = jnp.concatenate(blocks[4 * h : 4 * h + 4], axis=0)
            buf[h * ROWS : h * ROWS + R, :] = tall.T

    def half(d, count=1):
        return pl.ds(pl.multiple_of(core * ROWS + d * R, R), count * R)

    def spread(k, buf, parts):
        for name, lo, hi in parts:
            pending[f"{name}{k}"] = buf.at[half(lo, hi - lo), :]
            for slot in range(lo, hi):
                dy, dz = FAR_FIRST[slot]
                p = ((y - dy) % 4) * 2 + (z_lo + dz) % 2
                send(f"{name}{k}", buf.at[half(0), :], buf.at[half(slot), :], in_ex(p))

    def forward(k, buf, name):
        lo, hi = (4, 8) if name == "a" else (1, 4)
        if f"s{name}{k}" in pending:
            arrived(f"s{name}{k}")
        part = buf.at[half(lo, hi - lo), :]
        pending[f"f{name}{k}"] = part
        send(f"f{name}{k}", part, part, {"tp": zh * 2 + (1 - core)})

    first_stage(0, base)
    first_grams(0, [folded(repeated_gram(base, base))])
    second_stage(0)
    second_grams(0, 1)
    third_stage(0)
    (norm0,) = grams_of(0, 1)
    eye = (
        lax.broadcasted_iota(jnp.int32, (Q, Q), 0) == lax.broadcasted_iota(jnp.int32, (Q, Q), 1)
    ).astype(F32)
    inverse0 = eliminated(norm0, eye)
    blocks0 = rows_of(0)
    rows0 = jnp.concatenate(blocks0, axis=1)

    back = bdot((rows0 * scale).astype(BF16), db_v[...])
    for p in range(EX):
        zsend[p] = back[16 * (p // 4) : 16 * (p // 4) + 16, (p % 4) * R : (p % 4 + 1) * R]
    push("z1", lambda p: zsend.at[p], z1.at[e], e, EX, in_ex, z1.at[pl.ds(0, EX - 1)])
    z1[e] = zsend[e]
    zg[e] = folded(repeated_gram(rows0, rows0))
    push("zg", lambda p: zg.at[e], zg.at[e], e, EX, in_ex, zg.at[pl.ds(0, EX - 1)])
    own_packed(s0, blocks0)
    arrived("z1")
    zfull[e] = summed([z1[s] for s in range(EX)])
    push("z3", lambda p: zfull.at[e], zfull.at[e], e, EX, in_ex, zfull.at[pl.ds(0, EX - 1)])
    arrived("zg")
    row_gram = unfolded(summed([zg[s] for s in range(EX)]))
    step0 = eliminated(row_gram * (scale * scale) + DAMPING * norm0, norm0)
    arrived("z3")
    spread(0, s0, (("sa", 4, 8), ("sb", 1, 4)))
    back = jnp.concatenate(
        [jnp.concatenate([zfull[4 * h + j] for j in range(4)], axis=1) for h in range(2)], axis=0
    )
    image = back * scale + DAMPING * base
    residual = base - fdot(step0, image, TN)

    first_stage(1, residual)
    first_grams(
        1, [folded(repeated_gram(residual, residual)), folded(repeated_gram(residual, base))]
    )
    second_stage(1)
    second_grams(1, 2)
    forward(0, s0, "a")
    forward(0, s0, "b")
    to_scalar.wait()
    third_stage(1)
    pending["ma"] = far.at[0]
    for slot in range(4, 8):
        dy, dz = FAR_FIRST[slot]
        p = ((y - dy) % 4) * 2 + (z_lo + dz) % 2
        send("ma", yfull.at[1, g], far.at[x, slot - 4], in_ex(p))
    block0, block1 = yfull[0, g], yfull[1, g]
    cbuf[e] = jnp.concatenate(
        [folded(repeated_gram(block1, block1)), folded(repeated_gram(block1, block0))], axis=0
    )
    push("c1", lambda p: cbuf.at[e], cbuf.at[e], e, EX, in_ex, cbuf.at[pl.ds(0, EX - 1)])
    norm1, cross = grams_of(1, 2)
    mixing = fdot(inverse0, norm1)

    def pick(source, side):
        def line(hi, carry):
            for lo in range(Q):
                at = where_s[hi, lo] & (2 * ROWS - 1)
                picked[side, pl.ds(hi * Q + lo, 1), :] = source[pl.ds(at, 1), :]
            return carry

        lax.fori_loop(0, Q, line, 0)

    blocks1 = rows_of(1)
    own_packed(s1, blocks1)
    arrived("c1")
    dbuf[g] = summed([cbuf[s] for s in range(EX)])
    push("c2", lambda p: dbuf.at[g], dbuf.at[g], g, GROUP, in_group, dbuf.at[pl.ds(0, GROUP - 1)])
    spread(1, s1, (("sb", 1, 4),))
    arrived("ma")
    pending["mx"] = far.at[pl.ds(0, 3)]
    for dx in (2, 1, 3):
        send("mx", far.at[x], far.at[x], {"co": (x + dx) % 4})
    gram = (
        norm1
        + fdot(cross, mixing)
        + fdot(mixing, cross, ((0,), (1,)))
        + fdot(mixing, fdot(norm0, mixing), TN)
    )
    arrived("fa0")
    arrived("fb0")
    pick(s0, 0)
    arrived("c2")
    total = summed([dbuf[s] for s in range(GROUP)])
    square, mixed = unfolded(total[:8]), unfolded(total[8:])
    rows_gram = (
        square
        + fdot(mixed, mixing)
        + fdot(mixing, mixed, ((0,), (1,)))
        + fdot(mixing, fdot(row_gram, mixing), TN)
    )
    forward(1, s1, "b")
    step1 = eliminated(rows_gram * (scale * scale) + DAMPING * gram, norm1)
    arrived("mx")
    for slot in range(4, 8):
        tall = jnp.concatenate([far[s, slot - 4] for s in range(4)], axis=0)
        s1[half(slot), :] = tall.T
    forward(1, s1, "a")
    first = step0 + fdot(mixing, step1)
    out_ref[:, :COORDS] = fdot(first, base, TN) + fdot(step1, residual, TN)
    arrived("fa1")
    arrived("fb1")
    pick(s1, 1)
    mask = mask_v[...]
    chosen = jnp.concatenate([picked[0] * mask, picked[1] * mask], axis=1)
    coeffs = jnp.concatenate([first] * 4 + [step1] * 4, axis=0)
    out_ref[:, COORDS:] = three_pass(coeffs, chosen, ((0,), (1,)))

    for phase in list(pending):
        sent(phase)


def local(
    query_states, out_cotangent, query_of_token, gate_weight, up_weight, proj_in, proj_out,
    database, stored_ids,
):
    anywhere = pl.BlockSpec(memory_space=pl.ANY)
    vmem = pl.BlockSpec(memory_space=pltpu.VMEM)
    out = pl.pallas_call(
        kernel,
        out_shape=pltpu.VMEM((Q, COORDS + ROWS), F32),
        in_specs=[anywhere] * 9,
        out_specs=vmem,
        scratch_shapes=[
            pltpu.VMEM((TOK, D), BF16),
            pltpu.VMEM((TOK, R), BF16),
            pltpu.VMEM((8, R), jnp.int32),
            pltpu.VMEM((FFL, D), BF16),
            pltpu.VMEM((FFL, D), BF16),
            pltpu.VMEM((FFL, R), BF16),
            pltpu.VMEM((R, R), BF16),
            pltpu.VMEM((ROWS, COORDS), BF16),
            pltpu.VMEM((EX, 8, R), jnp.int32),
            pltpu.VMEM((ZH, GROUP, Q, R), F32),
            pltpu.VMEM((GROUP, ZH, Q, R), F32),
            pltpu.VMEM((ZH, Q, R), F32),
            pltpu.VMEM((ZH, Q, R), F32),
            pltpu.VMEM((GROUP, Q, R), F32),
            pltpu.VMEM((CHUNKS, GROUP, 16, CHUNK), F32),
            pltpu.VMEM((CHUNKS, GROUP, 16, CHUNK), F32),
            pltpu.VMEM((CHUNKS, 16, CHUNK), F32),
            pltpu.VMEM((ZH, 16, CHUNK), F32),
            pltpu.VMEM((ZH, 16, R), F32),
            pltpu.VMEM((ZH, 16, R), F32),
            pltpu.VMEM((16 * EX, R), F32),
            pltpu.VMEM((2, GROUP, Q, R), F32),
            pltpu.VMEM((2, GROUP, Q, R), F32),
            pltpu.VMEM((2, ZH, Q, R), F32),
            pltpu.VMEM((2, GROUP, Q, R), F32),
            pltpu.VMEM((2, GROUP, 16, R), F32),
            pltpu.VMEM((2, ZH, 16, R), F32),
            pltpu.VMEM((EX, 16, R), F32),
            pltpu.VMEM((EX, 16, R), F32),
            pltpu.VMEM((EX, 8, R), F32),
            pltpu.VMEM((EX, 16, R), F32),
            pltpu.VMEM((EX, 16, R), F32),
            pltpu.VMEM((GROUP, 16, R), F32),
            pltpu.VMEM((4, 4, Q, R), F32),
            pltpu.VMEM((2 * ROWS, R), F32),
            pltpu.VMEM((2 * ROWS, R), F32),
            pltpu.VMEM((2, ROWS, R), F32),
            pltpu.VMEM((ROWS, R), F32),
            pltpu.VMEM((Q, R), jnp.int32),
            pltpu.SMEM((Q, R), jnp.int32),
            pltpu.SemaphoreType.DMA((7,)),
            pltpu.SemaphoreType.DMA((CHUNKS,)),
            pltpu.SemaphoreType.DMA((2,)),
            pltpu.SemaphoreType.DMA((len(PHASES),)),
            pltpu.SemaphoreType.DMA((len(PHASES),)),
        ],
        compiler_params=pltpu.CompilerParams(
            collective_id=0, has_side_effects=True, vmem_limit_bytes=60 * 1024 * 1024
        ),
        name="logra",
    )(
        query_states,
        out_cotangent,
        query_of_token.reshape(8, R),
        gate_weight.T,
        up_weight.T,
        proj_in,
        proj_out,
        database,
        stored_ids.reshape(8, R),
    )
    return out[:, :COORDS].T, out[:, COORDS:].T * (1.0 / math.sqrt(K))


def solution(mesh):
    both = ("tp", "co")
    in_specs = (
        P("ex", None),
        P("ex", both),
        P("ex"),
        P(None, both),
        P(None, both),
        P(both, None),
        P(both, None),
        P("ex", both),
        P("ex"),
    )
    out_specs = (P(both, None), P("ex", None))
    return jax.shard_map(local, mesh=mesh, in_specs=in_specs, out_specs=out_specs, check_vma=False)
```

```python
import functools
import math

import jax
import jax.numpy as jnp
from jax import lax
from jax.experimental import pallas as pl
from jax.experimental.pallas import tpu as pltpu
from jax.sharding import PartitionSpec as P

D = 4096
FFL = 448
TOK = 1024
CHUNK = 256
CHUNKS = TOK // CHUNK
R = 128
Q = 32
QPG = 4
COORDS = 512
ROWS = 1024
EX = 8
GROUP = 8
ZH = 4
K = 16384
NSTORE = 8192
DAMPING = 1.0
HIGHEST = lax.Precision.HIGHEST
MESH = pl.DeviceIdType.MESH
F32 = jnp.float32
BF16 = jnp.bfloat16

PHASES = (
    ["ids", "r1", "r2", "r3"]
    + [f"l1{c}" for c in range(CHUNKS)]
    + ["l2", "gz", "b", "z1", "zg", "z3", "c1", "c2", "ma", "mx"]
    + [f"{name}{k}" for name in ("y1", "y2", "y3", "g1", "g2", "sa", "sb", "fa", "fb") for k in (0, 1)]
)
FAR_FIRST = {4: (2, 1), 5: (1, 1), 6: (3, 1), 7: (2, 0), 1: (1, 0), 2: (3, 0), 3: (0, 1)}
PHASE = {name: at for at, name in enumerate(PHASES)}


def fdot(a, b, dims=((1,), (0,))):
    return lax.dot_general(a, b, (dims, ((), ())), precision=HIGHEST, preferred_element_type=F32)


def bdot(a, b, dims=((1,), (0,))):
    return lax.dot_general(a, b, (dims, ((), ())), preferred_element_type=F32)


TN = ((0,), (0,))
NT = ((1,), (1,))


def eliminated(matrix, target):
    n = matrix.shape[0]
    both = jnp.concatenate([matrix, target], axis=1)
    shape = both.shape
    lines = lax.broadcasted_iota(jnp.int32, shape, 0)
    for k in range(0, n, 2):
        one = jnp.broadcast_to(both[:, k : k + 1], shape)
        two = jnp.broadcast_to(both[:, k + 1 : k + 2], shape)
        pivot = 1.0 / one[k : k + 1]
        row = both[k : k + 1] * pivot
        ratio = two[k : k + 1] * pivot
        below = one[k + 1 : k + 2]
        last = (both[k + 1 : k + 2] - below * row) / (two[k + 1 : k + 2] - below * ratio)
        row = row - ratio * last
        rest = both - one * row - two * last
        both = jnp.where(lines == k, row, jnp.where(lines == k + 1, last, rest))
    return both[:, n:]


def three_pass(a, b, dims):
    a_high, b_high = a.astype(BF16), b.astype(BF16)
    a_low, b_low = (a - a_high.astype(F32)).astype(BF16), (b - b_high.astype(F32)).astype(BF16)
    return bdot(a_high, b_high, dims) + bdot(a_low, b_high, dims) + bdot(a_high, b_low, dims)


def repeated_gram(a, b):
    return fdot(a, jnp.concatenate([b] * 4, axis=0), NT)


def folded(gram):
    groups = lax.broadcasted_iota(jnp.int32, (8, R), 1) // Q
    out = jnp.where(groups == 0, gram[:8], 0.0)
    for k in range(1, 4):
        out = jnp.where(groups == k, gram[8 * k : 8 * k + 8], out)
    return out


def unfolded(tile):
    parts = [tile] + [pltpu.roll(tile, R - Q * k, 1) for k in range(1, 4)]
    return jnp.concatenate(parts, axis=0)[:, :Q]


def summed(slots):
    total = slots[0]
    for s in slots[1:]:
        total = total + s
    return total


def kernel(
    q_hbm, cot_hbm, qot_hbm, gw_hbm, uw_hbm, pin_hbm, pout_hbm, db_hbm, ids_hbm,
    out_ref,
    q_v, cot_v, qot_v, gw_v, uw_v, pin_v, pout_v, db_v,
    ids_all, rsend, r1, r2s, r2, right,
    lsend, l1, l2s, l2, gsend, gz,
    bbuf,
    ysend, y1, y2, yfull, gram1_v, gram2_v,
    zsend, z1, zg, zfull,
    cbuf, dbuf, far, s0, s1, picked, mask_v, where_v, where_s,
    small_sem, q_sem, w_sem, send_sem, recv_sem,
):
    tp = lax.axis_index("tp")
    e = lax.axis_index("ex")
    x = lax.axis_index("co")
    zh = tp // 2
    core = tp % 2
    g = core * 4 + x
    scale = 1.0 / math.sqrt(float(NSTORE))

    def in_group(p):
        return {"tp": zh * 2 + p // 4, "co": p % 4}

    def in_z(p):
        return {"tp": p * 2 + core}

    def in_ex(p):
        return {"ex": p}

    y, z_lo = e // 2, e % 2

    def peers(me, n):
        if n == ZH:
            return [(zh + d) % ZH for d in (2, 1, 3)]
        if me is e:
            return [
                ((y + dy) % 4) * 2 + (z_lo + dz) % 2
                for dy, dz in ((2, 1), (2, 0), (1, 1), (3, 1), (1, 0), (3, 0), (0, 1))
            ]
        return [
            ((core + dc) % 2) * 4 + (x + dx) % 4
            for dx, dc in ((2, 1), (2, 0), (1, 1), (3, 1), (1, 0), (3, 0), (0, 1))
        ]

    pending = {}

    def send(phase, src, dst, device):
        at = PHASE[phase]
        pltpu.make_async_remote_copy(
            src, dst, send_sem.at[at], recv_sem.at[at], device, MESH
        ).start()

    def push(phase, src_of, dst, me, n, device_of, slots):
        pending[phase] = slots
        for p in peers(me, n):
            send(phase, src_of(p), dst, device_of(p))

    def arrived(phase):
        slots = pending[phase]
        pltpu.make_async_copy(slots, slots, recv_sem.at[PHASE[phase]]).wait()

    def sent(phase):
        slots = pending.pop(phase)
        pltpu.make_async_copy(slots, slots, send_sem.at[PHASE[phase]]).wait()

    copies = [
        pltpu.make_async_copy(cot_hbm, cot_v, small_sem.at[0]),
        pltpu.make_async_copy(pout_hbm, pout_v, small_sem.at[1]),
        pltpu.make_async_copy(ids_hbm, ids_all.at[e], small_sem.at[2]),
        pltpu.make_async_copy(qot_hbm, qot_v, small_sem.at[3]),
        pltpu.make_async_copy(pin_hbm, pin_v, small_sem.at[4]),
        pltpu.make_async_copy(db_hbm, db_v, small_sem.at[5]),
        pltpu.make_async_copy(gw_hbm, gw_v, w_sem.at[0]),
        pltpu.make_async_copy(uw_hbm, uw_v, w_sem.at[1]),
    ]

    def q_copy(c):
        rows = pl.ds(c * CHUNK, CHUNK)
        return pltpu.make_async_copy(q_hbm.at[rows, :], q_v.at[rows, :], q_sem.at[c])

    barrier = pltpu.get_barrier_semaphore()
    for n, me, device_of in ((ZH, zh, in_z), (EX, e, in_ex), (GROUP, g, in_group)):
        for p in peers(me, n):
            pl.semaphore_signal(barrier, inc=1, device_id=device_of(p), device_id_type=MESH)

    for at in (0, 1, 2, 4):
        copies[at].start()
    q_copy(0).start()
    copies[6].start()
    copies[7].start()
    for c in range(1, CHUNKS):
        q_copy(c).start()
    copies[3].start()
    copies[5].start()

    copies[0].wait()
    copies[1].wait()
    rsend[...] = bdot(cot_v[...], pout_v[...]).reshape(ZH, GROUP, Q, R)
    copies[2].wait()

    pl.semaphore_wait(barrier, (GROUP - 1) + (ZH - 1) + (EX - 1))
    push(
        "r1", lambda p: rsend.at[:, p], r1.at[g], g, GROUP, in_group, r1.at[pl.ds(0, GROUP - 1)]
    )
    push(
        "ids", lambda p: ids_all.at[e], ids_all.at[e], e, EX, in_ex, ids_all.at[pl.ds(0, EX - 1)]
    )
    r1[g] = rsend[:, g]
    copies[4].wait()
    old = lax.broadcasted_iota(jnp.int32, (R, R), 0)
    new = lax.broadcasted_iota(jnp.int32, (R, R), 1)
    moved = old == 32 * ((new >> 2) & 3) + 4 * (new >> 4) + (new & 3)
    proj = bdot(pin_v[...], jnp.where(moved, 1.0, 0.0).astype(BF16))
    pin_v[...] = proj.astype(BF16)
    copies[6].wait()
    copies[7].wait()

    def matmul(c):
        q_copy(c).wait()
        a = q_v[c * CHUNK : (c + 1) * CHUNK, :]
        gate = bdot(gw_v[...], a, NT)
        up = bdot(uw_v[...], a, NT)
        hidden = ((gate / (1.0 + jnp.exp(-gate))) * up).astype(BF16)
        lsend[c] = bdot(pin_v[...], hidden, TN).reshape(GROUP, 16, CHUNK)
        push(
            f"l1{c}", lambda p: lsend.at[c, p], l1.at[c, g], g, GROUP, in_group,
            l1.at[c, pl.ds(0, GROUP - 1)],
        )
        l1[c, g] = lsend[c, g]

    def left_second(c):
        pending["l2"] = l2.at[pl.ds(0, ZH - 1)]
        arrived(f"l1{c}")
        l2s[c] = summed([l1[c, s] for s in range(GROUP)])

        @pl.when(zh != c)
        def _():
            send("l2", l2s.at[c], l2.at[zh], in_z(c))

        @pl.when(zh == c)
        def _():
            l2[zh] = l2s[c]

    matmul(0)
    matmul(1)
    matmul(2)
    arrived("r1")
    r2s[...] = summed([r1[s] for s in range(GROUP)])
    push("r2", lambda p: r2s.at[p], r2.at[zh], zh, ZH, in_z, r2.at[pl.ds(0, ZH - 1)])
    r2[zh] = r2s[zh]
    matmul(3)
    left_second(0)
    left_second(1)
    left_second(2)

    arrived("ids")
    kinds = lax.broadcasted_iota(jnp.int32, (Q, R), 0)
    lane = lax.broadcasted_iota(jnp.int32, (Q, R), 1)
    places = jnp.zeros((Q, 2 * Q), F32)
    places_t = jnp.zeros((Q, Q), F32)
    for d in range(EX):
        dy, dz = FAR_FIRST[d] if d else (0, 0)
        source = ((y + dy) % 4) * 2 + (z_lo + dz) % 2
        his, los = [], []
        for r in range(8):
            own = ids_all[source, pl.ds(r, 1), :] - e * ROWS
            hit_low = (own & 31) == kinds
            part = d + 8 * (r // 4) + 16 * (r % 4)
            his.append(jnp.where((own >> 5) == kinds, 1.0, 0.0).astype(BF16))
            los.append(
                jnp.concatenate(
                    [
                        jnp.where(hit_low, float(part), 0.0),
                        jnp.where(hit_low, lane.astype(F32), 0.0),
                    ],
                    axis=0,
                ).astype(BF16)
            )
        his = jnp.concatenate(his, axis=1)
        los = jnp.concatenate(los, axis=1)
        places = places + bdot(his, los, NT)
        places_t = places_t + bdot(los[:Q], his, NT)
    at = (places[:, :Q].astype(jnp.int32) & 15) * R + places[:, Q:].astype(jnp.int32)
    where_v[...] = jnp.concatenate([at] * 4, axis=1)
    to_scalar = pltpu.make_async_copy(where_v, where_s, small_sem.at[6])
    to_scalar.start()
    group_t = places_t.astype(jnp.int32) >> 4
    for hi in range(Q):
        mask_v[hi * Q : (hi + 1) * Q, :] = jnp.where(
            group_t[:, hi : hi + 1] == (lane >> 5), 1.0, 0.0
        )

    arrived("r2")
    right[g] = summed([r2[s] for s in range(ZH)])
    push(
        "r3", lambda p: right.at[g], right.at[g], g, GROUP, in_group,
        right.at[pl.ds(0, GROUP - 1)],
    )
    left_second(3)
    copies[3].wait()
    query = (
        jnp.concatenate([qot_v[pl.ds(2 * zh, 1), :], qot_v[pl.ds(2 * zh + 1, 1), :]], axis=1)
        - e * QPG
    )
    arrived("r3")
    arrived("l2")
    left = summed([l2[s] for s in range(ZH)])
    weighted = jnp.concatenate([jnp.where(query == k, left, 0.0) for k in range(QPG)], axis=0)
    grads = fdot(weighted, right[...].reshape(CHUNK, R))
    low = lax.broadcasted_iota(jnp.int32, (8, R), 0) < 4
    for p in range(ZH):
        for pair in range(2):
            one, two = [
                grads[q * 16 + 8 * (p // 2) : q * 16 + 8 * (p // 2) + 8]
                for q in (2 * pair, 2 * pair + 1)
            ]
            if p % 2:
                tile = jnp.where(low, pltpu.roll(one, 4, 0), two)
            else:
                tile = jnp.where(low, one, pltpu.roll(two, 4, 0))
            gsend[p, 8 * pair : 8 * pair + 8] = tile
    push("gz", lambda p: gsend.at[p], gz.at[zh], zh, ZH, in_z, gz.at[pl.ds(0, ZH - 1)])
    gz[zh] = gsend[zh]
    arrived("gz")
    own_rows = pl.ds(pl.multiple_of(e * 16, 16), 16)
    bbuf[own_rows, :] = summed([gz[s] for s in range(ZH)])
    push(
        "b", lambda p: bbuf.at[own_rows, :], bbuf.at[own_rows, :], e, EX, in_ex,
        bbuf.at[pl.ds(0, 16 * (EX - 1)), :],
    )
    copies[5].wait()
    arrived("b")
    base = jnp.concatenate([bbuf[pl.ds(i, Q, stride=4), :] for i in range(4)], axis=1)

    def first_stage(k, vectors):
        part = bdot(vectors.astype(BF16), db_v[...], NT)
        for p in range(GROUP):
            ysend[k, p] = part[:, p * R : (p + 1) * R]
        push(
            f"y1{k}", lambda p: ysend.at[k, p], y1.at[k, g], g, GROUP, in_group,
            y1.at[k, pl.ds(0, GROUP - 1)],
        )
        y1[k, g] = ysend[k, g]

    def first_grams(k, tiles):
        rows = pl.ds(0, 8 * len(tiles))
        gram1_v[k, g, rows] = jnp.concatenate(tiles, axis=0)
        push(
            f"g1{k}", lambda p: gram1_v.at[k, g, rows], gram1_v.at[k, g, rows], g, GROUP, in_group,
            gram1_v.at[k, pl.ds(0, GROUP - 1), rows],
        )

    def second_stage(k):
        arrived(f"y1{k}")
        y2[k, zh] = summed([y1[k, s] for s in range(GROUP)])
        push(
            f"y2{k}", lambda p: y2.at[k, zh], y2.at[k, zh], zh, ZH, in_z,
            y2.at[k, pl.ds(0, ZH - 1)],
        )

    def second_grams(k, count):
        rows = pl.ds(0, 8 * count)
        arrived(f"g1{k}")
        gram2_v[k, zh, rows] = summed([gram1_v[k, s, rows] for s in range(GROUP)])
        push(
            f"g2{k}", lambda p: gram2_v.at[k, zh, rows], gram2_v.at[k, zh, rows], zh, ZH, in_z,
            gram2_v.at[k, pl.ds(0, ZH - 1), rows],
        )

    def third_stage(k):
        arrived(f"y2{k}")
        yfull[k, g] = summed([y2[k, s] for s in range(ZH)])
        push(
            f"y3{k}", lambda p: yfull.at[k, g], yfull.at[k, g], g, GROUP, in_group,
            yfull.at[k, pl.ds(0, GROUP - 1)],
        )

    def grams_of(k, count):
        rows = pl.ds(0, 8 * count)
        arrived(f"g2{k}")
        total = summed([gram2_v[k, s, rows] for s in range(ZH)])
        return [unfolded(total[8 * at : 8 * at + 8]) for at in range(count)]

    def rows_of(k):
        arrived(f"y3{k}")
        return [yfull[k, s] for s in range(GROUP)]

    def own_packed(buf, blocks):
        for h in range(2):
            tall = jnp.concatenate(blocks[4 * h : 4 * h + 4], axis=0)
            buf[h * ROWS : h * ROWS + R, :] = tall.T

    def half(d, count=1):
        return pl.ds(pl.multiple_of(core * ROWS + d * R, R), count * R)

    def spread(k, buf, parts):
        for name, lo, hi in parts:
            pending[f"{name}{k}"] = buf.at[half(lo, hi - lo), :]
            for slot in range(lo, hi):
                dy, dz = FAR_FIRST[slot]
                p = ((y - dy) % 4) * 2 + (z_lo + dz) % 2
                send(f"{name}{k}", buf.at[half(0), :], buf.at[half(slot), :], in_ex(p))

    def forward(k, buf, name):
        lo, hi = (4, 8) if name == "a" else (1, 4)
        if f"s{name}{k}" in pending:
            arrived(f"s{name}{k}")
        part = buf.at[half(lo, hi - lo), :]
        pending[f"f{name}{k}"] = part
        send(f"f{name}{k}", part, part, {"tp": zh * 2 + (1 - core)})

    first_stage(0, base)
    first_grams(0, [folded(repeated_gram(base, base))])
    second_stage(0)
    second_grams(0, 1)
    third_stage(0)
    (norm0,) = grams_of(0, 1)
    eye = (
        lax.broadcasted_iota(jnp.int32, (Q, Q), 0) == lax.broadcasted_iota(jnp.int32, (Q, Q), 1)
    ).astype(F32)
    inverse0 = eliminated(norm0, eye)
    blocks0 = rows_of(0)
    rows0 = jnp.concatenate(blocks0, axis=1)

    back = bdot((rows0 * scale).astype(BF16), db_v[...])
    for p in range(EX):
        zsend[p] = back[16 * (p // 4) : 16 * (p // 4) + 16, (p % 4) * R : (p % 4 + 1) * R]
    push("z1", lambda p: zsend.at[p], z1.at[e], e, EX, in_ex, z1.at[pl.ds(0, EX - 1)])
    z1[e] = zsend[e]
    zg[e] = folded(repeated_gram(rows0, rows0))
    push("zg", lambda p: zg.at[e], zg.at[e], e, EX, in_ex, zg.at[pl.ds(0, EX - 1)])
    own_packed(s0, blocks0)
    arrived("z1")
    zfull[e] = summed([z1[s] for s in range(EX)])
    push("z3", lambda p: zfull.at[e], zfull.at[e], e, EX, in_ex, zfull.at[pl.ds(0, EX - 1)])
    arrived("zg")
    row_gram = unfolded(summed([zg[s] for s in range(EX)]))
    step0 = eliminated(row_gram * (scale * scale) + DAMPING * norm0, norm0)
    arrived("z3")
    spread(0, s0, (("sa", 4, 8), ("sb", 1, 4)))
    back = jnp.concatenate(
        [jnp.concatenate([zfull[4 * h + j] for j in range(4)], axis=1) for h in range(2)], axis=0
    )
    image = back * scale + DAMPING * base
    residual = base - fdot(step0, image, TN)

    first_stage(1, residual)
    first_grams(
        1, [folded(repeated_gram(residual, residual)), folded(repeated_gram(residual, base))]
    )
    second_stage(1)
    second_grams(1, 2)
    forward(0, s0, "a")
    forward(0, s0, "b")
    to_scalar.wait()
    third_stage(1)
    pending["ma"] = far.at[0]
    for slot in range(4, 8):
        dy, dz = FAR_FIRST[slot]
        p = ((y - dy) % 4) * 2 + (z_lo + dz) % 2
        send("ma", yfull.at[1, g], far.at[x, slot - 4], in_ex(p))
    block0, block1 = yfull[0, g], yfull[1, g]
    cbuf[e] = jnp.concatenate(
        [folded(repeated_gram(block1, block1)), folded(repeated_gram(block1, block0))], axis=0
    )
    push("c1", lambda p: cbuf.at[e], cbuf.at[e], e, EX, in_ex, cbuf.at[pl.ds(0, EX - 1)])
    norm1, cross = grams_of(1, 2)
    mixing = fdot(inverse0, norm1)

    def pick(source, side):
        def line(hi, carry):
            for lo in range(Q):
                at = where_s[hi, lo] & (2 * ROWS - 1)
                picked[side, pl.ds(hi * Q + lo, 1), :] = source[pl.ds(at, 1), :]
            return carry

        lax.fori_loop(0, Q, line, 0)

    arrived("ma")
    pending["mx"] = far.at[pl.ds(0, 3)]
    for dx in (2, 1, 3):
        send("mx", far.at[x], far.at[x], {"co": (x + dx) % 4})
    blocks1 = rows_of(1)
    own_packed(s1, blocks1)
    spread(1, s1, (("sb", 1, 4),))
    arrived("c1")
    dbuf[g] = summed([cbuf[s] for s in range(EX)])
    push("c2", lambda p: dbuf.at[g], dbuf.at[g], g, GROUP, in_group, dbuf.at[pl.ds(0, GROUP - 1)])
    gram = (
        norm1
        + fdot(cross, mixing)
        + fdot(mixing, cross, ((0,), (1,)))
        + fdot(mixing, fdot(norm0, mixing), TN)
    )
    spare = fdot(mixing, fdot(row_gram, mixing), TN)
    arrived("fa0")
    arrived("fb0")
    pick(s0, 0)
    forward(1, s1, "b")
    arrived("c2")
    total = summed([dbuf[s] for s in range(GROUP)])
    square, mixed = unfolded(total[:8]), unfolded(total[8:])
    rows_gram = square + fdot(mixed, mixing) + fdot(mixing, mixed, ((0,), (1,))) + spare
    step1 = eliminated(rows_gram * (scale * scale) + DAMPING * gram, norm1)
    arrived("mx")
    for slot in range(4, 8):
        tall = jnp.concatenate([far[s, slot - 4] for s in range(4)], axis=0)
        s1[half(slot), :] = tall.T
    forward(1, s1, "a")
    first = step0 + fdot(mixing, step1)
    out_ref[:, :COORDS] = fdot(first, base, TN) + fdot(step1, residual, TN)
    mask = mask_v[...]
    across = ((0,), (1,))
    scores = three_pass(jnp.concatenate([first] * 4, axis=0), picked[0] * mask, across)
    arrived("fa1")
    arrived("fb1")
    pick(s1, 1)
    out_ref[:, COORDS:] = scores + three_pass(
        jnp.concatenate([step1] * 4, axis=0), picked[1] * mask, across
    )

    for phase in list(pending):
        sent(phase)


def local(
    query_states, out_cotangent, query_of_token, gate_weight, up_weight, proj_in, proj_out,
    database, stored_ids,
):
    anywhere = pl.BlockSpec(memory_space=pl.ANY)
    vmem = pl.BlockSpec(memory_space=pltpu.VMEM)
    out = pl.pallas_call(
        kernel,
        out_shape=pltpu.VMEM((Q, COORDS + ROWS), F32),
        in_specs=[anywhere] * 9,
        out_specs=vmem,
        scratch_shapes=[
            pltpu.VMEM((TOK, D), BF16),
            pltpu.VMEM((TOK, R), BF16),
            pltpu.VMEM((8, R), jnp.int32),
            pltpu.VMEM((FFL, D), BF16),
            pltpu.VMEM((FFL, D), BF16),
            pltpu.VMEM((FFL, R), BF16),
            pltpu.VMEM((R, R), BF16),
            pltpu.VMEM((ROWS, COORDS), BF16),
            pltpu.VMEM((EX, 8, R), jnp.int32),
            pltpu.VMEM((ZH, GROUP, Q, R), F32),
            pltpu.VMEM((GROUP, ZH, Q, R), F32),
            pltpu.VMEM((ZH, Q, R), F32),
            pltpu.VMEM((ZH, Q, R), F32),
            pltpu.VMEM((GROUP, Q, R), F32),
            pltpu.VMEM((CHUNKS, GROUP, 16, CHUNK), F32),
            pltpu.VMEM((CHUNKS, GROUP, 16, CHUNK), F32),
            pltpu.VMEM((CHUNKS, 16, CHUNK), F32),
            pltpu.VMEM((ZH, 16, CHUNK), F32),
            pltpu.VMEM((ZH, 16, R), F32),
            pltpu.VMEM((ZH, 16, R), F32),
            pltpu.VMEM((16 * EX, R), F32),
            pltpu.VMEM((2, GROUP, Q, R), F32),
            pltpu.VMEM((2, GROUP, Q, R), F32),
            pltpu.VMEM((2, ZH, Q, R), F32),
            pltpu.VMEM((2, GROUP, Q, R), F32),
            pltpu.VMEM((2, GROUP, 16, R), F32),
            pltpu.VMEM((2, ZH, 16, R), F32),
            pltpu.VMEM((EX, 16, R), F32),
            pltpu.VMEM((EX, 16, R), F32),
            pltpu.VMEM((EX, 8, R), F32),
            pltpu.VMEM((EX, 16, R), F32),
            pltpu.VMEM((EX, 16, R), F32),
            pltpu.VMEM((GROUP, 16, R), F32),
            pltpu.VMEM((4, 4, Q, R), F32),
            pltpu.VMEM((2 * ROWS, R), F32),
            pltpu.VMEM((2 * ROWS, R), F32),
            pltpu.VMEM((2, ROWS, R), F32),
            pltpu.VMEM((ROWS, R), F32),
            pltpu.VMEM((Q, R), jnp.int32),
            pltpu.SMEM((Q, R), jnp.int32),
            pltpu.SemaphoreType.DMA((7,)),
            pltpu.SemaphoreType.DMA((CHUNKS,)),
            pltpu.SemaphoreType.DMA((2,)),
            pltpu.SemaphoreType.DMA((len(PHASES),)),
            pltpu.SemaphoreType.DMA((len(PHASES),)),
        ],
        compiler_params=pltpu.CompilerParams(
            collective_id=0, has_side_effects=True, vmem_limit_bytes=60 * 1024 * 1024
        ),
        name="logra",
    )(
        query_states,
        out_cotangent,
        query_of_token.reshape(8, R),
        gate_weight.T,
        up_weight.T,
        proj_in,
        proj_out,
        database,
        stored_ids.reshape(8, R),
    )
    return out[:, :COORDS].T, out[:, COORDS:].T * (1.0 / math.sqrt(K))


def solution(mesh):
    both = ("tp", "co")
    in_specs = (
        P("ex", None),
        P("ex", both),
        P("ex"),
        P(None, both),
        P(None, both),
        P(both, None),
        P(both, None),
        P("ex", both),
        P("ex"),
    )
    out_specs = (P(both, None), P("ex", None))
    return jax.shard_map(local, mesh=mesh, in_specs=in_specs, out_specs=out_specs, check_vma=False)
```

```python
import functools
import math

import jax
import jax.numpy as jnp
from jax import lax
from jax.experimental import pallas as pl
from jax.experimental.pallas import tpu as pltpu
from jax.sharding import PartitionSpec as P

D = 4096
FFL = 448
TOK = 1024
CHUNK = 256
CHUNKS = TOK // CHUNK
R = 128
Q = 32
QPG = 4
COORDS = 512
ROWS = 1024
EX = 8
GROUP = 8
ZH = 4
K = 16384
NSTORE = 8192
DAMPING = 1.0
HIGHEST = lax.Precision.HIGHEST
MESH = pl.DeviceIdType.MESH
F32 = jnp.float32
BF16 = jnp.bfloat16

PHASES = (
    ["ids", "r1", "r2", "r3"]
    + [f"l1{c}" for c in range(CHUNKS)]
    + ["l2", "gz", "b", "z1", "zg", "z3", "c1", "c2"]
    + [f"{name}{k}" for name in ("y1", "y2", "y3", "g1", "g2", "ma", "mx", "sb", "fa", "fb") for k in (0, 1)]
)
FAR_FIRST = {4: (2, 1), 5: (1, 1), 6: (3, 1), 7: (2, 0), 1: (1, 0), 2: (3, 0), 3: (0, 1)}
PHASE = {name: at for at, name in enumerate(PHASES)}


def fdot(a, b, dims=((1,), (0,))):
    return lax.dot_general(a, b, (dims, ((), ())), precision=HIGHEST, preferred_element_type=F32)


def bdot(a, b, dims=((1,), (0,))):
    return lax.dot_general(a, b, (dims, ((), ())), preferred_element_type=F32)


TN = ((0,), (0,))
NT = ((1,), (1,))


def eliminated(matrix, target):
    n = matrix.shape[0]
    both = jnp.concatenate([matrix, target], axis=1)
    shape = both.shape
    lines = lax.broadcasted_iota(jnp.int32, shape, 0)
    for k in range(0, n, 2):
        one = jnp.broadcast_to(both[:, k : k + 1], shape)
        two = jnp.broadcast_to(both[:, k + 1 : k + 2], shape)
        pivot = 1.0 / one[k : k + 1]
        row = both[k : k + 1] * pivot
        ratio = two[k : k + 1] * pivot
        below = one[k + 1 : k + 2]
        last = (both[k + 1 : k + 2] - below * row) / (two[k + 1 : k + 2] - below * ratio)
        row = row - ratio * last
        rest = both - one * row - two * last
        both = jnp.where(lines == k, row, jnp.where(lines == k + 1, last, rest))
    return both[:, n:]


def three_pass(a, b, dims):
    a_high, b_high = a.astype(BF16), b.astype(BF16)
    a_low, b_low = (a - a_high.astype(F32)).astype(BF16), (b - b_high.astype(F32)).astype(BF16)
    return bdot(a_high, b_high, dims) + bdot(a_low, b_high, dims) + bdot(a_high, b_low, dims)


def repeated_gram(a, b):
    return fdot(a, jnp.concatenate([b] * 4, axis=0), NT)


def folded(gram):
    groups = lax.broadcasted_iota(jnp.int32, (8, R), 1) // Q
    out = jnp.where(groups == 0, gram[:8], 0.0)
    for k in range(1, 4):
        out = jnp.where(groups == k, gram[8 * k : 8 * k + 8], out)
    return out


def unfolded(tile):
    parts = [tile] + [pltpu.roll(tile, R - Q * k, 1) for k in range(1, 4)]
    return jnp.concatenate(parts, axis=0)[:, :Q]


def summed(slots):
    total = slots[0]
    for s in slots[1:]:
        total = total + s
    return total


def kernel(
    q_hbm, cot_hbm, qot_hbm, gw_hbm, uw_hbm, pin_hbm, pout_hbm, db_hbm, ids_hbm,
    out_ref,
    q_v, cot_v, qot_v, gw_v, uw_v, pin_v, pout_v, db_v,
    ids_all, rsend, r1, r2s, r2, right,
    lsend, l1, l2s, l2, gsend, gz,
    bbuf,
    ysend, y1, y2, yfull, gram1_v, gram2_v,
    zsend, z1, zg, zfull,
    cbuf, dbuf, far, s0, s1, picked, mask_v, where_v, where_s,
    small_sem, q_sem, w_sem, send_sem, recv_sem,
):
    tp = lax.axis_index("tp")
    e = lax.axis_index("ex")
    x = lax.axis_index("co")
    zh = tp // 2
    core = tp % 2
    g = core * 4 + x
    scale = 1.0 / math.sqrt(float(NSTORE))

    def in_group(p):
        return {"tp": zh * 2 + p // 4, "co": p % 4}

    def in_z(p):
        return {"tp": p * 2 + core}

    def in_ex(p):
        return {"ex": p}

    y, z_lo = e // 2, e % 2

    def peers(me, n):
        if n == ZH:
            return [(zh + d) % ZH for d in (2, 1, 3)]
        if me is e:
            return [
                ((y + dy) % 4) * 2 + (z_lo + dz) % 2
                for dy, dz in ((2, 1), (2, 0), (1, 1), (3, 1), (1, 0), (3, 0), (0, 1))
            ]
        return [
            ((core + dc) % 2) * 4 + (x + dx) % 4
            for dx, dc in ((2, 1), (2, 0), (1, 1), (3, 1), (1, 0), (3, 0), (0, 1))
        ]

    pending = {}

    def send(phase, src, dst, device):
        at = PHASE[phase]
        pltpu.make_async_remote_copy(
            src, dst, send_sem.at[at], recv_sem.at[at], device, MESH
        ).start()

    def push(phase, src_of, dst, me, n, device_of, slots):
        pending[phase] = slots
        for p in peers(me, n):
            send(phase, src_of(p), dst, device_of(p))

    def arrived(phase):
        slots = pending[phase]
        pltpu.make_async_copy(slots, slots, recv_sem.at[PHASE[phase]]).wait()

    def sent(phase):
        slots = pending.pop(phase)
        pltpu.make_async_copy(slots, slots, send_sem.at[PHASE[phase]]).wait()

    copies = [
        pltpu.make_async_copy(cot_hbm, cot_v, small_sem.at[0]),
        pltpu.make_async_copy(pout_hbm, pout_v, small_sem.at[1]),
        pltpu.make_async_copy(ids_hbm, ids_all.at[e], small_sem.at[2]),
        pltpu.make_async_copy(qot_hbm, qot_v, small_sem.at[3]),
        pltpu.make_async_copy(pin_hbm, pin_v, small_sem.at[4]),
        pltpu.make_async_copy(db_hbm, db_v, small_sem.at[5]),
        pltpu.make_async_copy(gw_hbm, gw_v, w_sem.at[0]),
        pltpu.make_async_copy(uw_hbm, uw_v, w_sem.at[1]),
    ]

    def q_copy(c):
        rows = pl.ds(c * CHUNK, CHUNK)
        return pltpu.make_async_copy(q_hbm.at[rows, :], q_v.at[rows, :], q_sem.at[c])

    barrier = pltpu.get_barrier_semaphore()
    for n, me, device_of in ((ZH, zh, in_z), (EX, e, in_ex), (GROUP, g, in_group)):
        for p in peers(me, n):
            pl.semaphore_signal(barrier, inc=1, device_id=device_of(p), device_id_type=MESH)

    for at in (0, 1, 2, 4):
        copies[at].start()
    q_copy(0).start()
    copies[6].start()
    copies[7].start()
    for c in range(1, CHUNKS):
        q_copy(c).start()
    copies[3].start()
    copies[5].start()

    copies[0].wait()
    copies[1].wait()
    rsend[...] = bdot(cot_v[...], pout_v[...]).reshape(ZH, GROUP, Q, R)
    copies[2].wait()

    pl.semaphore_wait(barrier, (GROUP - 1) + (ZH - 1) + (EX - 1))
    push(
        "r1", lambda p: rsend.at[:, p], r1.at[g], g, GROUP, in_group, r1.at[pl.ds(0, GROUP - 1)]
    )
    push(
        "ids", lambda p: ids_all.at[e], ids_all.at[e], e, EX, in_ex, ids_all.at[pl.ds(0, EX - 1)]
    )
    r1[g] = rsend[:, g]
    copies[4].wait()
    old = lax.broadcasted_iota(jnp.int32, (R, R), 0)
    new = lax.broadcasted_iota(jnp.int32, (R, R), 1)
    moved = old == 32 * ((new >> 2) & 3) + 4 * (new >> 4) + (new & 3)
    proj = bdot(pin_v[...], jnp.where(moved, 1.0, 0.0).astype(BF16))
    pin_v[...] = proj.astype(BF16)
    copies[6].wait()
    copies[7].wait()

    def matmul(c):
        q_copy(c).wait()
        a = q_v[c * CHUNK : (c + 1) * CHUNK, :]
        gate = bdot(gw_v[...], a, NT)
        up = bdot(uw_v[...], a, NT)
        hidden = ((gate / (1.0 + jnp.exp(-gate))) * up).astype(BF16)
        lsend[c] = bdot(pin_v[...], hidden, TN).reshape(GROUP, 16, CHUNK)
        push(
            f"l1{c}", lambda p: lsend.at[c, p], l1.at[c, g], g, GROUP, in_group,
            l1.at[c, pl.ds(0, GROUP - 1)],
        )
        l1[c, g] = lsend[c, g]

    def left_second(c):
        pending["l2"] = l2.at[pl.ds(0, ZH - 1)]
        arrived(f"l1{c}")
        l2s[c] = summed([l1[c, s] for s in range(GROUP)])

        @pl.when(zh != c)
        def _():
            send("l2", l2s.at[c], l2.at[zh], in_z(c))

        @pl.when(zh == c)
        def _():
            l2[zh] = l2s[c]

    matmul(0)
    matmul(1)
    matmul(2)
    arrived("r1")
    r2s[...] = summed([r1[s] for s in range(GROUP)])
    push("r2", lambda p: r2s.at[p], r2.at[zh], zh, ZH, in_z, r2.at[pl.ds(0, ZH - 1)])
    r2[zh] = r2s[zh]
    matmul(3)
    left_second(0)
    left_second(1)
    left_second(2)

    arrived("ids")
    kinds = lax.broadcasted_iota(jnp.int32, (Q, R), 0)
    lane = lax.broadcasted_iota(jnp.int32, (Q, R), 1)
    places = jnp.zeros((Q, 2 * Q), F32)
    places_t = jnp.zeros((Q, Q), F32)
    for d in range(EX):
        dy, dz = FAR_FIRST[d] if d else (0, 0)
        source = ((y + dy) % 4) * 2 + (z_lo + dz) % 2
        his, los = [], []
        for r in range(8):
            own = ids_all[source, pl.ds(r, 1), :] - e * ROWS
            hit_low = (own & 31) == kinds
            part = d + 8 * (r // 4) + 16 * (r % 4)
            his.append(jnp.where((own >> 5) == kinds, 1.0, 0.0).astype(BF16))
            los.append(
                jnp.concatenate(
                    [
                        jnp.where(hit_low, float(part), 0.0),
                        jnp.where(hit_low, lane.astype(F32), 0.0),
                    ],
                    axis=0,
                ).astype(BF16)
            )
        his = jnp.concatenate(his, axis=1)
        los = jnp.concatenate(los, axis=1)
        places = places + bdot(his, los, NT)
        places_t = places_t + bdot(los[:Q], his, NT)
    at = (places[:, :Q].astype(jnp.int32) & 15) * R + places[:, Q:].astype(jnp.int32)
    where_v[...] = jnp.concatenate([at] * 4, axis=1)
    to_scalar = pltpu.make_async_copy(where_v, where_s, small_sem.at[6])
    to_scalar.start()
    group_t = places_t.astype(jnp.int32) >> 4
    for hi in range(Q):
        mask_v[hi * Q : (hi + 1) * Q, :] = jnp.where(
            group_t[:, hi : hi + 1] == (lane >> 5), 1.0, 0.0
        )

    arrived("r2")
    right[g] = summed([r2[s] for s in range(ZH)])
    push(
        "r3", lambda p: right.at[g], right.at[g], g, GROUP, in_group,
        right.at[pl.ds(0, GROUP - 1)],
    )
    left_second(3)
    copies[3].wait()
    query = (
        jnp.concatenate([qot_v[pl.ds(2 * zh, 1), :], qot_v[pl.ds(2 * zh + 1, 1), :]], axis=1)
        - e * QPG
    )
    arrived("r3")
    arrived("l2")
    left = summed([l2[s] for s in range(ZH)])
    weighted = jnp.concatenate([jnp.where(query == k, left, 0.0) for k in range(QPG)], axis=0)
    grads = fdot(weighted, right[...].reshape(CHUNK, R))
    low = lax.broadcasted_iota(jnp.int32, (8, R), 0) < 4
    for p in range(ZH):
        for pair in range(2):
            one, two = [
                grads[q * 16 + 8 * (p // 2) : q * 16 + 8 * (p // 2) + 8]
                for q in (2 * pair, 2 * pair + 1)
            ]
            if p % 2:
                tile = jnp.where(low, pltpu.roll(one, 4, 0), two)
            else:
                tile = jnp.where(low, one, pltpu.roll(two, 4, 0))
            gsend[p, 8 * pair : 8 * pair + 8] = tile
    push("gz", lambda p: gsend.at[p], gz.at[zh], zh, ZH, in_z, gz.at[pl.ds(0, ZH - 1)])
    gz[zh] = gsend[zh]
    arrived("gz")
    own_rows = pl.ds(pl.multiple_of(e * 16, 16), 16)
    bbuf[own_rows, :] = summed([gz[s] for s in range(ZH)])
    push(
        "b", lambda p: bbuf.at[own_rows, :], bbuf.at[own_rows, :], e, EX, in_ex,
        bbuf.at[pl.ds(0, 16 * (EX - 1)), :],
    )
    copies[5].wait()
    arrived("b")
    base = jnp.concatenate([bbuf[pl.ds(i, Q, stride=4), :] for i in range(4)], axis=1)

    def first_stage(k, vectors):
        part = bdot(vectors.astype(BF16), db_v[...], NT)
        for p in range(GROUP):
            ysend[k, p] = part[:, p * R : (p + 1) * R]
        push(
            f"y1{k}", lambda p: ysend.at[k, p], y1.at[k, g], g, GROUP, in_group,
            y1.at[k, pl.ds(0, GROUP - 1)],
        )
        y1[k, g] = ysend[k, g]

    def first_grams(k, tiles):
        rows = pl.ds(0, 8 * len(tiles))
        gram1_v[k, g, rows] = jnp.concatenate(tiles, axis=0)
        push(
            f"g1{k}", lambda p: gram1_v.at[k, g, rows], gram1_v.at[k, g, rows], g, GROUP, in_group,
            gram1_v.at[k, pl.ds(0, GROUP - 1), rows],
        )

    def second_stage(k):
        arrived(f"y1{k}")
        y2[k, zh] = summed([y1[k, s] for s in range(GROUP)])
        push(
            f"y2{k}", lambda p: y2.at[k, zh], y2.at[k, zh], zh, ZH, in_z,
            y2.at[k, pl.ds(0, ZH - 1)],
        )

    def second_grams(k, count):
        rows = pl.ds(0, 8 * count)
        arrived(f"g1{k}")
        gram2_v[k, zh, rows] = summed([gram1_v[k, s, rows] for s in range(GROUP)])
        push(
            f"g2{k}", lambda p: gram2_v.at[k, zh, rows], gram2_v.at[k, zh, rows], zh, ZH, in_z,
            gram2_v.at[k, pl.ds(0, ZH - 1), rows],
        )

    def third_stage(k):
        arrived(f"y2{k}")
        yfull[k, g] = summed([y2[k, s] for s in range(ZH)])
        push(
            f"y3{k}", lambda p: yfull.at[k, g], yfull.at[k, g], g, GROUP, in_group,
            yfull.at[k, pl.ds(0, GROUP - 1)],
        )

    def grams_of(k, count):
        rows = pl.ds(0, 8 * count)
        arrived(f"g2{k}")
        total = summed([gram2_v[k, s, rows] for s in range(ZH)])
        return [unfolded(total[8 * at : 8 * at + 8]) for at in range(count)]

    def rows_of(k):
        arrived(f"y3{k}")
        return [yfull[k, s] for s in range(GROUP)]

    def own_packed(buf, blocks):
        for h in range(2):
            tall = jnp.concatenate(blocks[4 * h : 4 * h + 4], axis=0)
            buf[h * ROWS : h * ROWS + R, :] = tall.T

    def half(d, count=1):
        return pl.ds(pl.multiple_of(core * ROWS + d * R, R), count * R)

    def ex_peer(slot):
        dy, dz = FAR_FIRST[slot]
        return in_ex(((y - dy) % 4) * 2 + (z_lo + dz) % 2)

    def near_rows(k, buf):
        pending[f"sb{k}"] = buf.at[half(1, 3), :]
        for slot in range(1, 4):
            send(f"sb{k}", buf.at[half(0), :], buf.at[half(slot), :], ex_peer(slot))

    def far_blocks(k):
        pending[f"ma{k}"] = far.at[k, 0]
        for slot in range(4, 8):
            send(f"ma{k}", yfull.at[k, g], far.at[k, x, slot - 4], ex_peer(slot))

    def far_rows(k):
        arrived(f"ma{k}")
        pending[f"mx{k}"] = far.at[k, pl.ds(0, 3)]
        for dx in (2, 1, 3):
            send(f"mx{k}", far.at[k, x], far.at[k, x], {"co": (x + dx) % 4})

    def far_packed(k, buf):
        arrived(f"mx{k}")
        for slot in range(4, 8):
            tall = jnp.concatenate([far[k, s, slot - 4] for s in range(4)], axis=0)
            buf[half(slot), :] = tall.T
        forward(k, buf, "a")

    def forward(k, buf, name):
        lo, hi = (4, 8) if name == "a" else (1, 4)
        if f"s{name}{k}" in pending:
            arrived(f"s{name}{k}")
        part = buf.at[half(lo, hi - lo), :]
        pending[f"f{name}{k}"] = part
        send(f"f{name}{k}", part, part, {"tp": zh * 2 + (1 - core)})

    first_stage(0, base)
    first_grams(0, [folded(repeated_gram(base, base))])
    second_stage(0)
    second_grams(0, 1)
    third_stage(0)
    far_blocks(0)
    (norm0,) = grams_of(0, 1)
    eye = (
        lax.broadcasted_iota(jnp.int32, (Q, Q), 0) == lax.broadcasted_iota(jnp.int32, (Q, Q), 1)
    ).astype(F32)
    inverse0 = eliminated(norm0, eye)
    blocks0 = rows_of(0)
    rows0 = jnp.concatenate(blocks0, axis=1)

    back = bdot((rows0 * scale).astype(BF16), db_v[...])
    for p in range(EX):
        zsend[p] = back[16 * (p // 4) : 16 * (p // 4) + 16, (p % 4) * R : (p % 4 + 1) * R]
    push("z1", lambda p: zsend.at[p], z1.at[e], e, EX, in_ex, z1.at[pl.ds(0, EX - 1)])
    z1[e] = zsend[e]
    far_rows(0)
    zg[e] = folded(repeated_gram(rows0, rows0))
    push("zg", lambda p: zg.at[e], zg.at[e], e, EX, in_ex, zg.at[pl.ds(0, EX - 1)])
    own_packed(s0, blocks0)
    arrived("z1")
    zfull[e] = summed([z1[s] for s in range(EX)])
    push("z3", lambda p: zfull.at[e], zfull.at[e], e, EX, in_ex, zfull.at[pl.ds(0, EX - 1)])
    arrived("zg")
    row_gram = unfolded(summed([zg[s] for s in range(EX)]))
    step0 = eliminated(row_gram * (scale * scale) + DAMPING * norm0, norm0)
    far_packed(0, s0)
    arrived("z3")
    near_rows(0, s0)
    back = jnp.concatenate(
        [jnp.concatenate([zfull[4 * h + j] for j in range(4)], axis=1) for h in range(2)], axis=0
    )
    image = back * scale + DAMPING * base
    residual = base - fdot(step0, image, TN)

    first_stage(1, residual)
    first_grams(
        1, [folded(repeated_gram(residual, residual)), folded(repeated_gram(residual, base))]
    )
    second_stage(1)
    second_grams(1, 2)
    third_stage(1)
    far_blocks(1)
    block0, block1 = yfull[0, g], yfull[1, g]
    cbuf[e] = jnp.concatenate(
        [folded(repeated_gram(block1, block1)), folded(repeated_gram(block1, block0))], axis=0
    )
    push("c1", lambda p: cbuf.at[e], cbuf.at[e], e, EX, in_ex, cbuf.at[pl.ds(0, EX - 1)])
    norm1, cross = grams_of(1, 2)
    mixing = fdot(inverse0, norm1)

    def pick(source, side):
        def line(hi, carry):
            for lo in range(Q):
                at = where_s[hi, lo] & (2 * ROWS - 1)
                picked[side, pl.ds(hi * Q + lo, 1), :] = source[pl.ds(at, 1), :]
            return carry

        lax.fori_loop(0, Q, line, 0)

    forward(0, s0, "b")
    to_scalar.wait()
    far_rows(1)
    blocks1 = rows_of(1)
    own_packed(s1, blocks1)
    near_rows(1, s1)
    arrived("c1")
    dbuf[g] = summed([cbuf[s] for s in range(EX)])
    push("c2", lambda p: dbuf.at[g], dbuf.at[g], g, GROUP, in_group, dbuf.at[pl.ds(0, GROUP - 1)])
    gram = (
        norm1
        + fdot(cross, mixing)
        + fdot(mixing, cross, ((0,), (1,)))
        + fdot(mixing, fdot(norm0, mixing), TN)
    )
    spare = fdot(mixing, fdot(row_gram, mixing), TN)
    arrived("fa0")
    arrived("fb0")
    pick(s0, 0)
    forward(1, s1, "b")
    arrived("c2")
    total = summed([dbuf[s] for s in range(GROUP)])
    square, mixed = unfolded(total[:8]), unfolded(total[8:])
    rows_gram = square + fdot(mixed, mixing) + fdot(mixing, mixed, ((0,), (1,))) + spare
    step1 = eliminated(rows_gram * (scale * scale) + DAMPING * gram, norm1)
    far_packed(1, s1)
    first = step0 + fdot(mixing, step1)
    out_ref[:, :COORDS] = fdot(first, base, TN) + fdot(step1, residual, TN)
    mask = mask_v[...]
    across = ((0,), (1,))
    scores = three_pass(jnp.concatenate([first] * 4, axis=0), picked[0] * mask, across)
    arrived("fa1")
    arrived("fb1")
    pick(s1, 1)
    out_ref[:, COORDS:] = scores + three_pass(
        jnp.concatenate([step1] * 4, axis=0), picked[1] * mask, across
    )

    for phase in list(pending):
        sent(phase)


def local(
    query_states, out_cotangent, query_of_token, gate_weight, up_weight, proj_in, proj_out,
    database, stored_ids,
):
    anywhere = pl.BlockSpec(memory_space=pl.ANY)
    vmem = pl.BlockSpec(memory_space=pltpu.VMEM)
    out = pl.pallas_call(
        kernel,
        out_shape=pltpu.VMEM((Q, COORDS + ROWS), F32),
        in_specs=[anywhere] * 9,
        out_specs=vmem,
        scratch_shapes=[
            pltpu.VMEM((TOK, D), BF16),
            pltpu.VMEM((TOK, R), BF16),
            pltpu.VMEM((8, R), jnp.int32),
            pltpu.VMEM((FFL, D), BF16),
            pltpu.VMEM((FFL, D), BF16),
            pltpu.VMEM((FFL, R), BF16),
            pltpu.VMEM((R, R), BF16),
            pltpu.VMEM((ROWS, COORDS), BF16),
            pltpu.VMEM((EX, 8, R), jnp.int32),
            pltpu.VMEM((ZH, GROUP, Q, R), F32),
            pltpu.VMEM((GROUP, ZH, Q, R), F32),
            pltpu.VMEM((ZH, Q, R), F32),
            pltpu.VMEM((ZH, Q, R), F32),
            pltpu.VMEM((GROUP, Q, R), F32),
            pltpu.VMEM((CHUNKS, GROUP, 16, CHUNK), F32),
            pltpu.VMEM((CHUNKS, GROUP, 16, CHUNK), F32),
            pltpu.VMEM((CHUNKS, 16, CHUNK), F32),
            pltpu.VMEM((ZH, 16, CHUNK), F32),
            pltpu.VMEM((ZH, 16, R), F32),
            pltpu.VMEM((ZH, 16, R), F32),
            pltpu.VMEM((16 * EX, R), F32),
            pltpu.VMEM((2, GROUP, Q, R), F32),
            pltpu.VMEM((2, GROUP, Q, R), F32),
            pltpu.VMEM((2, ZH, Q, R), F32),
            pltpu.VMEM((2, GROUP, Q, R), F32),
            pltpu.VMEM((2, GROUP, 16, R), F32),
            pltpu.VMEM((2, ZH, 16, R), F32),
            pltpu.VMEM((EX, 16, R), F32),
            pltpu.VMEM((EX, 16, R), F32),
            pltpu.VMEM((EX, 8, R), F32),
            pltpu.VMEM((EX, 16, R), F32),
            pltpu.VMEM((EX, 16, R), F32),
            pltpu.VMEM((GROUP, 16, R), F32),
            pltpu.VMEM((2, 4, 4, Q, R), F32),
            pltpu.VMEM((2 * ROWS, R), F32),
            pltpu.VMEM((2 * ROWS, R), F32),
            pltpu.VMEM((2, ROWS, R), F32),
            pltpu.VMEM((ROWS, R), F32),
            pltpu.VMEM((Q, R), jnp.int32),
            pltpu.SMEM((Q, R), jnp.int32),
            pltpu.SemaphoreType.DMA((7,)),
            pltpu.SemaphoreType.DMA((CHUNKS,)),
            pltpu.SemaphoreType.DMA((2,)),
            pltpu.SemaphoreType.DMA((len(PHASES),)),
            pltpu.SemaphoreType.DMA((len(PHASES),)),
        ],
        compiler_params=pltpu.CompilerParams(
            collective_id=0, has_side_effects=True, vmem_limit_bytes=60 * 1024 * 1024
        ),
        name="logra",
    )(
        query_states,
        out_cotangent,
        query_of_token.reshape(8, R),
        gate_weight.T,
        up_weight.T,
        proj_in,
        proj_out,
        database,
        stored_ids.reshape(8, R),
    )
    return out[:, :COORDS].T, out[:, COORDS:].T * (1.0 / math.sqrt(K))


def solution(mesh):
    both = ("tp", "co")
    in_specs = (
        P("ex", None),
        P("ex", both),
        P("ex"),
        P(None, both),
        P(None, both),
        P(both, None),
        P(both, None),
        P("ex", both),
        P("ex"),
    )
    out_specs = (P(both, None), P("ex", None))
    return jax.shard_map(local, mesh=mesh, in_specs=in_specs, out_specs=out_specs, check_vma=False)
```

```python
import functools
import math

import jax
import jax.numpy as jnp
from jax import lax
from jax.experimental import pallas as pl
from jax.experimental.pallas import tpu as pltpu
from jax.sharding import PartitionSpec as P

D = 4096
HALF = D // 2
FFL = 448
TOK = 1024
CHUNK = 256
CHUNKS = TOK // CHUNK
R = 128
Q = 32
QPG = 4
COORDS = 512
ROWS = 1024
EX = 8
GROUP = 8
ZH = 4
K = 16384
NSTORE = 8192
DAMPING = 1.0
HIGHEST = lax.Precision.HIGHEST
MESH = pl.DeviceIdType.MESH
F32 = jnp.float32
BF16 = jnp.bfloat16

PHASES = (
    ["ids", "r1", "r2", "r3"]
    + [f"l1{c}" for c in range(CHUNKS)]
    + ["l2", "gz", "b", "z1", "zg", "z3", "c1", "c2"]
    + [f"{name}{k}" for name in ("y1", "y2", "y3", "g1", "g2", "ma", "mx", "my", "sb", "fa", "fb", "fc") for k in (0, 1)]
)
FAR_FIRST = {4: (2, 1), 5: (1, 1), 6: (3, 1), 7: (2, 0), 1: (1, 0), 2: (3, 0), 3: (0, 1)}
PHASE = {name: at for at, name in enumerate(PHASES)}


def fdot(a, b, dims=((1,), (0,))):
    return lax.dot_general(a, b, (dims, ((), ())), precision=HIGHEST, preferred_element_type=F32)


def bdot(a, b, dims=((1,), (0,))):
    return lax.dot_general(a, b, (dims, ((), ())), preferred_element_type=F32)


TN = ((0,), (0,))
NT = ((1,), (1,))


def eliminated(matrix, target):
    n = matrix.shape[0]
    both = jnp.concatenate([matrix, target], axis=1)
    shape = both.shape
    lines = lax.broadcasted_iota(jnp.int32, shape, 0)
    for k in range(0, n, 2):
        one = jnp.broadcast_to(both[:, k : k + 1], shape)
        two = jnp.broadcast_to(both[:, k + 1 : k + 2], shape)
        pivot = 1.0 / one[k : k + 1]
        row = both[k : k + 1] * pivot
        ratio = two[k : k + 1] * pivot
        below = one[k + 1 : k + 2]
        last = (both[k + 1 : k + 2] - below * row) / (two[k + 1 : k + 2] - below * ratio)
        row = row - ratio * last
        rest = both - one * row - two * last
        both = jnp.where(lines == k, row, jnp.where(lines == k + 1, last, rest))
    return both[:, n:]


def three_pass(a, b, dims):
    a_high, b_high = a.astype(BF16), b.astype(BF16)
    a_low, b_low = (a - a_high.astype(F32)).astype(BF16), (b - b_high.astype(F32)).astype(BF16)
    return bdot(a_high, b_high, dims) + bdot(a_low, b_high, dims) + bdot(a_high, b_low, dims)


def repeated_gram(a, b):
    return fdot(a, jnp.concatenate([b] * 4, axis=0), NT)


def folded(gram):
    groups = lax.broadcasted_iota(jnp.int32, (8, R), 1) // Q
    out = jnp.where(groups == 0, gram[:8], 0.0)
    for k in range(1, 4):
        out = jnp.where(groups == k, gram[8 * k : 8 * k + 8], out)
    return out


def unfolded(tile):
    parts = [tile] + [pltpu.roll(tile, R - Q * k, 1) for k in range(1, 4)]
    return jnp.concatenate(parts, axis=0)[:, :Q]


def summed(slots):
    total = slots[0]
    for s in slots[1:]:
        total = total + s
    return total


def kernel(
    q_hbm, cot_hbm, qot_hbm, gw_hbm, uw_hbm, pin_hbm, pout_hbm, db_hbm, ids_hbm,
    out_ref,
    q_v, cot_v, qot_v, gw_v, uw_v, pin_v, pout_v, db_v,
    ids_all, rsend, r1, r2s, r2, right,
    lsend, l1, l2s, l2, gsend, gz,
    bbuf,
    ysend, y1, y2, yfull, gram1_v, gram2_v,
    zsend, z1, zg, zfull,
    cbuf, dbuf, far, s0, s1, picked, mask_v, where_v, where_s,
    small_sem, q_sem, w_sem, send_sem, recv_sem,
):
    tp = lax.axis_index("tp")
    e = lax.axis_index("ex")
    x = lax.axis_index("co")
    zh = tp // 2
    core = tp % 2
    g = core * 4 + x
    scale = 1.0 / math.sqrt(float(NSTORE))

    def in_group(p):
        return {"tp": zh * 2 + p // 4, "co": p % 4}

    def in_z(p):
        return {"tp": p * 2 + core}

    def in_ex(p):
        return {"ex": p}

    y, z_lo = e // 2, e % 2

    def peers(me, n):
        if n == ZH:
            return [(zh + d) % ZH for d in (2, 1, 3)]
        if me is e:
            return [
                ((y + dy) % 4) * 2 + (z_lo + dz) % 2
                for dy, dz in ((2, 1), (2, 0), (1, 1), (3, 1), (1, 0), (3, 0), (0, 1))
            ]
        return [
            ((core + dc) % 2) * 4 + (x + dx) % 4
            for dx, dc in ((2, 1), (2, 0), (1, 1), (3, 1), (1, 0), (3, 0), (0, 1))
        ]

    pending = {}

    def send(phase, src, dst, device):
        at = PHASE[phase]
        pltpu.make_async_remote_copy(
            src, dst, send_sem.at[at], recv_sem.at[at], device, MESH
        ).start()

    def push(phase, src_of, dst, me, n, device_of, slots):
        pending[phase] = slots
        for p in peers(me, n):
            send(phase, src_of(p), dst, device_of(p))

    def arrived(phase):
        slots = pending[phase]
        pltpu.make_async_copy(slots, slots, recv_sem.at[PHASE[phase]]).wait()

    def sent(phase):
        slots = pending.pop(phase)
        pltpu.make_async_copy(slots, slots, send_sem.at[PHASE[phase]]).wait()

    copies = [
        pltpu.make_async_copy(cot_hbm, cot_v, small_sem.at[0]),
        pltpu.make_async_copy(pout_hbm, pout_v, small_sem.at[1]),
        pltpu.make_async_copy(ids_hbm, ids_all.at[e], small_sem.at[2]),
        pltpu.make_async_copy(qot_hbm, qot_v, small_sem.at[3]),
        pltpu.make_async_copy(pin_hbm, pin_v, small_sem.at[4]),
        pltpu.make_async_copy(db_hbm, db_v, small_sem.at[5]),
    ]

    for depth in range(2):
        cols = pl.ds(depth * HALF, HALF)
        for side, (src, dst) in enumerate(((gw_hbm, gw_v), (uw_hbm, uw_v))):
            copies.append(
                pltpu.make_async_copy(src.at[:, cols], dst.at[:, cols], w_sem.at[2 * depth + side])
            )

    def q_copy(c):
        rows = pl.ds(c * CHUNK, CHUNK)
        return pltpu.make_async_copy(q_hbm.at[rows, :], q_v.at[rows, :], q_sem.at[c])

    barrier = pltpu.get_barrier_semaphore()
    for n, me, device_of in ((ZH, zh, in_z), (EX, e, in_ex), (GROUP, g, in_group)):
        for p in peers(me, n):
            pl.semaphore_signal(barrier, inc=1, device_id=device_of(p), device_id_type=MESH)

    for at in (0, 1, 2, 4):
        copies[at].start()
    q_copy(0).start()
    for at in (6, 7, 8, 9):
        copies[at].start()
    for c in range(1, CHUNKS):
        q_copy(c).start()
    copies[3].start()
    copies[5].start()

    copies[0].wait()
    copies[1].wait()
    rsend[...] = bdot(cot_v[...], pout_v[...]).reshape(ZH, GROUP, Q, R)
    copies[2].wait()

    pl.semaphore_wait(barrier, (GROUP - 1) + (ZH - 1) + (EX - 1))
    push(
        "r1", lambda p: rsend.at[:, p], r1.at[g], g, GROUP, in_group, r1.at[pl.ds(0, GROUP - 1)]
    )
    push(
        "ids", lambda p: ids_all.at[e], ids_all.at[e], e, EX, in_ex, ids_all.at[pl.ds(0, EX - 1)]
    )
    r1[g] = rsend[:, g]
    copies[4].wait()
    old = lax.broadcasted_iota(jnp.int32, (R, R), 0)
    new = lax.broadcasted_iota(jnp.int32, (R, R), 1)
    moved = old == 32 * ((new >> 2) & 3) + 4 * (new >> 4) + (new & 3)
    proj = bdot(pin_v[...], jnp.where(moved, 1.0, 0.0).astype(BF16))
    pin_v[...] = proj.astype(BF16)

    def matmul(c):
        q_copy(c).wait()
        a = q_v[c * CHUNK : (c + 1) * CHUNK, :]
        if c == 0:
            copies[6].wait()
            copies[7].wait()
            gate = bdot(gw_v[:, :HALF], a[:, :HALF], NT)
            up = bdot(uw_v[:, :HALF], a[:, :HALF], NT)
            copies[8].wait()
            copies[9].wait()
            gate = gate + bdot(gw_v[:, HALF:], a[:, HALF:], NT)
            up = up + bdot(uw_v[:, HALF:], a[:, HALF:], NT)
        else:
            gate = bdot(gw_v[...], a, NT)
            up = bdot(uw_v[...], a, NT)
        hidden = ((gate / (1.0 + jnp.exp(-gate))) * up).astype(BF16)
        lsend[c] = bdot(pin_v[...], hidden, TN).reshape(GROUP, 16, CHUNK)
        push(
            f"l1{c}", lambda p: lsend.at[c, p], l1.at[c, g], g, GROUP, in_group,
            l1.at[c, pl.ds(0, GROUP - 1)],
        )
        l1[c, g] = lsend[c, g]

    def left_second(c):
        pending["l2"] = l2.at[pl.ds(0, ZH - 1)]
        arrived(f"l1{c}")
        l2s[c] = summed([l1[c, s] for s in range(GROUP)])

        @pl.when(zh != c)
        def _():
            send("l2", l2s.at[c], l2.at[zh], in_z(c))

        @pl.when(zh == c)
        def _():
            l2[zh] = l2s[c]

    matmul(0)
    matmul(1)
    matmul(2)
    matmul(3)
    arrived("r1")
    r2s[...] = summed([r1[s] for s in range(GROUP)])
    push("r2", lambda p: r2s.at[p], r2.at[zh], zh, ZH, in_z, r2.at[pl.ds(0, ZH - 1)])
    r2[zh] = r2s[zh]
    left_second(0)
    left_second(1)
    left_second(2)

    arrived("ids")
    kinds = lax.broadcasted_iota(jnp.int32, (Q, R), 0)
    lane = lax.broadcasted_iota(jnp.int32, (Q, R), 1)
    places = jnp.zeros((Q, 2 * Q), F32)
    places_t = jnp.zeros((Q, Q), F32)
    for d in range(EX):
        dy, dz = FAR_FIRST[d] if d else (0, 0)
        source = ((y + dy) % 4) * 2 + (z_lo + dz) % 2
        his, los = [], []
        for r in range(8):
            own = ids_all[source, pl.ds(r, 1), :] - e * ROWS
            hit_low = (own & 31) == kinds
            part = d + 8 * (r // 4) + 16 * (r % 4)
            his.append(jnp.where((own >> 5) == kinds, 1.0, 0.0).astype(BF16))
            los.append(
                jnp.concatenate(
                    [
                        jnp.where(hit_low, float(part), 0.0),
                        jnp.where(hit_low, lane.astype(F32), 0.0),
                    ],
                    axis=0,
                ).astype(BF16)
            )
        his = jnp.concatenate(his, axis=1)
        los = jnp.concatenate(los, axis=1)
        places = places + bdot(his, los, NT)
        places_t = places_t + bdot(los[:Q], his, NT)
    at = (places[:, :Q].astype(jnp.int32) & 15) * R + places[:, Q:].astype(jnp.int32)
    where_v[...] = jnp.concatenate([at] * 4, axis=1)
    to_scalar = pltpu.make_async_copy(where_v, where_s, small_sem.at[6])
    to_scalar.start()
    group_t = places_t.astype(jnp.int32) >> 4
    for hi in range(Q):
        mask_v[hi * Q : (hi + 1) * Q, :] = jnp.where(
            group_t[:, hi : hi + 1] == (lane >> 5), 1.0, 0.0
        )

    arrived("r2")
    right[g] = summed([r2[s] for s in range(ZH)])
    push(
        "r3", lambda p: right.at[g], right.at[g], g, GROUP, in_group,
        right.at[pl.ds(0, GROUP - 1)],
    )
    left_second(3)
    copies[3].wait()
    query = (
        jnp.concatenate([qot_v[pl.ds(2 * zh, 1), :], qot_v[pl.ds(2 * zh + 1, 1), :]], axis=1)
        - e * QPG
    )
    arrived("r3")
    arrived("l2")
    left = summed([l2[s] for s in range(ZH)])
    weighted = jnp.concatenate([jnp.where(query == k, left, 0.0) for k in range(QPG)], axis=0)
    grads = fdot(weighted, right[...].reshape(CHUNK, R))
    low = lax.broadcasted_iota(jnp.int32, (8, R), 0) < 4
    for p in range(ZH):
        for pair in range(2):
            one, two = [
                grads[q * 16 + 8 * (p // 2) : q * 16 + 8 * (p // 2) + 8]
                for q in (2 * pair, 2 * pair + 1)
            ]
            if p % 2:
                tile = jnp.where(low, pltpu.roll(one, 4, 0), two)
            else:
                tile = jnp.where(low, one, pltpu.roll(two, 4, 0))
            gsend[p, 8 * pair : 8 * pair + 8] = tile
    push("gz", lambda p: gsend.at[p], gz.at[zh], zh, ZH, in_z, gz.at[pl.ds(0, ZH - 1)])
    gz[zh] = gsend[zh]
    arrived("gz")
    own_rows = pl.ds(pl.multiple_of(e * 16, 16), 16)
    bbuf[own_rows, :] = summed([gz[s] for s in range(ZH)])
    push(
        "b", lambda p: bbuf.at[own_rows, :], bbuf.at[own_rows, :], e, EX, in_ex,
        bbuf.at[pl.ds(0, 16 * (EX - 1)), :],
    )
    copies[5].wait()
    arrived("b")
    base = jnp.concatenate([bbuf[pl.ds(i, Q, stride=4), :] for i in range(4)], axis=1)

    def first_stage(k, vectors):
        part = bdot(vectors.astype(BF16), db_v[...], NT)
        for p in range(GROUP):
            ysend[k, p] = part[:, p * R : (p + 1) * R]
        push(
            f"y1{k}", lambda p: ysend.at[k, p], y1.at[k, g], g, GROUP, in_group,
            y1.at[k, pl.ds(0, GROUP - 1)],
        )
        y1[k, g] = ysend[k, g]

    def first_grams(k, tiles):
        rows = pl.ds(0, 8 * len(tiles))
        gram1_v[k, g, rows] = jnp.concatenate(tiles, axis=0)
        push(
            f"g1{k}", lambda p: gram1_v.at[k, g, rows], gram1_v.at[k, g, rows], g, GROUP, in_group,
            gram1_v.at[k, pl.ds(0, GROUP - 1), rows],
        )

    def second_stage(k):
        arrived(f"y1{k}")
        y2[k, zh] = summed([y1[k, s] for s in range(GROUP)])
        push(
            f"y2{k}", lambda p: y2.at[k, zh], y2.at[k, zh], zh, ZH, in_z,
            y2.at[k, pl.ds(0, ZH - 1)],
        )

    def second_grams(k, count):
        rows = pl.ds(0, 8 * count)
        arrived(f"g1{k}")
        gram2_v[k, zh, rows] = summed([gram1_v[k, s, rows] for s in range(GROUP)])
        push(
            f"g2{k}", lambda p: gram2_v.at[k, zh, rows], gram2_v.at[k, zh, rows], zh, ZH, in_z,
            gram2_v.at[k, pl.ds(0, ZH - 1), rows],
        )

    def third_stage(k):
        arrived(f"y2{k}")
        yfull[k, g] = summed([y2[k, s] for s in range(ZH)])
        push(
            f"y3{k}", lambda p: yfull.at[k, g], yfull.at[k, g], g, GROUP, in_group,
            yfull.at[k, pl.ds(0, GROUP - 1)],
        )

    def grams_of(k, count):
        rows = pl.ds(0, 8 * count)
        arrived(f"g2{k}")
        total = summed([gram2_v[k, s, rows] for s in range(ZH)])
        return [unfolded(total[8 * at : 8 * at + 8]) for at in range(count)]

    def rows_of(k):
        arrived(f"y3{k}")
        return [yfull[k, s] for s in range(GROUP)]

    def own_packed(buf, blocks):
        for h in range(2):
            tall = jnp.concatenate(blocks[4 * h : 4 * h + 4], axis=0)
            buf[h * ROWS : h * ROWS + R, :] = tall.T

    def half(d, count=1):
        return pl.ds(pl.multiple_of(core * ROWS + d * R, R), count * R)

    def ex_peer(slot):
        dy, dz = FAR_FIRST[slot]
        return in_ex(((y - dy) % 4) * 2 + (z_lo + dz) % 2)

    def near_rows(k, buf):
        pending[f"sb{k}"] = buf.at[half(1, 3), :]
        for slot in range(1, 4):
            send(f"sb{k}", buf.at[half(0), :], buf.at[half(slot), :], ex_peer(slot))

    def far_blocks(k):
        pending[f"ma{k}"] = far.at[k, 0]
        for slot in range(4, 8):
            send(f"ma{k}", yfull.at[k, g], far.at[k, x, slot - 4], ex_peer(slot))

    def far_rows(k):
        arrived(f"ma{k}")
        for name, pair in (("mx", pl.ds(0, 2)), ("my", pl.ds(2, 2))):
            pending[f"{name}{k}"] = far.at[k, pl.ds(0, 3), pair]
            for dx in (2, 1, 3):
                send(f"{name}{k}", far.at[k, x, pair], far.at[k, x, pair], {"co": (x + dx) % 4})

    def far_packed(k, buf):
        for name, lo, onward in (("mx", 4, "a"), ("my", 6, "c")):
            arrived(f"{name}{k}")
            for slot in range(lo, lo + 2):
                tall = jnp.concatenate([far[k, s, slot - 4] for s in range(4)], axis=0)
                buf[half(slot), :] = tall.T
            forward(k, buf, onward)

    def forward(k, buf, name):
        lo, hi = {"a": (4, 6), "c": (6, 8), "b": (1, 4)}[name]
        if f"s{name}{k}" in pending:
            arrived(f"s{name}{k}")
        part = buf.at[half(lo, hi - lo), :]
        pending[f"f{name}{k}"] = part
        send(f"f{name}{k}", part, part, {"tp": zh * 2 + (1 - core)})

    first_stage(0, base)
    first_grams(0, [folded(repeated_gram(base, base))])
    second_stage(0)
    second_grams(0, 1)
    third_stage(0)
    far_blocks(0)
    (norm0,) = grams_of(0, 1)
    eye = (
        lax.broadcasted_iota(jnp.int32, (Q, Q), 0) == lax.broadcasted_iota(jnp.int32, (Q, Q), 1)
    ).astype(F32)
    inverse0 = eliminated(norm0, eye)
    blocks0 = rows_of(0)
    rows0 = jnp.concatenate(blocks0, axis=1)

    back = bdot((rows0 * scale).astype(BF16), db_v[...])
    for p in range(EX):
        zsend[p] = back[16 * (p // 4) : 16 * (p // 4) + 16, (p % 4) * R : (p % 4 + 1) * R]
    push("z1", lambda p: zsend.at[p], z1.at[e], e, EX, in_ex, z1.at[pl.ds(0, EX - 1)])
    z1[e] = zsend[e]
    far_rows(0)
    zg[e] = folded(repeated_gram(rows0, rows0))
    push("zg", lambda p: zg.at[e], zg.at[e], e, EX, in_ex, zg.at[pl.ds(0, EX - 1)])
    own_packed(s0, blocks0)
    arrived("z1")
    zfull[e] = summed([z1[s] for s in range(EX)])
    push("z3", lambda p: zfull.at[e], zfull.at[e], e, EX, in_ex, zfull.at[pl.ds(0, EX - 1)])
    arrived("zg")
    row_gram = unfolded(summed([zg[s] for s in range(EX)]))
    step0 = eliminated(row_gram * (scale * scale) + DAMPING * norm0, norm0)
    far_packed(0, s0)
    arrived("z3")
    near_rows(0, s0)
    back = jnp.concatenate(
        [jnp.concatenate([zfull[4 * h + j] for j in range(4)], axis=1) for h in range(2)], axis=0
    )
    image = back * scale + DAMPING * base
    residual = base - fdot(step0, image, TN)

    first_stage(1, residual)
    first_grams(
        1, [folded(repeated_gram(residual, residual)), folded(repeated_gram(residual, base))]
    )
    second_stage(1)
    second_grams(1, 2)
    third_stage(1)
    far_blocks(1)
    block0, block1 = yfull[0, g], yfull[1, g]
    cbuf[e] = jnp.concatenate(
        [folded(repeated_gram(block1, block1)), folded(repeated_gram(block1, block0))], axis=0
    )
    push("c1", lambda p: cbuf.at[e], cbuf.at[e], e, EX, in_ex, cbuf.at[pl.ds(0, EX - 1)])
    norm1, cross = grams_of(1, 2)
    mixing = fdot(inverse0, norm1)

    def pick(source, side):
        def line(hi, carry):
            for lo in range(Q):
                at = where_s[hi, lo] & (2 * ROWS - 1)
                picked[side, pl.ds(hi * Q + lo, 1), :] = source[pl.ds(at, 1), :]
            return carry

        lax.fori_loop(0, Q, line, 0)

    forward(0, s0, "b")
    to_scalar.wait()
    far_rows(1)
    blocks1 = rows_of(1)
    own_packed(s1, blocks1)
    near_rows(1, s1)
    arrived("c1")
    dbuf[g] = summed([cbuf[s] for s in range(EX)])
    push("c2", lambda p: dbuf.at[g], dbuf.at[g], g, GROUP, in_group, dbuf.at[pl.ds(0, GROUP - 1)])
    gram = (
        norm1
        + fdot(cross, mixing)
        + fdot(mixing, cross, ((0,), (1,)))
        + fdot(mixing, fdot(norm0, mixing), TN)
    )
    spare = fdot(mixing, fdot(row_gram, mixing), TN)
    arrived("fa0")
    arrived("fc0")
    arrived("fb0")
    pick(s0, 0)
    forward(1, s1, "b")
    arrived("c2")
    total = summed([dbuf[s] for s in range(GROUP)])
    square, mixed = unfolded(total[:8]), unfolded(total[8:])
    rows_gram = square + fdot(mixed, mixing) + fdot(mixing, mixed, ((0,), (1,))) + spare
    step1 = eliminated(rows_gram * (scale * scale) + DAMPING * gram, norm1)
    far_packed(1, s1)
    first = step0 + fdot(mixing, step1)
    out_ref[:, :COORDS] = fdot(first, base, TN) + fdot(step1, residual, TN)
    mask = mask_v[...]
    across = ((0,), (1,))
    scores = three_pass(jnp.concatenate([first] * 4, axis=0), picked[0] * mask, across)
    arrived("fa1")
    arrived("fc1")
    arrived("fb1")
    pick(s1, 1)
    out_ref[:, COORDS:] = scores + three_pass(
        jnp.concatenate([step1] * 4, axis=0), picked[1] * mask, across
    )

    for phase in list(pending):
        sent(phase)


def local(
    query_states, out_cotangent, query_of_token, gate_weight, up_weight, proj_in, proj_out,
    database, stored_ids,
):
    anywhere = pl.BlockSpec(memory_space=pl.ANY)
    vmem = pl.BlockSpec(memory_space=pltpu.VMEM)
    out = pl.pallas_call(
        kernel,
        out_shape=pltpu.VMEM((Q, COORDS + ROWS), F32),
        in_specs=[anywhere] * 9,
        out_specs=vmem,
        scratch_shapes=[
            pltpu.VMEM((TOK, D), BF16),
            pltpu.VMEM((TOK, R), BF16),
            pltpu.VMEM((8, R), jnp.int32),
            pltpu.VMEM((FFL, D), BF16),
            pltpu.VMEM((FFL, D), BF16),
            pltpu.VMEM((FFL, R), BF16),
            pltpu.VMEM((R, R), BF16),
            pltpu.VMEM((ROWS, COORDS), BF16),
            pltpu.VMEM((EX, 8, R), jnp.int32),
            pltpu.VMEM((ZH, GROUP, Q, R), F32),
            pltpu.VMEM((GROUP, ZH, Q, R), F32),
            pltpu.VMEM((ZH, Q, R), F32),
            pltpu.VMEM((ZH, Q, R), F32),
            pltpu.VMEM((GROUP, Q, R), F32),
            pltpu.VMEM((CHUNKS, GROUP, 16, CHUNK), F32),
            pltpu.VMEM((CHUNKS, GROUP, 16, CHUNK), F32),
            pltpu.VMEM((CHUNKS, 16, CHUNK), F32),
            pltpu.VMEM((ZH, 16, CHUNK), F32),
            pltpu.VMEM((ZH, 16, R), F32),
            pltpu.VMEM((ZH, 16, R), F32),
            pltpu.VMEM((16 * EX, R), F32),
            pltpu.VMEM((2, GROUP, Q, R), F32),
            pltpu.VMEM((2, GROUP, Q, R), F32),
            pltpu.VMEM((2, ZH, Q, R), F32),
            pltpu.VMEM((2, GROUP, Q, R), F32),
            pltpu.VMEM((2, GROUP, 16, R), F32),
            pltpu.VMEM((2, ZH, 16, R), F32),
            pltpu.VMEM((EX, 16, R), F32),
            pltpu.VMEM((EX, 16, R), F32),
            pltpu.VMEM((EX, 8, R), F32),
            pltpu.VMEM((EX, 16, R), F32),
            pltpu.VMEM((EX, 16, R), F32),
            pltpu.VMEM((GROUP, 16, R), F32),
            pltpu.VMEM((2, 4, 4, Q, R), F32),
            pltpu.VMEM((2 * ROWS, R), F32),
            pltpu.VMEM((2 * ROWS, R), F32),
            pltpu.VMEM((2, ROWS, R), F32),
            pltpu.VMEM((ROWS, R), F32),
            pltpu.VMEM((Q, R), jnp.int32),
            pltpu.SMEM((Q, R), jnp.int32),
            pltpu.SemaphoreType.DMA((7,)),
            pltpu.SemaphoreType.DMA((CHUNKS,)),
            pltpu.SemaphoreType.DMA((4,)),
            pltpu.SemaphoreType.DMA((len(PHASES),)),
            pltpu.SemaphoreType.DMA((len(PHASES),)),
        ],
        compiler_params=pltpu.CompilerParams(
            collective_id=0, has_side_effects=True, vmem_limit_bytes=60 * 1024 * 1024
        ),
        name="logra",
    )(
        query_states,
        out_cotangent,
        query_of_token.reshape(8, R),
        gate_weight.T,
        up_weight.T,
        proj_in,
        proj_out,
        database,
        stored_ids.reshape(8, R),
    )
    return out[:, :COORDS].T, out[:, COORDS:].T * (1.0 / math.sqrt(K))


def solution(mesh):
    both = ("tp", "co")
    in_specs = (
        P("ex", None),
        P("ex", both),
        P("ex"),
        P(None, both),
        P(None, both),
        P(both, None),
        P(both, None),
        P("ex", both),
        P("ex"),
    )
    out_specs = (P(both, None), P("ex", None))
    return jax.shard_map(local, mesh=mesh, in_specs=in_specs, out_specs=out_specs, check_vma=False)
```

```python
import functools
import math

import jax
import jax.numpy as jnp
from jax import lax
from jax.experimental import pallas as pl
from jax.experimental.pallas import tpu as pltpu
from jax.sharding import PartitionSpec as P

D = 4096
HALF = D // 2
FFL = 448
TOK = 1024
CHUNK = 256
CHUNKS = TOK // CHUNK
R = 128
Q = 32
QPG = 4
COORDS = 512
ROWS = 1024
EX = 8
GROUP = 8
ZH = 4
K = 16384
NSTORE = 8192
DAMPING = 1.0
HIGHEST = lax.Precision.HIGHEST
MESH = pl.DeviceIdType.MESH
F32 = jnp.float32
BF16 = jnp.bfloat16

PHASES = (
    ["ids", "r1", "r2", "r3"]
    + [f"l1{c}" for c in range(CHUNKS)]
    + ["l2", "gz", "b", "z1", "zg", "z3", "c1", "c2"]
    + [f"{name}{k}" for name in ("y1", "y2", "y3", "g1", "g2", "ma", "mx", "my", "sb", "fa", "fb", "fc") for k in (0, 1)]
)
FAR_FIRST = {4: (2, 1), 5: (1, 1), 6: (3, 1), 7: (2, 0), 1: (1, 0), 2: (3, 0), 3: (0, 1)}
PHASE = {name: at for at, name in enumerate(PHASES)}


def fdot(a, b, dims=((1,), (0,))):
    return lax.dot_general(a, b, (dims, ((), ())), precision=HIGHEST, preferred_element_type=F32)


def bdot(a, b, dims=((1,), (0,))):
    return lax.dot_general(a, b, (dims, ((), ())), preferred_element_type=F32)


TN = ((0,), (0,))
NT = ((1,), (1,))


def eliminated(matrix, target):
    n = matrix.shape[0]
    both = jnp.concatenate([matrix, target], axis=1)
    shape = both.shape
    lines = lax.broadcasted_iota(jnp.int32, shape, 0)
    for k in range(0, n, 2):
        one = jnp.broadcast_to(both[:, k : k + 1], shape)
        two = jnp.broadcast_to(both[:, k + 1 : k + 2], shape)
        pivot = 1.0 / one[k : k + 1]
        row = both[k : k + 1] * pivot
        ratio = two[k : k + 1] * pivot
        below = one[k + 1 : k + 2]
        last = (both[k + 1 : k + 2] - below * row) / (two[k + 1 : k + 2] - below * ratio)
        row = row - ratio * last
        rest = both - one * row - two * last
        both = jnp.where(lines == k, row, jnp.where(lines == k + 1, last, rest))
    return both[:, n:]


def three_pass(a, b, dims):
    a_high, b_high = a.astype(BF16), b.astype(BF16)
    a_low, b_low = (a - a_high.astype(F32)).astype(BF16), (b - b_high.astype(F32)).astype(BF16)
    return bdot(a_high, b_high, dims) + bdot(a_low, b_high, dims) + bdot(a_high, b_low, dims)


def repeated_gram(a, b):
    return fdot(a, jnp.concatenate([b] * 4, axis=0), NT)


def folded(gram):
    groups = lax.broadcasted_iota(jnp.int32, (8, R), 1) // Q
    out = jnp.where(groups == 0, gram[:8], 0.0)
    for k in range(1, 4):
        out = jnp.where(groups == k, gram[8 * k : 8 * k + 8], out)
    return out


def unfolded(tile):
    parts = [tile] + [pltpu.roll(tile, R - Q * k, 1) for k in range(1, 4)]
    return jnp.concatenate(parts, axis=0)[:, :Q]


def summed(slots):
    total = slots[0]
    for s in slots[1:]:
        total = total + s
    return total


def kernel(
    q_hbm, cot_hbm, qot_hbm, gw_hbm, uw_hbm, pin_hbm, pout_hbm, db_hbm, ids_hbm,
    out_ref,
    q_v, cot_v, qot_v, gw_v, uw_v, pin_v, pout_v, db_v,
    ids_all, rsend, r1, r2s, r2, right,
    lsend, l1, l2s, l2, gsend, gz,
    bbuf,
    ysend, y1, y2, yfull, gram1_v, gram2_v,
    zsend, z1, zg, zfull,
    cbuf, dbuf, far, s0, s1, picked, mask_v, where_v, where_s,
    small_sem, q_sem, w_sem, send_sem, recv_sem,
):
    tp = lax.axis_index("tp")
    e = lax.axis_index("ex")
    x = lax.axis_index("co")
    zh = tp // 2
    core = tp % 2
    g = core * 4 + x
    scale = 1.0 / math.sqrt(float(NSTORE))

    def in_group(p):
        return {"tp": zh * 2 + p // 4, "co": p % 4}

    def in_z(p):
        return {"tp": p * 2 + core}

    def in_ex(p):
        return {"ex": p}

    y, z_lo = e // 2, e % 2

    def peers(me, n):
        if n == ZH:
            return [(zh + d) % ZH for d in (2, 1, 3)]
        if me is e:
            return [
                ((y + dy) % 4) * 2 + (z_lo + dz) % 2
                for dy, dz in ((2, 1), (2, 0), (1, 1), (3, 1), (1, 0), (3, 0), (0, 1))
            ]
        return [
            ((core + dc) % 2) * 4 + (x + dx) % 4
            for dx, dc in ((2, 1), (2, 0), (1, 1), (3, 1), (1, 0), (3, 0), (0, 1))
        ]

    pending = {}

    def send(phase, src, dst, device):
        at = PHASE[phase]
        pltpu.make_async_remote_copy(
            src, dst, send_sem.at[at], recv_sem.at[at], device, MESH
        ).start()

    def push(phase, src_of, dst, me, n, device_of, slots):
        pending[phase] = slots
        for p in peers(me, n):
            send(phase, src_of(p), dst, device_of(p))

    def arrived(phase):
        slots = pending[phase]
        pltpu.make_async_copy(slots, slots, recv_sem.at[PHASE[phase]]).wait()

    def sent(phase):
        slots = pending.pop(phase)
        pltpu.make_async_copy(slots, slots, send_sem.at[PHASE[phase]]).wait()

    copies = [
        pltpu.make_async_copy(cot_hbm, cot_v, small_sem.at[0]),
        pltpu.make_async_copy(pout_hbm, pout_v, small_sem.at[1]),
        pltpu.make_async_copy(ids_hbm, ids_all.at[e], small_sem.at[2]),
        pltpu.make_async_copy(qot_hbm, qot_v, small_sem.at[3]),
        pltpu.make_async_copy(pin_hbm, pin_v, small_sem.at[4]),
        pltpu.make_async_copy(db_hbm, db_v, small_sem.at[5]),
    ]

    for depth in range(2):
        cols = pl.ds(depth * HALF, HALF)
        for side, (src, dst) in enumerate(((gw_hbm, gw_v), (uw_hbm, uw_v))):
            copies.append(
                pltpu.make_async_copy(src.at[:, cols], dst.at[:, cols], w_sem.at[2 * depth + side])
            )

    def q_copy(c):
        rows = pl.ds(c * CHUNK, CHUNK)
        return pltpu.make_async_copy(q_hbm.at[rows, :], q_v.at[rows, :], q_sem.at[c])

    barrier = pltpu.get_barrier_semaphore()
    for n, me, device_of in ((ZH, zh, in_z), (EX, e, in_ex), (GROUP, g, in_group)):
        for p in peers(me, n):
            pl.semaphore_signal(barrier, inc=1, device_id=device_of(p), device_id_type=MESH)

    for at in (0, 1, 2, 4):
        copies[at].start()
    q_copy(0).start()
    for at in (6, 7, 8, 9):
        copies[at].start()
    for c in range(1, CHUNKS):
        q_copy(c).start()
    copies[3].start()
    copies[5].start()

    copies[0].wait()
    copies[1].wait()
    rsend[...] = bdot(cot_v[...], pout_v[...]).reshape(ZH, GROUP, Q, R)
    copies[2].wait()

    pl.semaphore_wait(barrier, (GROUP - 1) + (ZH - 1) + (EX - 1))
    push(
        "r1", lambda p: rsend.at[:, p], r1.at[g], g, GROUP, in_group, r1.at[pl.ds(0, GROUP - 1)]
    )
    push(
        "ids", lambda p: ids_all.at[e], ids_all.at[e], e, EX, in_ex, ids_all.at[pl.ds(0, EX - 1)]
    )
    r1[g] = rsend[:, g]
    copies[4].wait()
    old = lax.broadcasted_iota(jnp.int32, (R, R), 0)
    new = lax.broadcasted_iota(jnp.int32, (R, R), 1)
    moved = old == 32 * ((new >> 2) & 3) + 4 * (new >> 4) + (new & 3)
    proj = bdot(pin_v[...], jnp.where(moved, 1.0, 0.0).astype(BF16))
    pin_v[...] = proj.astype(BF16)

    def matmul(c):
        q_copy(c).wait()
        a = q_v[c * CHUNK : (c + 1) * CHUNK, :]
        if c == 0:
            copies[6].wait()
            copies[7].wait()
            gate = bdot(gw_v[:, :HALF], a[:, :HALF], NT)
            up = bdot(uw_v[:, :HALF], a[:, :HALF], NT)
            copies[8].wait()
            copies[9].wait()
            gate = gate + bdot(gw_v[:, HALF:], a[:, HALF:], NT)
            up = up + bdot(uw_v[:, HALF:], a[:, HALF:], NT)
        else:
            gate = bdot(gw_v[...], a, NT)
            up = bdot(uw_v[...], a, NT)
        hidden = ((gate / (1.0 + jnp.exp(-gate))) * up).astype(BF16)
        lsend[c] = bdot(pin_v[...], hidden, TN).reshape(GROUP, 16, CHUNK)
        push(
            f"l1{c}", lambda p: lsend.at[c, p], l1.at[c, g], g, GROUP, in_group,
            l1.at[c, pl.ds(0, GROUP - 1)],
        )
        l1[c, g] = lsend[c, g]

    def left_second(c):
        pending["l2"] = l2.at[pl.ds(0, ZH - 1)]
        arrived(f"l1{c}")
        l2s[c] = summed([l1[c, s] for s in range(GROUP)])

        @pl.when(zh != c)
        def _():
            send("l2", l2s.at[c], l2.at[zh], in_z(c))

        @pl.when(zh == c)
        def _():
            l2[zh] = l2s[c]

    matmul(0)
    matmul(1)
    matmul(2)
    arrived("r1")
    r2s[...] = summed([r1[s] for s in range(GROUP)])
    push("r2", lambda p: r2s.at[p], r2.at[zh], zh, ZH, in_z, r2.at[pl.ds(0, ZH - 1)])
    r2[zh] = r2s[zh]
    matmul(3)
    left_second(0)
    left_second(1)
    left_second(2)

    arrived("ids")
    kinds = lax.broadcasted_iota(jnp.int32, (Q, R), 0)
    lane = lax.broadcasted_iota(jnp.int32, (Q, R), 1)
    places = jnp.zeros((Q, 2 * Q), F32)
    places_t = jnp.zeros((Q, Q), F32)
    for d in range(EX):
        dy, dz = FAR_FIRST[d] if d else (0, 0)
        source = ((y + dy) % 4) * 2 + (z_lo + dz) % 2
        his, los = [], []
        for r in range(8):
            own = ids_all[source, pl.ds(r, 1), :] - e * ROWS
            hit_low = (own & 31) == kinds
            part = d + 8 * (r // 4) + 16 * (r % 4)
            his.append(jnp.where((own >> 5) == kinds, 1.0, 0.0).astype(BF16))
            los.append(
                jnp.concatenate(
                    [
                        jnp.where(hit_low, float(part), 0.0),
                        jnp.where(hit_low, lane.astype(F32), 0.0),
                    ],
                    axis=0,
                ).astype(BF16)
            )
        his = jnp.concatenate(his, axis=1)
        los = jnp.concatenate(los, axis=1)
        places = places + bdot(his, los, NT)
        places_t = places_t + bdot(los[:Q], his, NT)
    at = (places[:, :Q].astype(jnp.int32) & 15) * R + places[:, Q:].astype(jnp.int32)
    where_v[...] = jnp.concatenate([at] * 4, axis=1)
    to_scalar = pltpu.make_async_copy(where_v, where_s, small_sem.at[6])
    to_scalar.start()
    group_t = places_t.astype(jnp.int32) >> 4
    for hi in range(Q):
        mask_v[hi * Q : (hi + 1) * Q, :] = jnp.where(
            group_t[:, hi : hi + 1] == (lane >> 5), 1.0, 0.0
        )

    arrived("r2")
    right[g] = summed([r2[s] for s in range(ZH)])
    push(
        "r3", lambda p: right.at[g], right.at[g], g, GROUP, in_group,
        right.at[pl.ds(0, GROUP - 1)],
    )
    left_second(3)
    copies[3].wait()
    query = (
        jnp.concatenate([qot_v[pl.ds(2 * zh, 1), :], qot_v[pl.ds(2 * zh + 1, 1), :]], axis=1)
        - e * QPG
    )
    arrived("r3")
    arrived("l2")
    left = summed([l2[s] for s in range(ZH)])
    weighted = jnp.concatenate([jnp.where(query == k, left, 0.0) for k in range(QPG)], axis=0)
    grads = fdot(weighted, right[...].reshape(CHUNK, R))
    low = lax.broadcasted_iota(jnp.int32, (8, R), 0) < 4
    for p in range(ZH):
        for pair in range(2):
            one, two = [
                grads[q * 16 + 8 * (p // 2) : q * 16 + 8 * (p // 2) + 8]
                for q in (2 * pair, 2 * pair + 1)
            ]
            if p % 2:
                tile = jnp.where(low, pltpu.roll(one, 4, 0), two)
            else:
                tile = jnp.where(low, one, pltpu.roll(two, 4, 0))
            gsend[p, 8 * pair : 8 * pair + 8] = tile
    push("gz", lambda p: gsend.at[p], gz.at[zh], zh, ZH, in_z, gz.at[pl.ds(0, ZH - 1)])
    gz[zh] = gsend[zh]
    arrived("gz")
    own_rows = pl.ds(pl.multiple_of(e * 16, 16), 16)
    bbuf[own_rows, :] = summed([gz[s] for s in range(ZH)])
    push(
        "b", lambda p: bbuf.at[own_rows, :], bbuf.at[own_rows, :], e, EX, in_ex,
        bbuf.at[pl.ds(0, 16 * (EX - 1)), :],
    )
    copies[5].wait()
    arrived("b")
    base = jnp.concatenate([bbuf[pl.ds(i, Q, stride=4), :] for i in range(4)], axis=1)

    def first_stage(k, vectors):
        part = bdot(vectors.astype(BF16), db_v[...], NT)
        for p in range(GROUP):
            ysend[k, p] = part[:, p * R : (p + 1) * R]
        push(
            f"y1{k}", lambda p: ysend.at[k, p], y1.at[k, g], g, GROUP, in_group,
            y1.at[k, pl.ds(0, GROUP - 1)],
        )
        y1[k, g] = ysend[k, g]

    def first_grams(k, tiles):
        rows = pl.ds(0, 8 * len(tiles))
        gram1_v[k, g, rows] = jnp.concatenate(tiles, axis=0)
        push(
            f"g1{k}", lambda p: gram1_v.at[k, g, rows], gram1_v.at[k, g, rows], g, GROUP, in_group,
            gram1_v.at[k, pl.ds(0, GROUP - 1), rows],
        )

    def second_stage(k):
        arrived(f"y1{k}")
        y2[k, zh] = summed([y1[k, s] for s in range(GROUP)])
        push(
            f"y2{k}", lambda p: y2.at[k, zh], y2.at[k, zh], zh, ZH, in_z,
            y2.at[k, pl.ds(0, ZH - 1)],
        )

    def second_grams(k, count):
        rows = pl.ds(0, 8 * count)
        arrived(f"g1{k}")
        gram2_v[k, zh, rows] = summed([gram1_v[k, s, rows] for s in range(GROUP)])
        push(
            f"g2{k}", lambda p: gram2_v.at[k, zh, rows], gram2_v.at[k, zh, rows], zh, ZH, in_z,
            gram2_v.at[k, pl.ds(0, ZH - 1), rows],
        )

    def third_stage(k):
        arrived(f"y2{k}")
        yfull[k, g] = summed([y2[k, s] for s in range(ZH)])
        push(
            f"y3{k}", lambda p: yfull.at[k, g], yfull.at[k, g], g, GROUP, in_group,
            yfull.at[k, pl.ds(0, GROUP - 1)],
        )

    def grams_of(k, count):
        rows = pl.ds(0, 8 * count)
        arrived(f"g2{k}")
        total = summed([gram2_v[k, s, rows] for s in range(ZH)])
        return [unfolded(total[8 * at : 8 * at + 8]) for at in range(count)]

    def rows_of(k):
        arrived(f"y3{k}")
        return [yfull[k, s] for s in range(GROUP)]

    def own_packed(buf, blocks):
        for h in range(2):
            tall = jnp.concatenate(blocks[4 * h : 4 * h + 4], axis=0)
            buf[h * ROWS : h * ROWS + R, :] = tall.T

    def half(d, count=1):
        return pl.ds(pl.multiple_of(core * ROWS + d * R, R), count * R)

    def ex_peer(slot):
        dy, dz = FAR_FIRST[slot]
        return in_ex(((y - dy) % 4) * 2 + (z_lo + dz) % 2)

    def near_rows(k, buf):
        pending[f"sb{k}"] = buf.at[half(1, 3), :]
        for slot in range(1, 4):
            send(f"sb{k}", buf.at[half(0), :], buf.at[half(slot), :], ex_peer(slot))

    def far_blocks(k):
        pending[f"ma{k}"] = far.at[k, 0]
        for slot in range(4, 8):
            send(f"ma{k}", yfull.at[k, g], far.at[k, x, slot - 4], ex_peer(slot))

    def far_rows(k):
        arrived(f"ma{k}")
        for name, pair in (("mx", pl.ds(0, 2)), ("my", pl.ds(2, 2))):
            pending[f"{name}{k}"] = far.at[k, pl.ds(0, 3), pair]
            for dx in (2, 1, 3):
                send(f"{name}{k}", far.at[k, x, pair], far.at[k, x, pair], {"co": (x + dx) % 4})

    def far_packed(k, buf):
        for name, lo, onward in (("mx", 4, "a"), ("my", 6, "c")):
            arrived(f"{name}{k}")
            for slot in range(lo, lo + 2):
                tall = jnp.concatenate([far[k, s, slot - 4] for s in range(4)], axis=0)
                buf[half(slot), :] = tall.T
            forward(k, buf, onward)

    def forward(k, buf, name):
        lo, hi = {"a": (4, 6), "c": (6, 8), "b": (1, 4)}[name]
        if f"s{name}{k}" in pending:
            arrived(f"s{name}{k}")
        part = buf.at[half(lo, hi - lo), :]
        pending[f"f{name}{k}"] = part
        send(f"f{name}{k}", part, part, {"tp": zh * 2 + (1 - core)})

    first_stage(0, base)
    first_grams(0, [folded(repeated_gram(base, base))])
    second_stage(0)
    second_grams(0, 1)
    third_stage(0)
    far_blocks(0)
    (norm0,) = grams_of(0, 1)
    eye = (
        lax.broadcasted_iota(jnp.int32, (Q, Q), 0) == lax.broadcasted_iota(jnp.int32, (Q, Q), 1)
    ).astype(F32)
    inverse0 = eliminated(norm0, eye)
    blocks0 = rows_of(0)
    rows0 = jnp.concatenate(blocks0, axis=1)

    back = bdot((rows0 * scale).astype(BF16), db_v[...])
    for p in range(EX):
        zsend[p] = back[16 * (p // 4) : 16 * (p // 4) + 16, (p % 4) * R : (p % 4 + 1) * R]
    push("z1", lambda p: zsend.at[p], z1.at[e], e, EX, in_ex, z1.at[pl.ds(0, EX - 1)])
    z1[e] = zsend[e]
    far_rows(0)
    zg[e] = folded(repeated_gram(rows0, rows0))
    push("zg", lambda p: zg.at[e], zg.at[e], e, EX, in_ex, zg.at[pl.ds(0, EX - 1)])
    own_packed(s0, blocks0)
    arrived("z1")
    zfull[e] = summed([z1[s] for s in range(EX)])
    push("z3", lambda p: zfull.at[e], zfull.at[e], e, EX, in_ex, zfull.at[pl.ds(0, EX - 1)])
    arrived("zg")
    row_gram = unfolded(summed([zg[s] for s in range(EX)]))
    step0 = eliminated(row_gram * (scale * scale) + DAMPING * norm0, norm0)
    far_packed(0, s0)
    arrived("z3")
    near_rows(0, s0)
    back = jnp.concatenate(
        [jnp.concatenate([zfull[4 * h + j] for j in range(4)], axis=1) for h in range(2)], axis=0
    )
    image = back * scale + DAMPING * base
    residual = base - fdot(step0, image, TN)

    first_stage(1, residual)
    first_grams(
        1, [folded(repeated_gram(residual, residual)), folded(repeated_gram(residual, base))]
    )
    second_stage(1)
    second_grams(1, 2)
    third_stage(1)
    far_blocks(1)
    block0, block1 = yfull[0, g], yfull[1, g]
    cbuf[e] = jnp.concatenate(
        [folded(repeated_gram(block1, block1)), folded(repeated_gram(block1, block0))], axis=0
    )
    push("c1", lambda p: cbuf.at[e], cbuf.at[e], e, EX, in_ex, cbuf.at[pl.ds(0, EX - 1)])
    norm1, cross = grams_of(1, 2)
    mixing = fdot(inverse0, norm1)

    def pick(source, side):
        def line(hi, carry):
            for lo in range(Q):
                at = where_s[hi, lo] & (2 * ROWS - 1)
                picked[side, pl.ds(hi * Q + lo, 1), :] = source[pl.ds(at, 1), :]
            return carry

        lax.fori_loop(0, Q, line, 0)

    forward(0, s0, "b")
    to_scalar.wait()
    far_rows(1)
    blocks1 = rows_of(1)
    own_packed(s1, blocks1)
    near_rows(1, s1)
    arrived("c1")
    dbuf[g] = summed([cbuf[s] for s in range(EX)])
    push("c2", lambda p: dbuf.at[g], dbuf.at[g], g, GROUP, in_group, dbuf.at[pl.ds(0, GROUP - 1)])
    gram = (
        norm1
        + fdot(cross, mixing)
        + fdot(mixing, cross, ((0,), (1,)))
        + fdot(mixing, fdot(norm0, mixing), TN)
    )
    spare = fdot(mixing, fdot(row_gram, mixing), TN)
    arrived("fa0")
    arrived("fc0")
    arrived("fb0")
    pick(s0, 0)
    forward(1, s1, "b")
    arrived("c2")
    total = summed([dbuf[s] for s in range(GROUP)])
    square, mixed = unfolded(total[:8]), unfolded(total[8:])
    rows_gram = square + fdot(mixed, mixing) + fdot(mixing, mixed, ((0,), (1,))) + spare
    step1 = eliminated(rows_gram * (scale * scale) + DAMPING * gram, norm1)
    far_packed(1, s1)
    first = step0 + fdot(mixing, step1)
    out_ref[:, :COORDS] = fdot(first, base, TN) + fdot(step1, residual, TN)
    mask = mask_v[...]
    across = ((0,), (1,))
    scores = three_pass(jnp.concatenate([first] * 4, axis=0), picked[0] * mask, across)
    arrived("fa1")
    arrived("fc1")
    arrived("fb1")
    pick(s1, 1)
    out_ref[:, COORDS:] = scores + three_pass(
        jnp.concatenate([step1] * 4, axis=0), picked[1] * mask, across
    )

    for phase in list(pending):
        sent(phase)


def local(
    query_states, out_cotangent, query_of_token, gate_weight, up_weight, proj_in, proj_out,
    database, stored_ids,
):
    anywhere = pl.BlockSpec(memory_space=pl.ANY)
    vmem = pl.BlockSpec(memory_space=pltpu.VMEM)
    out = pl.pallas_call(
        kernel,
        out_shape=pltpu.VMEM((Q, COORDS + ROWS), F32),
        in_specs=[anywhere] * 9,
        out_specs=vmem,
        scratch_shapes=[
            pltpu.VMEM((TOK, D), BF16),
            pltpu.VMEM((TOK, R), BF16),
            pltpu.VMEM((8, R), jnp.int32),
            pltpu.VMEM((FFL, D), BF16),
            pltpu.VMEM((FFL, D), BF16),
            pltpu.VMEM((FFL, R), BF16),
            pltpu.VMEM((R, R), BF16),
            pltpu.VMEM((ROWS, COORDS), BF16),
            pltpu.VMEM((EX, 8, R), jnp.int32),
            pltpu.VMEM((ZH, GROUP, Q, R), F32),
            pltpu.VMEM((GROUP, ZH, Q, R), F32),
            pltpu.VMEM((ZH, Q, R), F32),
            pltpu.VMEM((ZH, Q, R), F32),
            pltpu.VMEM((GROUP, Q, R), F32),
            pltpu.VMEM((CHUNKS, GROUP, 16, CHUNK), F32),
            pltpu.VMEM((CHUNKS, GROUP, 16, CHUNK), F32),
            pltpu.VMEM((CHUNKS, 16, CHUNK), F32),
            pltpu.VMEM((ZH, 16, CHUNK), F32),
            pltpu.VMEM((ZH, 16, R), F32),
            pltpu.VMEM((ZH, 16, R), F32),
            pltpu.VMEM((16 * EX, R), F32),
            pltpu.VMEM((2, GROUP, Q, R), F32),
            pltpu.VMEM((2, GROUP, Q, R), F32),
            pltpu.VMEM((2, ZH, Q, R), F32),
            pltpu.VMEM((2, GROUP, Q, R), F32),
            pltpu.VMEM((2, GROUP, 16, R), F32),
            pltpu.VMEM((2, ZH, 16, R), F32),
            pltpu.VMEM((EX, 16, R), F32),
            pltpu.VMEM((EX, 16, R), F32),
            pltpu.VMEM((EX, 8, R), F32),
            pltpu.VMEM((EX, 16, R), F32),
            pltpu.VMEM((EX, 16, R), F32),
            pltpu.VMEM((GROUP, 16, R), F32),
            pltpu.VMEM((2, 4, 4, Q, R), F32),
            pltpu.VMEM((2 * ROWS, R), F32),
            pltpu.VMEM((2 * ROWS, R), F32),
            pltpu.VMEM((2, ROWS, R), F32),
            pltpu.VMEM((ROWS, R), F32),
            pltpu.VMEM((Q, R), jnp.int32),
            pltpu.SMEM((Q, R), jnp.int32),
            pltpu.SemaphoreType.DMA((7,)),
            pltpu.SemaphoreType.DMA((CHUNKS,)),
            pltpu.SemaphoreType.DMA((4,)),
            pltpu.SemaphoreType.DMA((len(PHASES),)),
            pltpu.SemaphoreType.DMA((len(PHASES),)),
        ],
        compiler_params=pltpu.CompilerParams(
            collective_id=0, has_side_effects=True, vmem_limit_bytes=60 * 1024 * 1024
        ),
        name="logra",
    )(
        query_states,
        out_cotangent,
        query_of_token.reshape(8, R),
        gate_weight.T,
        up_weight.T,
        proj_in,
        proj_out,
        database,
        stored_ids.reshape(8, R),
    )
    return out[:, :COORDS].T, out[:, COORDS:].T * (1.0 / math.sqrt(K))


def solution(mesh):
    both = ("tp", "co")
    in_specs = (
        P("ex", None),
        P("ex", both),
        P("ex"),
        P(None, both),
        P(None, both),
        P(both, None),
        P(both, None),
        P("ex", both),
        P("ex"),
    )
    out_specs = (P(both, None), P("ex", None))
    return jax.shard_map(local, mesh=mesh, in_specs=in_specs, out_specs=out_specs, check_vma=False)
```
